32 devices in a mesh: req: 8 (over y, x, core), mdl: 4 (over z).
Axes of the slice: x: 2, y: 2, z: 4, core: 2. Of those that a mesh axis runs over, the one named last changes fastest.
Arguments:
- tokens: bfloat16 [256, 4, 2048], P('req', None, 'mdl'), may hold values from -6 to 6
- counts: int32 [256], P('req'), may hold values from 1 to 4
- new_owner: int32 [256], replicated, may hold values from 0 to 255, as said below
- wkv_state: float32 [256, 32, 4096], P('req', 'mdl'), may hold values from -12 to 12
- att_shift: bfloat16 [256, 2048], P('req', 'mdl'), may hold values from -6 to 6
- ffn_shift: bfloat16 [256, 2048], P('req', 'mdl'), may hold values from -6 to 6
- norm_params: float32 [4, 2048], replicated, may hold values from 0.25 to 1.75
- mix_coeffs: float32 [7, 2048], replicated, may hold values from 0 to 1
- head_params: float32 [7, 2048], P(None, 'mdl'), may hold values from -6 to 2
- recept_weight: bfloat16 [2048, 2048], P(None, 'mdl'), may hold values from -0.125 to 0.125
- key_weight: bfloat16 [2048, 2048], P(None, 'mdl'), may hold values from -0.125 to 0.125
- value_weight: bfloat16 [2048, 2048], P(None, 'mdl'), may hold values from -0.125 to 0.125
- output_weight: bfloat16 [2048, 2048], P('mdl'), may hold values from -0.125 to 0.125
- decay_down: bfloat16 [2048, 96], P('mdl'), may hold values from -0.125 to 0.125
- decay_up: bfloat16 [96, 2048], P(None, 'mdl'), may hold values from -0.625 to 0.625
- alpha_down: bfloat16 [2048, 96], P('mdl'), may hold values from -0.125 to 0.125
- alpha_up: bfloat16 [96, 2048], P(None, 'mdl'), may hold values from -0.625 to 0.625
- gate_down: bfloat16 [2048, 256], P('mdl'), may hold values from -0.125 to 0.125
- gate_up: bfloat16 [256, 2048], P(None, 'mdl'), may hold values from -0.375 to 0.375
- ffn_key_weight: bfloat16 [2048, 4096], P(None, 'mdl'), may hold values from -0.125 to 0.125
- ffn_value_weight: bfloat16 [4096, 2048], P('mdl'), may hold values from -0.09375 to 0.09375
Outputs:
- block_output: bfloat16 [256, 4, 2048], P('req', None, 'mdl')
- new_state: float32 [256, 32, 4096], P('req', 'mdl')
- new_att_shift: bfloat16 [256, 2048], P('req', 'mdl')
- new_ffn_shift: bfloat16 [256, 2048], P('req', 'mdl')
The draws below stay inside these ranges and needn't reach their ends.
Inputs may be any that keep to these rules, and one draw needn't show every extreme that they name: new_owner is a permutation: the states of request i move to position new_owner[i]. Of the 32 requests of each aligned block of positions, exactly 4 move into each aligned block.
All inputs are finite; a program needn't handle non-finite values.
Results may differ from the reference program's by a relative error of at most 0.0095.
Values may be sent and summed in bfloat16 or wider, within the bound.
No kernel may reach another device: no remote copies, remote signals or barrier semaphores. Data moves between devices by JAX's collectives and lax.ppermute only.
A program may use at most 256 MiB of HBM per device.

```python
import jax
import jax.numpy as jnp
from jax import lax

D = 2048
HS = 64
HEADS = 32
FF = 4096
DECAY_RANK = 96
ALPHA_RANK = 96
GATE_RANK = 256
TOKENS_REQ = 4
REQ_DEV = 32
REQUESTS = 256
PER_PAIR = 4


def shuffle_rows(key, group_count):

    def one_row(subkey):
        return jax.random.permutation(subkey, REQ_DEV).astype(jnp.int32)
    return jax.vmap(one_row)(jax.random.split(key, group_count))


def draw_new_owner(key, part):
    group_count = REQUESTS // REQ_DEV
    key_one = jax.random.fold_in(key, 11)
    key_two = jax.random.fold_in(key, 23)
    shuffle = shuffle_rows(key_one, group_count)
    target = shuffle // PER_PAIR
    within = jnp.arange(group_count, dtype=jnp.int32)[:, None] * PER_PAIR + shuffle % PER_PAIR
    arrival = shuffle_rows(key_two, group_count)
    placed = target * REQ_DEV + arrival[target, within]
    return placed.reshape(-1).astype(jnp.int32)


def draw_head_params(key, part):
    unit_draw = jax.random.uniform(key, (7, D), jnp.float32)
    low_ends = jnp.array([-5.0, -2.0, 0.5, 0.0, -1.0, 0.5, -0.5], jnp.float32)
    high_ends = jnp.array([2.0, 2.0, 1.5, 1.0, 1.0, 1.5, 0.5], jnp.float32)
    return low_ends[:, None] + (high_ends - low_ends)[:, None] * unit_draw


def set_ends(values, key, low, top_value):
    longest = values.shape.index(max(values.shape))
    spots = []
    for shift in (0, 1):
        where = [jax.random.randint(jax.random.fold_in(key, axis), (), 0, length) for axis, length in enumerate(values.shape)]
        where[longest] = (where[longest] + shift) % values.shape[longest]
        spots.append(tuple(where))
    return values.at[spots[0]].set(low).at[spots[1]].set(top_value)


def block_scale(key, dims, cuts, least, high):
    level, own = 1.0, jax.random.fold_in(key, 6)
    for axis_at, shards_of in cuts:
        steps = jnp.exp(jax.random.uniform(jax.random.fold_in(own, axis_at), (shards_of,), jnp.float32, least / len(cuts), high / len(cuts)))
        level = level * jnp.repeat(steps, dims[axis_at] // shards_of).reshape([-1 if axis == axis_at else 1 for axis in range(len(dims))])
    return level


def centred(own_key, dims, deviation, reach, cuts=(), kind=jnp.bfloat16):
    drawn = jax.random.normal(own_key, dims, jnp.float32) * deviation
    if len(cuts) > 0:
        drawn = block_scale(own_key, dims, cuts, -0.22, 0.18) * drawn
    return jnp.clip(drawn, min=-reach, max=reach).astype(kind)


def setup_inputs(seed: int = 0) -> dict:
    key_of = jax.random.split(jax.random.key(seed), 22)
    return {
        "tokens": centred(key_of[0], (REQUESTS, TOKENS_REQ, D), 1.0, 6.0, ((0, 8), (2, 4))),
        "counts": set_ends(jax.random.randint(key_of[1], (REQUESTS,), 1, TOKENS_REQ + 1), jax.random.fold_in(key_of[1], 1), 1, TOKENS_REQ).astype(jnp.int32),
        "new_owner": draw_new_owner(jax.random.fold_in(key_of[21], 71), 0),
        "wkv_state": centred(key_of[3], (REQUESTS, HEADS, HS * HS), 2.0, 12.0, ((0, 8), (1, 4)), jnp.float32),
        "att_shift": centred(key_of[4], (REQUESTS, D), 1.0, 6.0, ((0, 8), (1, 4))),
        "ffn_shift": centred(key_of[5], (REQUESTS, D), 1.0, 6.0, ((0, 8), (1, 4))),
        "norm_params": jnp.clip(1.0 + 0.15 * jax.random.normal(key_of[6], (4, D), jnp.float32), 0.25, 1.75),
        "mix_coeffs": jnp.clip(jax.random.uniform(key_of[7], (7, D), jnp.float32, 0.0, 1.0), 0.0, 1.0),
        "head_params": draw_head_params(jax.random.fold_in(key_of[21], 71), 0),
        "recept_weight": centred(key_of[9], (D, D), D ** -0.5, 0.125, ((1, 4),)),
        "key_weight": centred(key_of[10], (D, D), D ** -0.5, 0.125, ((1, 4),)),
        "value_weight": centred(key_of[11], (D, D), D ** -0.5, 0.125, ((1, 4),)),
        "output_weight": centred(key_of[12], (D, D), D ** -0.5, 0.125, ((0, 4),)),
        "decay_down": centred(key_of[13], (D, DECAY_RANK), D ** -0.5, 0.125, ((0, 4),)),
        "decay_up": centred(key_of[14], (DECAY_RANK, D), DECAY_RANK ** -0.5, 0.625, ((1, 4),)),
        "alpha_down": centred(key_of[15], (D, ALPHA_RANK), D ** -0.5, 0.125, ((0, 4),)),
        "alpha_up": centred(key_of[16], (ALPHA_RANK, D), ALPHA_RANK ** -0.5, 0.625, ((1, 4),)),
        "gate_down": centred(key_of[17], (D, GATE_RANK), D ** -0.5, 0.125, ((0, 4),)),
        "gate_up": centred(key_of[18], (GATE_RANK, D), GATE_RANK ** -0.5, 0.375, ((1, 4),)),
        "ffn_key_weight": centred(key_of[19], (D, FF), D ** -0.5, 0.125, ((1, 4),)),
        "ffn_value_weight": centred(key_of[20], (FF, D), FF ** -0.5, 0.09375, ((0, 4),)),
    }


def layer_norm(stream, gain_row, offset):
    center = stream - lax.optimization_barrier(jnp.mean(stream, axis=-1, keepdims=True))
    spread = lax.optimization_barrier(jnp.mean(center * center, axis=-1, keepdims=True))
    return center / jnp.sqrt(spread + 1e-05) * gain_row + offset

def project(inputs, weight):
    return jnp.dot(inputs, weight, preferred_element_type=jnp.float32)

def advance(wkv_square, decay_now, key_now, value_now, unit_now, alpha_now, recept_now, is_valid):
    removal = -lax.optimization_barrier(jnp.sum(wkv_square * unit_now[:, :, None, :], axis=-1))
    updated = wkv_square * decay_now[:, :, None, :] + removal[..., None] * (unit_now * alpha_now)[:, :, None, :] + value_now[..., None] * key_now[:, :, None, :]
    memory_matrix_product = lax.optimization_barrier(jnp.sum(updated * recept_now[:, :, None, :], axis=-1))
    return (jnp.where(is_valid[:, None, None, None], updated, wkv_square), memory_matrix_product)

def time_heads(acceptance_matrix_lines, key_proj, values, decay_rate, in_context, sigmoid_scaling_entries, wkv_flat, counts, learned_weights, head_size):
    sequence_batch_count, decode_loop_steps_count, entire_channel_count = acceptance_matrix_lines.shape
    head_count = entire_channel_count // head_size

    def divided_into_groups(source):
        return source.reshape(sequence_batch_count, decode_loop_steps_count, head_count, head_size)
    scaled = divided_into_groups(key_proj * learned_weights[2])
    key_unit = scaled / jnp.sqrt(lax.optimization_barrier(jnp.sum(scaled * scaled, axis=-1, keepdims=True)) + 1e-06)
    lookup_adjust_factor = key_proj * (1.0 + (in_context - 1.0) * learned_weights[3])
    decay_heads = divided_into_groups(decay_rate)
    alpha_heads = divided_into_groups(in_context)
    recept_heads = divided_into_groups(acceptance_matrix_lines)
    payload_each_group = divided_into_groups(values)
    keymod_heads = divided_into_groups(lookup_adjust_factor)
    wkv_square = wkv_flat.reshape(sequence_batch_count, head_count, head_size, head_size)
    readouts = []
    for position in range(decode_loop_steps_count):
        is_valid = counts > position
        wkv_square, memory_matrix_product = advance(wkv_square, decay_heads[:, position], keymod_heads[:, position], payload_each_group[:, position], key_unit[:, position], alpha_heads[:, position], recept_heads[:, position], is_valid)
        readouts.append(memory_matrix_product)
    stacked = jnp.stack(readouts, axis=1)
    center = stacked - lax.optimization_barrier(jnp.mean(stacked, axis=-1, keepdims=True))
    spread = lax.optimization_barrier(jnp.mean(center * center, axis=-1, keepdims=True))
    layernormed_activations = (center / jnp.sqrt(spread + 0.00064)).reshape(sequence_batch_count, decode_loop_steps_count, entire_channel_count) * learned_weights[5] + learned_weights[6]
    extra_term_share = lax.optimization_barrier(jnp.sum(divided_into_groups(acceptance_matrix_lines * lookup_adjust_factor * learned_weights[4]), axis=-1, keepdims=True)) * payload_each_group
    attention_group_result = ((layernormed_activations + extra_term_share.reshape(sequence_batch_count, decode_loop_steps_count, entire_channel_count)) * sigmoid_scaling_entries).astype(jnp.bfloat16)
    return (attention_group_result, wkv_square.reshape(sequence_batch_count, head_count, head_size * head_size))

def reference(tokens, counts, new_owner, wkv_state, att_shift, ffn_shift, norm_params, mix_coeffs, head_params, recept_weight, key_weight, value_weight, output_weight, decay_down, decay_up, alpha_down, alpha_up, gate_down, gate_up, ffn_key_weight, ffn_value_weight):
    sequence_batch_count, decode_loop_steps_count, entire_channel_count = tokens.shape
    head_size = entire_channel_count // wkv_state.shape[1]
    moved_state = jnp.zeros_like(wkv_state).at[new_owner].set(wkv_state)
    moved_att = jnp.zeros_like(att_shift).at[new_owner].set(att_shift)
    moved_ffn = jnp.zeros_like(ffn_shift).at[new_owner].set(ffn_shift)
    stream = tokens.astype(jnp.float32)
    normed_one = layer_norm(stream, norm_params[0], norm_params[1])
    before_one = jnp.concatenate([moved_att.astype(jnp.float32)[:, None], normed_one[:, :-1]], axis=1)
    delta_one = before_one - normed_one
    row_count = sequence_batch_count * decode_loop_steps_count

    def mixed_input(mix_index):
        return (normed_one + delta_one * mix_coeffs[mix_index]).astype(jnp.bfloat16).reshape(row_count, entire_channel_count)
    acceptance_matrix_lines = project(mixed_input(0), recept_weight)
    decay_low = jnp.tanh(project(mixed_input(1), decay_down)).astype(jnp.bfloat16)
    key_proj = project(mixed_input(2), key_weight)
    values = project(mixed_input(3), value_weight)
    alpha_low = project(mixed_input(4), alpha_down).astype(jnp.bfloat16)
    gate_low = jax.nn.sigmoid(project(mixed_input(5), gate_down)).astype(jnp.bfloat16)
    decay_rate = jnp.exp(-0.606531 * jax.nn.sigmoid(head_params[0] + project(decay_low, decay_up)))
    in_context = jax.nn.sigmoid(head_params[1] + project(alpha_low, alpha_up))
    sigmoid_scaling_entries = project(gate_low, gate_up)
    block_size = 128 if sequence_batch_count % 128 == 0 else sequence_batch_count
    block_count = sequence_batch_count // block_size

    def blocked(source):
        return source.reshape((block_count, block_size) + source.shape[1:])

    def tokened(source):
        return source.reshape(block_count, block_size, decode_loop_steps_count, entire_channel_count)

    def per_block(pieces):
        return time_heads(pieces[0], pieces[1], pieces[2], pieces[3], pieces[4], pieces[5], pieces[6], pieces[7], head_params, head_size)
    head_blocks, state_blocks = lax.map(per_block, (tokened(acceptance_matrix_lines), tokened(key_proj), tokened(values), tokened(decay_rate), tokened(in_context), tokened(sigmoid_scaling_entries), blocked(moved_state), blocked(counts)))
    attention_group_result = head_blocks.reshape(row_count, entire_channel_count)
    new_state = state_blocks.reshape(wkv_state.shape)
    attended = project(attention_group_result, output_weight).reshape(sequence_batch_count, decode_loop_steps_count, entire_channel_count)
    midstream = (stream + attended).astype(jnp.bfloat16)
    normed_two = layer_norm(midstream.astype(jnp.float32), norm_params[2], norm_params[3])
    before_two = jnp.concatenate([moved_ffn.astype(jnp.float32)[:, None], normed_two[:, :-1]], axis=1)
    ffn_in = (normed_two + (before_two - normed_two) * mix_coeffs[6]).astype(jnp.bfloat16).reshape(row_count, entire_channel_count)
    hidden = jnp.square(jax.nn.relu(project(ffn_in, ffn_key_weight))).astype(jnp.bfloat16)
    ffn_out = project(hidden, ffn_value_weight).reshape(sequence_batch_count, decode_loop_steps_count, entire_channel_count)
    slot_ids = jnp.arange(decode_loop_steps_count, dtype=jnp.int32)
    live_slots = slot_ids[None, :] < counts[:, None]
    block_output = jnp.where(live_slots[..., None], midstream.astype(jnp.float32) + ffn_out, 0.0).astype(jnp.bfloat16)
    chosen = (slot_ids[None, :] == (counts - 1)[:, None]).astype(jnp.float32)
    new_att_shift = lax.optimization_barrier(jnp.sum(normed_one * chosen[..., None], axis=1)).astype(jnp.bfloat16)
    new_ffn_shift = lax.optimization_barrier(jnp.sum(normed_two * chosen[..., None], axis=1)).astype(jnp.bfloat16)
    return (block_output, new_state, new_att_shift, new_ffn_shift)
```

```python
import functools

import jax
import jax.numpy as jnp
from jax import lax
from jax.experimental import pallas as pl
from jax.experimental.pallas import tpu as pltpu
from jax.sharding import PartitionSpec as P

F32 = jnp.float32
BF16 = jnp.bfloat16
VMEM_LIMIT = 56 * 1024 * 1024


def xor_permute(x, axis, size, k):
    return lax.ppermute(x, axis, [(a, a ^ k) for a in range(size)])


def params(limit=VMEM_LIMIT):
    return pltpu.CompilerParams(vmem_limit_bytes=limit)


def full_spec(shape):
    return pl.BlockSpec(shape, lambda *_: (0,) * len(shape))


def dot32(a, b):
    return jnp.dot(a, b, preferred_element_type=F32)


def pack_states(wkv_state, order, per_pair, groups):
    heads, cells = wkv_state.shape[1:]

    def body(order_ref, in_ref, *out_refs):
        step = pl.program_id(0)
        for k in range(groups):

            @pl.when(step // per_pair == k)
            def _():
                out_refs[k][...] = in_ref[...].astype(BF16)

    def out_map(k, step, order_ref):
        return (jnp.clip(step - k * per_pair, 0, per_pair - 1), 0, 0)

    return pl.pallas_call(
        body,
        grid_spec=pltpu.PrefetchScalarGridSpec(
            num_scalar_prefetch=1,
            grid=(groups * per_pair,),
            in_specs=[pl.BlockSpec((1, heads, cells), lambda s, o: (o[s], 0, 0))],
            out_specs=[
                pl.BlockSpec((1, heads, cells), functools.partial(out_map, k))
                for k in range(groups)
            ],
        ),
        out_shape=[jax.ShapeDtypeStruct((per_pair, heads, cells), BF16) for _ in range(groups)],
        compiler_params=params(),
        name="pack_states",
    )(order, wkv_state)


def states_to_lanes(rank, payloads, requests, lanes):
    groups = len(payloads)
    per_pair, heads, cells = payloads[0].shape
    head_size = 64
    step_chunks = 4
    steps = cells // (128 * step_chunks)
    half = lanes // requests
    halves = heads // half

    def body(rank_ref, *refs):
        ins, out_ref, rows = refs[:groups], refs[groups], refs[groups + 1]
        for c in range(step_chunks):
            for k in range(groups):
                base = (rank_ref[0] ^ k) * (per_pair * heads)
                for j in range(per_pair):
                    tile = ins[k][j, :, c * 128 : (c + 1) * 128].astype(F32)
                    rows[c, pl.ds(pl.multiple_of(base + j * heads, heads), heads), :] = tile
        for c in range(step_chunks):
            for g in range(halves):
                block = jnp.concatenate(
                    [
                        rows[c, pl.ds(g * half + h, requests, stride=heads), :]
                        for h in range(half)
                    ],
                    axis=0,
                )
                turned = block.T
                out_ref[g, 2 * c] = turned[:head_size]
                out_ref[g, 2 * c + 1] = turned[head_size:]

    return pl.pallas_call(
        body,
        grid_spec=pltpu.PrefetchScalarGridSpec(
            num_scalar_prefetch=1,
            grid=(steps,),
            in_specs=[
                pl.BlockSpec((per_pair, heads, 128 * step_chunks), lambda s, r: (0, 0, s))
                for _ in range(groups)
            ],
            out_specs=pl.BlockSpec(
                (halves, 2 * step_chunks, head_size, lanes), lambda s, r: (0, s, 0, 0)
            ),
            scratch_shapes=[pltpu.VMEM((step_chunks, requests * heads, 128), F32)],
        ),
        out_shape=jax.ShapeDtypeStruct((halves, cells // head_size, head_size, lanes), F32),
        compiler_params=params(),
        name="states_to_lanes",
    )(rank, *payloads)


def first_norm(place, toks, atts, row_source, count_col, back_col, norm, mix, downs):
    rows, width = toks[0].shape
    parts = len(toks)
    total = parts * width
    requests = count_col.shape[0]
    slots = rows // requests
    rank_d, rank_a, rank_g = [w.shape[1] for w in downs]

    def body(place_ref, *refs):
        tok = refs[:parts]
        att = refs[parts : 2 * parts]
        src, cnt, back, nrm, mx, dd, ad, gd = refs[2 * parts : 2 * parts + 8]
        normed_ref, low_ref, lowsend_ref, shift_ref = refs[2 * parts + 8 :]
        pick = (lax.broadcasted_iota(jnp.int32, (rows, rows), 1) == src[...]).astype(BF16)
        xs = [dot32(pick, t[...]) for t in tok]
        mean = sum(jnp.sum(x, axis=1, keepdims=True) for x in xs) / total
        cs = [x - mean for x in xs]
        var = sum(jnp.sum(c * c, axis=1, keepdims=True) for c in cs) / total
        scale = lax.rsqrt(var + 1e-05)
        for k in range(parts):
            at = pl.ds(pl.multiple_of((place_ref[0] ^ k) * width, 128), width)
            normed_ref[k] = cs[k] * scale * nrm[0:1, at] + nrm[1:2, at]
        at = pl.ds(pl.multiple_of(place_ref[0] * width, 128), width)
        now = normed_ref[0]
        before = jnp.concatenate([att[0][0:requests].astype(F32), now[: rows - requests]], axis=0)
        delta = before - now
        low_ref[...] = jnp.zeros(low_ref.shape, F32)
        low_ref[:, 0:rank_d] = dot32((now + delta * mx[1:2, at]).astype(BF16), dd[...])
        low_ref[:, 128 : 128 + rank_a] = dot32((now + delta * mx[4:5, at]).astype(BF16), ad[...])
        low_ref[:, 256 : 256 + rank_g] = dot32((now + delta * mx[5:6, at]).astype(BF16), gd[...])
        lowsend_ref[...] = low_ref[...].astype(BF16)
        chosen = jnp.zeros((requests, width), F32)
        for t in range(slots):
            chosen = jnp.where(cnt[...] == t + 1, now[t * requests : (t + 1) * requests], chosen)
        unpick = (
            lax.broadcasted_iota(jnp.int32, (requests, requests), 1) == back[...]
        ).astype(BF16)
        shift_ref[...] = dot32(unpick, chosen.astype(BF16)).astype(BF16)

    low_width = 256 + rank_g
    args = (*toks, *atts, row_source, count_col, back_col, norm, mix, *downs)
    return pl.pallas_call(
        body,
        grid_spec=pltpu.PrefetchScalarGridSpec(
            num_scalar_prefetch=1,
            grid=(1,),
            in_specs=[full_spec(a.shape) for a in args],
            out_specs=[
                full_spec((parts, rows, width)),
                full_spec((rows, low_width)),
                full_spec((rows, low_width)),
                full_spec((requests, width)),
            ],
        ),
        out_shape=[
            jax.ShapeDtypeStruct((parts, rows, width), F32),
            jax.ShapeDtypeStruct((rows, low_width), F32),
            jax.ShapeDtypeStruct((rows, low_width), BF16),
            jax.ShapeDtypeStruct((requests, width), BF16),
        ],
        compiler_params=params(),
        name="first_norm",
    )(place, *args)


def projections(place, normed, atts, mix, weights, requests):
    parts, rows, width = normed.shape
    out_width = weights[0].shape[1]

    def body(place_ref, n_ref, *refs):
        att = refs[:parts]
        mx = refs[parts]
        w = refs[parts + 1 : parts + 4]
        outs = refs[parts + 4 : parts + 7]
        k = pl.program_id(0)
        at = pl.ds(pl.multiple_of((place_ref[0] ^ k) * width, 128), width)
        now = n_ref[0]
        prev = att[0][0:requests]
        for other in range(1, parts):
            prev = jnp.where(k == other, att[other][0:requests], prev)
        before = jnp.concatenate([prev.astype(F32), now[: rows - requests]], axis=0)
        delta = before - now
        for which, c in enumerate((0, 2, 3)):
            term = dot32((now + delta * mx[c : c + 1, at]).astype(BF16), w[which][...])

            @pl.when(k == 0)
            def _():
                outs[which][...] = term

            @pl.when(k > 0)
            def _():
                outs[which][...] += term

    return pl.pallas_call(
        body,
        grid_spec=pltpu.PrefetchScalarGridSpec(
            num_scalar_prefetch=1,
            grid=(parts,),
            in_specs=[pl.BlockSpec((1, rows, width), lambda k, p: (k, 0, 0))]
            + [full_spec(a.shape) for a in atts]
            + [full_spec(mix.shape)]
            + [pl.BlockSpec((width, out_width), lambda k, p: (p[0] ^ k, 0)) for _ in weights],
            out_specs=[full_spec((rows, out_width)) for _ in weights],
        ),
        out_shape=[jax.ShapeDtypeStruct((rows, out_width), F32) for _ in weights],
        compiler_params=params(),
        name="projections",
    )(place, normed, *atts, mix, *weights)


def swap_groups(arrays, lane_group, flag_one, flag_two):
    a0, a1, a2, a3 = arrays
    lanes = 4 * lane_group
    up = lambda x: pltpu.roll(x, lane_group, 1)
    down = lambda x: pltpu.roll(x, lanes - lane_group, 1)
    far = lambda x: pltpu.roll(x, 2 * lane_group, 1)
    b0 = jnp.where(flag_one, a0, up(a1))
    b1 = jnp.where(flag_one, down(a0), a1)
    b2 = jnp.where(flag_one, a2, up(a3))
    b3 = jnp.where(flag_one, down(a2), a3)
    return [
        jnp.where(flag_two, b0, far(b2)),
        jnp.where(flag_two, b1, far(b3)),
        jnp.where(flag_two, far(b0), b2),
        jnp.where(flag_two, far(b1), b3),
    ]


def fold_eight(items, flags):
    shift = 1
    for flag in flags:
        items = [
            jnp.where(flag, a, b) + pltpu.roll(jnp.where(flag, b, a), shift, 0)
            for a, b in zip(items[0::2], items[1::2])
        ]
        shift *= 2
    return items[0]


def heads_step(
    place, low_own, low_others, recept, key, value, states, head_params, ups, out_weight, count_row
):
    rows, width = recept.shape
    halves, size, _, lanes = states.shape
    parts = len(low_others) + 1
    slots = 4
    requests = rows // slots
    half = lanes // requests
    n_groups = width // 128
    rank_d, rank_a, rank_g = [w.shape[0] for w in ups]

    def body(place_ref, *refs):
        low = refs[0]
        others = refs[1:parts]
        (r_ref, k_ref, v_ref, st_hbm, hp, du, au, gu, wo_hbm, cnt) = refs[parts : parts + 10]
        outs = refs[parts + 10 : 2 * parts + 10]
        p_out, v_out, kq_out, uq_out, d_out = refs[2 * parts + 10 : 2 * parts + 15]
        st, wo, vec, wvec, prod, normed, sems = refs[2 * parts + 15 :]
        copy_states = pltpu.make_async_copy(st_hbm, st, sems.at[0])
        copy_weight = pltpu.make_async_copy(wo_hbm, wo, sems.at[1])
        copy_states.start()
        copy_weight.start()

        total = low[...]
        for o in others:
            total = total + o[...].astype(F32)
        dlow = jnp.tanh(total[:, 0:rank_d]).astype(BF16)
        alow = total[:, 128 : 128 + rank_a].astype(BF16)
        glow = jax.nn.sigmoid(total[:, 256 : 256 + rank_g]).astype(BF16)
        decay = jnp.exp(-0.606531 * jax.nn.sigmoid(hp[0:1] + dot32(dlow, du[...])))
        context = jax.nn.sigmoid(hp[1:2] + dot32(alow, au[...]))
        gate = dot32(glow, gu[...])
        r = r_ref[...]
        k = k_ref[...]
        v = v_ref[...]
        scaled = k * hp[2:3]
        kmod = k * (1.0 + (context - 1.0) * hp[3:4])
        rk = r * kmod * hp[4:5]

        lane = lax.broadcasted_iota(jnp.int32, (size, lanes), 1)
        flag_one = (lane // requests) % 2 == 0
        flag_two = (lane // requests) // 2 == 0
        for index, array in enumerate((r, kmod, scaled, decay, context, v)):
            pieces = []
            for g in range(n_groups):
                turned = array[:, g * 128 : (g + 1) * 128].T
                pieces += [turned[:size], turned[size:]]
            for g in range(halves):
                swapped = swap_groups(pieces[g * half : (g + 1) * half], requests, flag_one, flag_two)
                for t in range(slots):
                    vec[index, g, t] = swapped[t]

        sub = lax.broadcasted_iota(jnp.int32, (8, lanes), 0)
        folds = [(sub // s) % 2 == 0 for s in (1, 2, 4)]
        valid = [cnt[...] > t for t in range(slots)]
        ksum = lambda x, y: jnp.sum(x * y, axis=0, keepdims=True)

        coefs = []
        for g in range(halves):
            for t in range(slots):
                s = vec[2, g, t]
                unit = s * lax.rsqrt(jnp.sum(s * s, axis=0, keepdims=True) + 1e-06)
                vec[2, g, t] = unit
                vec[4, g, t] = unit * vec[4, g, t]
            cu, cr = {}, {}

            def back_through(x, top, into, s):
                for b in range(top, -1, -1):
                    into[s, b] = jnp.where(valid[b], ksum(vec[1, g, b], x), 0.0)
                    moved = vec[3, g, b] * x - vec[2, g, b] * ksum(vec[4, g, b], x)
                    x = jnp.where(valid[b], moved, x)
                return x

            for t in range(slots):
                wvec[g, t] = back_through(vec[2, g, t], t - 1, cu, t)
                x = vec[0, g, t]
                cr[t, t] = ksum(vec[1, g, t], x)
                x = vec[3, g, t] * x - vec[2, g, t] * ksum(vec[4, g, t], x)
                wvec[g, slots + t] = back_through(x, t - 1, cr, t)
            coefs.append((cu, cr))
            run = jnp.ones((size, lanes), F32)
            for t in range(slots - 1, -1, -1):
                kq_out[g, t] = jnp.where(valid[t], vec[1, g, t] * run, 0.0)
                uq_out[g, t] = jnp.where(valid[t], -(vec[4, g, t] * run), 0.0)
                run = jnp.where(valid[t], run * vec[3, g, t], run)
                v_out[g, t] = vec[5, g, t]
            d_out[g] = run

        copy_states.wait()
        quad = 4
        for g in range(halves):
            for part in range(2 * slots // quad):

                def products(block, _):
                    ws = [wvec[g, part * quad + w] for w in range(quad)]
                    sums = [[] for _ in range(quad)]
                    for i in range(8):
                        s = st[g, block * 8 + i]
                        for w in range(quad):
                            term = s * ws[w]
                            acc = term[0:8]
                            for jv in range(1, size // 8):
                                acc = acc + term[jv * 8 : (jv + 1) * 8]
                            sums[w].append(acc)
                    for w in range(quad):
                        prod[g, part * quad + w, pl.ds(pl.multiple_of(block * 8, 8), 8), :] = (
                            fold_eight(sums[w], folds)
                        )
                    return 0

                lax.fori_loop(0, size // 8, products, 0)

        backs = []
        for g in range(halves):
            cu, cr = coefs[g]
            outs_t = []
            for t in range(slots):
                removed = prod[g, t]
                y = prod[g, slots + t] + cr[t, t] * vec[5, g, t]
                for b in range(t):
                    removed = removed + cu[t, b] * vec[5, g, b]
                    y = y + cr[t, b] * vec[5, g, b]
                p_out[g, t] = removed
                center = y - jnp.mean(y, axis=0, keepdims=True)
                spread = jnp.mean(center * center, axis=0, keepdims=True)
                outs_t.append(center * lax.rsqrt(spread + 0.00064))
            backs += swap_groups(outs_t, requests, flag_one, flag_two)
        lane_r = lax.broadcasted_iota(jnp.int32, (128, 128), 0)
        lane_c = lax.broadcasted_iota(jnp.int32, (128, 128), 1)
        ones = ((lane_r // size) == (lane_c // size)).astype(BF16)
        for g in range(n_groups):
            cols = slice(g * 128, (g + 1) * 128)
            turned = jnp.concatenate([backs[2 * g], backs[2 * g + 1]], axis=0).T
            rkg = rk[:, cols]
            high = rkg.astype(BF16)
            bonus = dot32(high, ones) + dot32((rkg - high.astype(F32)).astype(BF16), ones)
            done = (turned * hp[5:6, cols] + hp[6:7, cols] + bonus * v[:, cols]) * gate[:, cols]
            normed[:, cols] = done.astype(BF16)
        copy_weight.wait()
        for q in range(parts):
            at = pl.ds(pl.multiple_of((place_ref[0] ^ q) * width, 128), width)
            outs[q][...] = dot32(normed[...], wo[:, at]).astype(outs[q].dtype)

    vector = lambda n: jax.ShapeDtypeStruct((halves, n, size, lanes), F32)
    args = (low_own, *low_others, recept, key, value)
    out_shape = (
        [jax.ShapeDtypeStruct((rows, width), F32)]
        + [jax.ShapeDtypeStruct((rows, width), BF16) for _ in range(parts - 1)]
        + [vector(slots) for _ in range(4)]
        + [jax.ShapeDtypeStruct((halves, size, lanes), F32)]
    )
    anywhere = pl.BlockSpec(memory_space=pl.ANY)
    return pl.pallas_call(
        body,
        grid_spec=pltpu.PrefetchScalarGridSpec(
            num_scalar_prefetch=1,
            grid=(1,),
            in_specs=[full_spec(a.shape) for a in args]
            + [anywhere, full_spec(head_params.shape)]
            + [full_spec(u.shape) for u in ups]
            + [anywhere, full_spec(count_row.shape)],
            out_specs=[full_spec(o.shape) for o in out_shape],
            scratch_shapes=[
                pltpu.VMEM(states.shape, F32),
                pltpu.VMEM(out_weight.shape, BF16),
                pltpu.VMEM((6, halves, slots, size, lanes), F32),
                pltpu.VMEM((halves, 2 * slots, size, lanes), F32),
                pltpu.VMEM((halves, 2 * slots, size, lanes), F32),
                pltpu.VMEM((rows, width), BF16),
                pltpu.SemaphoreType.DMA((2,)),
            ],
        ),
        out_shape=out_shape,
        compiler_params=params(),
        name="heads_step",
    )(place, *args, states, head_params, *ups, out_weight, count_row)


def final_states(arriving, states, removed, values, keys, units, decay, heads):
    halves, size, _, lanes = states.shape
    slots = removed.shape[1]
    requests = arriving.shape[0]
    half = lanes // requests
    step_chunks = 4
    steps = size // (2 * step_chunks)
    cells = size * size

    def body(arr_ref, st, p_ref, v_ref, kq_ref, uq_ref, d_ref, out_ref, new, rows):
        for g in range(halves):

            def update(block, _):
                first = block * 4
                lefts = []
                for i in range(4):
                    row = [v_ref[g, t, pl.ds(first + i, 1), :] for t in range(slots)]
                    row += [p_ref[g, t, pl.ds(first + i, 1), :] for t in range(slots)]
                    lefts.append([jnp.broadcast_to(x, (8, lanes)) for x in row])
                for jv in range(size // 8):
                    at = slice(jv * 8, (jv + 1) * 8)
                    rights = [kq_ref[g, t, at, :] for t in range(slots)]
                    rights += [uq_ref[g, t, at, :] for t in range(slots)]
                    decayed = d_ref[g, at, :]
                    for i in range(4):
                        acc = st[g, first + i, at, :] * decayed
                        for left, right in zip(lefts[i], rights):
                            acc = acc + left * right
                        new[g, first + i, at, :] = acc
                return 0

            lax.fori_loop(0, 2 * step_chunks // 4, update, 0)
        for c in range(step_chunks):
            for g in range(halves):
                turned = jnp.concatenate([new[g, 2 * c], new[g, 2 * c + 1]], axis=0).T
                for h in range(half):
                    rows[c, pl.ds(g * half + h, requests, stride=heads), :] = turned[
                        h * requests : (h + 1) * requests
                    ]
        for c in range(step_chunks):
            for q in range(requests):
                out_ref[arr_ref[q], :, c * 128 : (c + 1) * 128] = rows[
                    c, q * heads : (q + 1) * heads, :
                ]

    per_step = lambda s, a: (0, 0, s, 0)
    return pl.pallas_call(
        body,
        grid_spec=pltpu.PrefetchScalarGridSpec(
            num_scalar_prefetch=1,
            grid=(steps,),
            in_specs=[
                pl.BlockSpec((halves, 2 * step_chunks, size, lanes), lambda s, a: (0, s, 0, 0)),
                pl.BlockSpec((halves, slots, 2 * step_chunks, lanes), per_step),
                pl.BlockSpec((halves, slots, 2 * step_chunks, lanes), per_step),
                full_spec(keys.shape),
                full_spec(units.shape),
                full_spec(decay.shape),
            ],
            out_specs=pl.BlockSpec((requests, heads, 128 * step_chunks), lambda s, a: (0, 0, s)),
            scratch_shapes=[
                pltpu.VMEM((halves, 2 * step_chunks, size, lanes), F32),
                pltpu.VMEM((step_chunks, requests * heads, 128), F32),
            ],
        ),
        out_shape=jax.ShapeDtypeStruct((requests, heads, cells), F32),
        compiler_params=params(),
        name="final_states",
    )(arriving, states, removed, values, keys, units, decay)


def middle(tok, row_source, own, others):
    rows, width = tok.shape

    def body(tok_ref, src, own_ref, *refs):
        out = refs[-1]
        pick = (lax.broadcasted_iota(jnp.int32, (rows, rows), 1) == src[...]).astype(BF16)
        total = dot32(pick, tok_ref[...]) + own_ref[...]
        for o in refs[:-1]:
            total = total + o[...].astype(F32)
        out[...] = total.astype(BF16)

    args = (tok, row_source, own, *others)
    return pl.pallas_call(
        body,
        grid=(1,),
        in_specs=[full_spec(a.shape) for a in args],
        out_specs=full_spec((rows, width)),
        out_shape=jax.ShapeDtypeStruct((rows, width), BF16),
        compiler_params=params(),
        name="middle",
    )(*args)


def channel_mix(place, mids, prevs, count_col, back_col, norm, mix, key_weight, value_weight):
    parts = len(mids)
    rows, width = mids[0].shape
    total = parts * width
    hidden_width = key_weight.shape[1]
    requests = count_col.shape[0]
    slots = rows // requests

    def body(place_ref, *refs):
        mid = refs[:parts]
        prev = refs[parts : 2 * parts]
        cnt, back, nrm, mx, kw, vw = refs[2 * parts : 2 * parts + 6]
        outs = refs[2 * parts + 6 : 3 * parts + 6]
        shift_ref, inputs, acc, hidden = refs[3 * parts + 6 :]
        step = pl.program_id(0)

        @pl.when(step == 0)
        def _():
            xs = [m[...].astype(F32) for m in mid]
            mean = sum(jnp.sum(x, axis=1, keepdims=True) for x in xs) / total
            cs = [x - mean for x in xs]
            var = sum(jnp.sum(c * c, axis=1, keepdims=True) for c in cs) / total
            scale = lax.rsqrt(var + 1e-05)
            for k in range(parts):
                at = pl.ds(pl.multiple_of((place_ref[0] ^ k) * width, 128), width)
                now = cs[k] * scale * nrm[2:3, at] + nrm[3:4, at]
                before = jnp.concatenate(
                    [prev[k][requests:].astype(F32), now[: rows - requests]], axis=0
                )
                inputs[k] = (now + (before - now) * mx[6:7, at]).astype(BF16)
                if k == 0:
                    chosen = jnp.zeros((requests, width), F32)
                    for t in range(slots):
                        chosen = jnp.where(
                            cnt[...] == t + 1, now[t * requests : (t + 1) * requests], chosen
                        )
                    unpick = (
                        lax.broadcasted_iota(jnp.int32, (requests, requests), 1) == back[...]
                    ).astype(BF16)
                    shift_ref[...] = dot32(unpick, chosen.astype(BF16)).astype(BF16)
            acc[...] = dot32(inputs[0], kw[...])

        @pl.when((step > 0) & (step < parts))
        def _():
            acc[...] += dot32(inputs[step], kw[...])

        @pl.when(step == parts - 1)
        def _():
            h = jnp.maximum(acc[...], 0.0)
            hidden[...] = (h * h).astype(BF16)

        for q in range(parts):

            @pl.when(step == parts + q)
            def _():
                outs[q][...] = dot32(hidden[...], vw[...]).astype(outs[q].dtype)

    args = (*mids, *prevs, count_col, back_col, norm, mix)
    return pl.pallas_call(
        body,
        grid_spec=pltpu.PrefetchScalarGridSpec(
            num_scalar_prefetch=1,
            grid=(2 * parts,),
            in_specs=[full_spec(a.shape) for a in args]
            + [
                pl.BlockSpec(
                    (width, hidden_width), lambda s, p: (p[0] ^ jnp.minimum(s, parts - 1), 0)
                ),
                pl.BlockSpec(
                    (hidden_width, width), lambda s, p: (0, p[0] ^ jnp.maximum(s - parts, 0))
                ),
            ],
            out_specs=[full_spec((rows, width)) for _ in range(parts)]
            + [full_spec((requests, width))],
            scratch_shapes=[
                pltpu.VMEM((parts, rows, width), BF16),
                pltpu.VMEM((rows, hidden_width), F32),
                pltpu.VMEM((rows, hidden_width), BF16),
            ],
        ),
        out_shape=[jax.ShapeDtypeStruct((rows, width), F32)]
        + [jax.ShapeDtypeStruct((rows, width), BF16) for _ in range(parts - 1)]
        + [jax.ShapeDtypeStruct((requests, width), BF16)],
        compiler_params=params(),
        name="channel_mix",
    )(place, *args, key_weight, value_weight)


def finish(mid, own, others, live_col, row_back):
    rows, width = mid.shape

    def body(mid_ref, own_ref, *refs):
        out = refs[-1]
        live, back = refs[-3:-1]
        total = own_ref[...]
        for o in refs[:-3]:
            total = total + o[...].astype(F32)
        total = jnp.where(live[...] > 0, mid_ref[...].astype(F32) + total, 0.0).astype(BF16)
        pick = (lax.broadcasted_iota(jnp.int32, (rows, rows), 1) == back[...]).astype(BF16)
        out[...] = dot32(pick, total).astype(BF16)

    args = (mid, own, *others, live_col, row_back)
    return pl.pallas_call(
        body,
        grid=(1,),
        in_specs=[full_spec(a.shape) for a in args],
        out_specs=full_spec((rows, width)),
        out_shape=jax.ShapeDtypeStruct((rows, width), BF16),
        compiler_params=params(),
        name="finish",
    )(*args)


def per_device(
    groups,
    parts,
    tokens,
    counts,
    new_owner,
    wkv_state,
    att_shift,
    ffn_shift,
    norm_params,
    mix_coeffs,
    head_params,
    recept_weight,
    key_weight,
    value_weight,
    output_weight,
    decay_down,
    decay_up,
    alpha_down,
    alpha_up,
    gate_down,
    gate_up,
    ffn_key_weight,
    ffn_value_weight,
):
    requests, slots, width = tokens.shape
    heads = wkv_state.shape[1]
    per_pair = requests // groups
    rows = requests * slots
    rank = lax.axis_index("req").astype(jnp.int32)
    place = lax.axis_index("mdl").astype(jnp.int32)
    rank_one, place_one = rank.reshape(1), place.reshape(1)

    blocks = new_owner.reshape(groups, requests)
    target = blocks // requests
    ids = jnp.arange(requests, dtype=jnp.int32)
    own = lax.dynamic_slice_in_dim(new_owner, rank * requests, requests)
    own_target = own // requests
    own_turn = jnp.sum(
        (own_target[:, None] == own_target[None, :]) & (ids[None, :] < ids[:, None]), axis=1
    ).astype(jnp.int32)
    own_slot = own_target * per_pair + own_turn
    sending = jnp.sum(jnp.where(own_slot[None, :] == ids[:, None], ids[None, :], 0), axis=1)
    partner_slot = (own_target ^ rank) * per_pair + own_turn
    order = jnp.sum(jnp.where(partner_slot[None, :] == ids[:, None], ids[None, :], 0), axis=1)
    mine = target == rank
    turn = jnp.cumsum(mine.astype(jnp.int32), axis=1) - 1
    arrival = jnp.where(
        mine, jnp.arange(groups, dtype=jnp.int32)[:, None] * per_pair + turn, -1
    ).reshape(-1)
    local = new_owner - rank * requests
    arriving = jnp.sum(jnp.where(arrival[None, :] == ids[:, None], local[None, :], 0), axis=1)
    hit = arriving[None, :] == ids[:, None]
    inverse = jnp.sum(jnp.where(hit, ids[None, :], 0), axis=1)
    count_arr = jnp.sum(jnp.where(hit, counts[:, None], 0), axis=0)

    slot_ids = jnp.arange(slots, dtype=jnp.int32)
    row_source = (arriving[None, :] * slots + slot_ids[:, None]).reshape(rows, 1)
    row_back = (inverse[:, None] + slot_ids[None, :] * requests).reshape(rows, 1)
    live_col = (slot_ids[:, None] < count_arr[None, :]).astype(jnp.int32).reshape(rows, 1)
    count_col, back_col = count_arr[:, None], inverse[:, None]
    lanes = rows
    count_row = jnp.tile(count_arr, lanes // requests)[None, :]

    gather = lambda x: [x] + [xor_permute(x, "mdl", parts, k) for k in range(1, parts)]
    scatter = lambda xs: [xor_permute(xs[k], "mdl", parts, k) for k in range(1, parts)]

    toks = gather(tokens.reshape(rows, width))
    shifts = jnp.concatenate(
        [
            att_shift[sending].reshape(groups, per_pair, width),
            ffn_shift[sending].reshape(groups, per_pair, width),
        ],
        axis=1,
    )
    shifts = lax.all_to_all(shifts, "req", split_axis=0, concat_axis=0, tiled=True)
    shifts = jnp.concatenate(
        [
            shifts[:, :per_pair].reshape(requests, width),
            shifts[:, per_pair:].reshape(requests, width),
        ],
        axis=0,
    )
    prevs = gather(shifts)

    packed = pack_states(wkv_state, order, per_pair, groups)
    payloads = [packed[0]] + [xor_permute(packed[k], "req", groups, k) for k in range(1, groups)]
    states = states_to_lanes(rank_one, payloads, requests, lanes)

    normed, low, low_send, new_att = first_norm(
        place_one,
        toks,
        prevs,
        row_source,
        count_col,
        back_col,
        norm_params,
        mix_coeffs,
        (decay_down, alpha_down, gate_down),
    )
    low_others = gather(low_send)[1:]
    recept, key, value = projections(
        place_one, normed, prevs, mix_coeffs, (recept_weight, key_weight, value_weight), requests
    )
    results = heads_step(
        place_one,
        low,
        low_others,
        recept,
        key,
        value,
        states,
        head_params,
        (decay_up, alpha_up, gate_up),
        output_weight,
        count_row,
    )
    outs, (removed, vals, keys, units, decay) = results[:parts], results[parts:]
    mid = middle(toks[0], row_source, outs[0], scatter(outs))
    new_state = final_states(arriving, states, removed, vals, keys, units, decay, heads)
    mids = gather(mid)
    results = channel_mix(
        place_one,
        mids,
        prevs,
        count_col,
        back_col,
        norm_params,
        mix_coeffs,
        ffn_key_weight,
        ffn_value_weight,
    )
    outs, new_ffn = results[:parts], results[parts]
    block = finish(mid, outs[0], scatter(outs), live_col, row_back)
    return (block.reshape(requests, slots, width), new_state, new_att, new_ffn)


def solution(mesh):
    return jax.shard_map(
        functools.partial(per_device, mesh.shape["req"], mesh.shape["mdl"]),
        mesh=mesh,
        in_specs=(
            P("req", None, "mdl"),
            P("req"),
            P(),
            P("req", "mdl", None),
            P("req", "mdl"),
            P("req", "mdl"),
            P(),
            P(),
            P(None, "mdl"),
            P(None, "mdl"),
            P(None, "mdl"),
            P(None, "mdl"),
            P("mdl", None),
            P("mdl", None),
            P(None, "mdl"),
            P("mdl", None),
            P(None, "mdl"),
            P("mdl", None),
            P(None, "mdl"),
            P(None, "mdl"),
            P("mdl", None),
        ),
        out_specs=(P("req", None, "mdl"), P("req", "mdl", None), P("req", "mdl"), P("req", "mdl")),
        check_vma=False,
    )
```

```python
import functools

import jax
import jax.numpy as jnp
from jax import lax
from jax.experimental import pallas as pl
from jax.experimental.pallas import tpu as pltpu
from jax.sharding import PartitionSpec as P

F32 = jnp.float32
BF16 = jnp.bfloat16
I32 = jnp.int32
SCRATCH_LIMIT = 16 * 1024 * 1024


def xor_permute(x, axis, size, k):
    return lax.ppermute(x, axis, [(a, a ^ k) for a in range(size)])


def dot32(a, b):
    return jnp.dot(a, b, preferred_element_type=F32)


def dot32_turned(a, b):
    return lax.dot_general(a, b, (((1,), (1,)), ((), ())), preferred_element_type=F32)


def vmem(shape, dtype):
    return pltpu.VMEM(shape, dtype)


def run(body, name, scalars, args, outs, scratch=(), in_hbm=(), out_hbm=()):
    anywhere = pl.BlockSpec(memory_space=pl.ANY)
    near = pl.BlockSpec(memory_space=pltpu.VMEM)
    return pl.pallas_call(
        body,
        grid_spec=pltpu.PrefetchScalarGridSpec(
            num_scalar_prefetch=len(scalars),
            grid=(1,),
            in_specs=[anywhere if i in in_hbm else near for i in range(len(args))],
            out_specs=[
                pl.BlockSpec(memory_space=pltpu.SMEM)
                if o.memory_space == pltpu.SMEM
                else anywhere if i in out_hbm else near
                for i, o in enumerate(outs)
            ],
            scratch_shapes=scratch,
        ),
        out_shape=[
            jax.ShapeDtypeStruct(o.shape, o.dtype)
            if o.memory_space == pltpu.SMEM or i in out_hbm
            else o
            for i, o in enumerate(outs)
        ],
        compiler_params=pltpu.CompilerParams(vmem_limit_bytes=SCRATCH_LIMIT),
        name=name,
    )(
        *scalars,
        *[
            a if i in in_hbm else pltpu.with_memory_space_constraint(a, pltpu.VMEM)
            for i, a in enumerate(args)
        ],
    )


def positions(groups):
    return list(range(0, groups, 2)) + list(range(1, groups, 2))


SOURCE, BACK, LIVE, COUNT, UNSORT, ATT, FFN = range(7)


def make_plan(rank, new_owner, counts, att, ffn, groups, slots):
    requests, width = att.shape
    per_pair = requests // groups
    rows = requests * slots
    sent_rows = 2 * requests

    def body(
        rank_ref, owner, cnt, att_ref, ffn_ref, order, arriving, cols, lanes_ref, sent_ref,
        turn, inverse, att_f, ffn_f, sent_f,
    ):
        me = rank_ref[0]

        def place_of(k):
            return k // 2 + (k % 2) * (groups // 2)

        for g in range(groups):
            turn[g] = 0

        def own(i, _):
            spot = place_of((owner[me * requests + i] // requests) ^ me)
            order[spot * per_pair + turn[spot]] = i
            turn[spot] = turn[spot] + 1
            return 0

        lax.fori_loop(0, requests, own, 0)

        def source(s, _):
            base = place_of(s ^ me) * per_pair

            def one(i, found):
                v = owner[s * requests + i]
                mine = v // requests == me

                @pl.when(mine)
                def _():
                    arriving[base + found] = v % requests
                    inverse[v % requests] = base + found

                return found + mine.astype(I32)

            lax.fori_loop(0, requests, one, jnp.int32(0))
            return 0

        lax.fori_loop(0, groups, source, 0)

        att_f[...] = att_ref[...].astype(F32)
        ffn_f[...] = ffn_ref[...].astype(F32)
        for d in range(groups):
            base = place_of(me ^ d) * per_pair
            for j in range(per_pair):
                i = order[base + j]
                to = d * 2 * per_pair + j
                sent_f[to : to + 1, :] = att_f[pl.ds(i, 1), :]
                sent_f[to + per_pair : to + per_pair + 1, :] = ffn_f[pl.ds(i, 1), :]
        sent_ref[...] = sent_f[...].astype(BF16)

        row = lax.broadcasted_iota(I32, (requests, 128), 0)
        long_row = lax.broadcasted_iota(I32, (rows, 128), 0)
        lane = lax.broadcasted_iota(I32, (requests, 128), 1)
        long_lane = lax.broadcasted_iota(I32, (rows, 128), 1)
        arr = jnp.zeros((requests, 128), I32)
        inv = jnp.zeros((requests, 128), I32)
        num = jnp.zeros((requests, 128), I32)
        got = jnp.zeros((requests, 128), I32)
        back = jnp.zeros((rows, 128), I32)
        lane_row = lax.broadcasted_iota(I32, (8, 128), 1)
        sub_row = lax.broadcasted_iota(I32, (8, 128), 0)
        lane_counts = jnp.zeros((8, 128), I32)
        half = requests // 2
        partners = positions(groups)
        for q in range(requests):
            at = row == q
            a = arriving[q]
            n = cnt[a]
            arr = jnp.where(at, a, arr)
            num = jnp.where(at, n, num)
            inv = jnp.where(at, inverse[q], inv)
            got = jnp.where(
                at, (me ^ partners[q // per_pair]) * 2 * per_pair + q % per_pair, got
            )
            back = jnp.where(long_row // slots == q, inverse[q], back)
            lane_counts = jnp.where(
                (lane_row % half == q % half) & (sub_row == q // half), n, lane_counts
            )
        lanes_ref[...] = lane_counts
        blocks = []
        for t in range(slots):
            block = jnp.where(lane == SOURCE, arr * slots + t, 0)
            block = jnp.where(lane == LIVE, (num > t).astype(I32), block)
            block = jnp.where(lane == COUNT, num, block)
            block = jnp.where(lane == UNSORT, inv, block)
            block = jnp.where(lane == ATT, got, block)
            block = jnp.where(lane == FFN, got + per_pair, block)
            blocks.append(block)
        table = jnp.concatenate(blocks, axis=0)
        cols[...] = jnp.where(long_lane == BACK, back + (long_row % slots) * requests, table)

    return run(
        body,
        "make_plan",
        (rank, new_owner, counts),
        (att, ffn),
        [
            pltpu.SMEM((requests,), I32),
            pltpu.SMEM((requests,), I32),
            vmem((rows, 128), I32),
            vmem((8, 128), I32),
            vmem((sent_rows, width), BF16),
        ],
        scratch=[
            pltpu.SMEM((groups,), I32),
            pltpu.SMEM((requests,), I32),
            vmem((requests, width), F32),
            vmem((requests, width), F32),
            vmem((sent_rows, width), F32),
        ],
    )


def chooser(cols, lane, rows, columns):
    return (lax.broadcasted_iota(I32, (rows, columns), 1) == cols[0:rows, lane : lane + 1]).astype(
        BF16
    )


def sort_shifts(cols, got):
    sent_rows, width = got.shape
    requests = sent_rows // 2

    def body(cols_ref, got_ref, att, ffn):
        for lane, out in ((ATT, att), (FFN, ffn)):
            out[...] = dot32(chooser(cols_ref, lane, requests, sent_rows), got_ref[...]).astype(BF16)

    return run(body, "sort_shifts", (), (cols, got), [vmem((requests, width), BF16)] * 2)


def pack_states(order, wkv_state, groups):
    requests, heads, cells = wkv_state.shape
    per_pair = requests // groups

    def body(order_ref, src, *refs):
        outs, (stage, sems) = refs[:groups], refs[groups:]
        copies = [
            pltpu.make_async_copy(src.at[order_ref[q]], stage.at[q], sems.at[q])
            for q in range(requests)
        ]
        for c in copies:
            c.start()
        for q in range(requests):
            copies[q].wait()
            outs[q // per_pair][q % per_pair] = stage[q].astype(BF16)

    return run(
        body,
        "pack_states",
        (order,),
        (wkv_state,),
        [vmem((per_pair, heads, cells), BF16) for _ in range(groups)],
        scratch=[vmem(wkv_state.shape, F32), pltpu.SemaphoreType.DMA((requests,))],
        in_hbm=(0,),
    )


def states_to_lanes(payloads, size):
    per_pair, heads, cells = payloads[0].shape
    requests = per_pair * len(payloads)
    lanes = heads * requests
    together = 4

    def body(*refs):
        ins, out_ref, rows = refs[: len(payloads)], refs[len(payloads)], refs[len(payloads) + 1]

        def some(step, _):
            for c in range(together):
                at = pl.ds(pl.multiple_of((step * together + c) * 128, 128), 128)
                for k in range(len(payloads)):
                    for j in range(per_pair):
                        first = (k * per_pair + j) * heads
                        rows[c, first : first + heads, :] = ins[k][j, :, at].astype(F32)
            for c in range(together):
                block = jnp.concatenate(
                    [rows[c, pl.ds(h, requests, stride=heads), :] for h in range(heads)], axis=0
                )
                turned = block.T
                chunk = step * together + c
                for e in range(128 // size):
                    out_ref[chunk * (128 // size) + e] = turned[e * size : (e + 1) * size]
            return 0

        lax.fori_loop(0, cells // (128 * together), some, 0)

    return run(
        body,
        "states_to_lanes",
        (),
        payloads,
        [vmem((cells // size, size, lanes), F32)],
        scratch=[vmem((together, requests * heads, 128), F32)],
    )[0]


def first_norm(place, toks, att, cols, norm, mix, down_d, down_a, down_g):
    rows, width = toks[0].shape
    parts = len(toks)
    total = parts * width
    requests = att.shape[0]
    slots = rows // requests
    small = down_d.shape[0]
    rank_g = down_g.shape[1]
    low_width = rank_g + 2 * small

    def body(place_ref, *refs):
        tok = refs[:parts]
        att_ref, col, nrm, mx, dd, da, dg, normed, low, low_send, shift = refs[parts:]
        pick = chooser(col, SOURCE, rows, rows)
        xs = [dot32(pick, t[...]) for t in tok]
        mean = sum(jnp.sum(x, axis=1, keepdims=True) for x in xs) / total
        cs = [x - mean for x in xs]
        var = sum(jnp.sum(c * c, axis=1, keepdims=True) for c in cs) / total
        scale = lax.rsqrt(var + 1e-05)
        for k in range(parts):
            at = pl.ds(pl.multiple_of((place_ref[0] ^ k) * width, 128), width)
            normed[k] = cs[k] * scale * nrm[0:1, at] + nrm[1:2, at]
        at = pl.ds(pl.multiple_of(place_ref[0] * width, 128), width)
        now = normed[0]
        before = jnp.concatenate([att_ref[...].astype(F32), now[: rows - requests]], axis=0)
        delta = before - now
        mixed = lambda c: (now + delta * mx[c : c + 1, at]).astype(BF16)
        nothing = jnp.zeros((small, width), BF16)
        low[:, 0:rank_g] = dot32(mixed(5), dg[...])
        low[:, rank_g:low_width] = dot32_turned(
            mixed(1), jnp.concatenate([dd[...], nothing], axis=0)
        ) + dot32_turned(mixed(4), jnp.concatenate([nothing, da[...]], axis=0))
        low_send[...] = low[...].astype(BF16)
        chosen = jnp.zeros((requests, width), F32)
        number = col[0:requests, COUNT : COUNT + 1]
        for t in range(slots):
            chosen = jnp.where(number == t + 1, now[t * requests : (t + 1) * requests], chosen)
        unsort = chooser(col, UNSORT, requests, requests)
        shift[...] = dot32(unsort, chosen.astype(BF16)).astype(BF16)

    return run(
        body,
        "first_norm",
        (place,),
        (*toks, att, cols, norm, mix, down_d, down_a, down_g),
        [
            vmem((parts, rows, width), F32),
            vmem((rows, low_width), F32),
            vmem((rows, low_width), BF16),
            vmem((requests, width), BF16),
        ],
    )


def projections(place, normed, atts, mix, weights):
    parts, rows, width = normed.shape
    requests = atts[0].shape[0]
    out_width = weights[0].shape[1]

    def body(place_ref, n_ref, *refs):
        att, mx, w, outs = refs[:parts], refs[parts], refs[parts + 1 : parts + 4], refs[parts + 4 :]
        sums = [None] * 3
        for k in range(parts):
            at = pl.ds(pl.multiple_of((place_ref[0] ^ k) * width, 128), width)
            now = n_ref[k]
            before = jnp.concatenate([att[k][...].astype(F32), now[: rows - requests]], axis=0)
            delta = before - now
            for which, c in enumerate((0, 2, 3)):
                term = dot32((now + delta * mx[c : c + 1, at]).astype(BF16), w[which][at, :])
                sums[which] = term if k == 0 else sums[which] + term
        for out, value in zip(outs, sums):
            out[...] = value

    return run(
        body,
        "projections",
        (place,),
        (normed, *atts, mix, *weights),
        [vmem((rows, out_width), F32) for _ in weights],
    )


def swap_groups(arrays, group):
    arrays = list(arrays)
    lanes = arrays[0].shape[1]
    where = lax.broadcasted_iota(I32, arrays[0].shape, 1) // group
    bit = 1
    while bit < len(arrays):
        low = (where // bit) % 2 == 0
        out = list(arrays)
        for a in range(len(arrays)):
            if a & bit == 0:
                first, second = arrays[a], arrays[a | bit]
                out[a] = jnp.where(low, first, pltpu.roll(second, bit * group, 1))
                out[a | bit] = jnp.where(low, pltpu.roll(first, lanes - bit * group, 1), second)
        arrays = out
        bit *= 2
    return arrays


def fold_eight(items, flags):
    shift = 1
    for flag in flags:
        items = [
            jnp.where(flag, a, b) + pltpu.roll(jnp.where(flag, b, a), shift, 0)
            for a, b in zip(items[0::2], items[1::2])
        ]
        shift *= 2
    return items[0]


def head_vectors(low_own, low_others, recept, key, value, head_params, ups, lane_counts, size):
    rows, width = recept.shape
    lanes = 128
    heads = width // size
    group = lanes // heads
    slots = 4
    halves = rows // slots // group
    n_groups = width // 128
    small = ups[0].shape[0]
    rank_g = ups[2].shape[0]
    n_others = len(low_others)
    pairs = [(t, b) for t in range(slots) for b in range(t + 1)]

    def body(low, *refs):
        others = refs[:n_others]
        (r_ref, k_ref, v_ref, hp, du, au, gu, cnt) = refs[n_others : n_others + 8]
        (w_out, c_out, v_out, kq_out, uq_out, d_out, g_out, b_out, vec) = refs[n_others + 8 :]
        total = low[...]
        for o in others:
            total = total + o[...].astype(F32)
        glow = jax.nn.sigmoid(total[:, 0:rank_g]).astype(BF16)
        pair = total[:, rank_g : rank_g + 2 * small]
        nothing = jnp.zeros((small, width), BF16)
        decay_in = dot32(
            jnp.tanh(pair).astype(BF16), jnp.concatenate([du[...], nothing], axis=0)
        )
        context_in = dot32(pair.astype(BF16), jnp.concatenate([nothing, au[...]], axis=0))
        decay = jnp.exp(-0.606531 * jax.nn.sigmoid(hp[0:1] + decay_in))
        context = jax.nn.sigmoid(hp[1:2] + context_in)
        g_out[...] = dot32(glow, gu[...])
        r = r_ref[...]
        k = k_ref[...]
        v = v_ref[...]
        scaled = k * hp[2:3]
        kmod = k * (1.0 + (context - 1.0) * hp[3:4])
        rk = r * kmod * hp[4:5]
        lane_r = lax.broadcasted_iota(I32, (128, 128), 0)
        lane_c = lax.broadcasted_iota(I32, (128, 128), 1)
        ones = ((lane_r // size) == (lane_c // size)).astype(BF16)
        for g in range(n_groups):
            at = slice(g * 128, (g + 1) * 128)
            high = rk[:, at].astype(BF16)
            rest = (rk[:, at] - high.astype(F32)).astype(BF16)
            b_out[:, at] = (dot32(high, ones) + dot32(rest, ones)) * v[:, at]

        for index, array in enumerate((r, kmod, scaled, decay, context, v)):
            pieces = []
            for g in range(n_groups):
                turned = array[:, g * 128 : (g + 1) * 128].T
                pieces += [turned[e * size : (e + 1) * size] for e in range(128 // size)]
            for at, piece in enumerate(swap_groups(pieces, group)):
                vec[index, at % halves, at // halves] = piece

        ksum = lambda x, y: jnp.sum(x * y, axis=0, keepdims=True)
        for g in range(halves):
            valid = [cnt[g : g + 1, :] > t for t in range(slots)]
            for t in range(slots):
                s = vec[2, g, t]
                unit = s * lax.rsqrt(jnp.sum(s * s, axis=0, keepdims=True) + 1e-06)
                vec[2, g, t] = unit
                vec[4, g, t] = unit * vec[4, g, t]

            def back_through(x, top, base):
                for b in range(top, -1, -1):
                    at = base + pairs.index((top + 1, b))
                    c_out[g, at : at + 1, :] = jnp.where(valid[b], ksum(vec[1, g, b], x), 0.0)
                    moved = vec[3, g, b] * x - vec[2, g, b] * ksum(vec[4, g, b], x)
                    x = jnp.where(valid[b], moved, x)
                return x

            for t in range(slots):
                w_out[g, t] = back_through(vec[2, g, t], t - 1, 0)
                x = vec[0, g, t]
                at = len(pairs) + pairs.index((t, t))
                c_out[g, at : at + 1, :] = ksum(vec[1, g, t], x)
                x = vec[3, g, t] * x - vec[2, g, t] * ksum(vec[4, g, t], x)
                w_out[g, slots + t] = back_through(x, t - 1, len(pairs))
            run_decay = jnp.ones((size, lanes), F32)
            for t in range(slots - 1, -1, -1):
                kq_out[g, t] = jnp.where(valid[t], vec[1, g, t] * run_decay, 0.0)
                uq_out[g, t] = jnp.where(valid[t], -(vec[4, g, t] * run_decay), 0.0)
                run_decay = jnp.where(valid[t], run_decay * vec[3, g, t], run_decay)
                v_out[g, t] = vec[5, g, t]
            d_out[g] = run_decay

    return run(
        body,
        "head_vectors",
        (),
        (low_own, *low_others, recept, key, value, head_params, *ups, lane_counts),
        [
            vmem((halves, 2 * slots, size, lanes), F32),
            vmem((halves, 2 * len(pairs), lanes), F32),
            vmem((halves, slots, size, lanes), F32),
            vmem((halves, slots, size, lanes), F32),
            vmem((halves, slots, size, lanes), F32),
            vmem((halves, size, lanes), F32),
            vmem((rows, width), F32),
            vmem((rows, width), F32),
        ],
        scratch=[vmem((6, halves, slots, size, lanes), F32)],
    )


def head_outputs(place, states, weights, coefs, values, gate, bonus, head_params, out_weight, parts):
    rows, width = gate.shape
    halves = len(states)
    size, lanes = states[0].shape[1:]
    slots = values.shape[1]
    group = rows // slots // halves
    n_groups = width // 128
    pairs = [(t, b) for t in range(slots) for b in range(t + 1)]
    quad = 4

    def body(place_ref, *refs):
        st = refs[:halves]
        w_ref, c_ref, v_ref, gate_ref, bonus_ref, hp, wo = refs[halves : halves + 7]
        outs = refs[halves + 7 : halves + 7 + parts]
        p_out, prod, done = refs[halves + 7 + parts :]
        sub = lax.broadcasted_iota(I32, (8, lanes), 0)
        folds = [(sub // s) % 2 == 0 for s in (1, 2, 4)]
        for g in range(halves):
            for part in range(2 * slots // quad):

                def products(block, _):
                    ws = [w_ref[g, part * quad + w] for w in range(quad)]
                    sums = [[] for _ in range(quad)]
                    for i in range(8):
                        s = st[g][block * 8 + i]
                        for w in range(quad):
                            term = s * ws[w]
                            acc = term[0:8]
                            for jv in range(1, size // 8):
                                acc = acc + term[jv * 8 : (jv + 1) * 8]
                            sums[w].append(acc)
                    at = pl.ds(pl.multiple_of(block * 8, 8), 8)
                    for w in range(quad):
                        prod[g, part * quad + w, at, :] = fold_eight(sums[w], folds)
                    return 0

                lax.fori_loop(0, size // 8, products, 0)

        by_group = [None] * (halves * slots)
        for g in range(halves):
            for t in range(slots):
                removed = prod[g, t]
                y = prod[g, slots + t]
                for b in range(t + 1):
                    at = pairs.index((t, b))
                    if b < t:
                        removed = removed + c_ref[g, at : at + 1, :] * v_ref[g, b]
                    at += len(pairs)
                    y = y + c_ref[g, at : at + 1, :] * v_ref[g, b]
                p_out[g, t] = removed
                center = y - jnp.mean(y, axis=0, keepdims=True)
                spread = jnp.mean(center * center, axis=0, keepdims=True)
                by_group[t * halves + g] = center * lax.rsqrt(spread + 0.00064)
        backs = swap_groups(by_group, group)
        each = 128 // size
        for g in range(n_groups):
            at = slice(g * 128, (g + 1) * 128)
            turned = jnp.concatenate(backs[each * g : each * (g + 1)], axis=0).T
            full = (turned * hp[5:6, at] + hp[6:7, at] + bonus_ref[:, at]) * gate_ref[:, at]
            done[:, at] = full.astype(BF16)
        for q in range(parts):
            at = pl.ds(pl.multiple_of((place_ref[0] ^ q) * width, 128), width)
            outs[q][...] = dot32(done[...], wo[:, at]).astype(outs[q].dtype)

    return run(
        body,
        "head_outputs",
        (place,),
        (*states, weights, coefs, values, gate, bonus, head_params, out_weight),
        [vmem((rows, width), F32)]
        + [vmem((rows, width), BF16) for _ in range(parts - 1)]
        + [vmem(values.shape, F32)],
        scratch=[vmem(weights.shape, F32), vmem((rows, width), BF16)],
    )


def final_states(arriving, states, removed, values, keys, units, decay, heads):
    halves = len(states)
    size, _, lanes = states[0].shape
    slots = removed.shape[1]
    requests = arriving.shape[0]
    half = requests // halves
    step_chunks = 4
    per_chunk = 128 // size
    steps = size // (per_chunk * step_chunks)
    cells = size * size

    def body(arr_ref, *refs):
        st = refs[:halves]
        p_ref, v_ref, kq_ref, uq_ref, d_ref, out_ref, new, rows = refs[halves:]
        step = pl.program_id(0)
        for g in range(halves):

            def update(block, _):
                first = block * 4
                real = step * (per_chunk * step_chunks) + first
                lefts = []
                for i in range(4):
                    row = [v_ref[g, t, pl.ds(real + i, 1), :] for t in range(slots)]
                    row += [p_ref[g, t, pl.ds(real + i, 1), :] for t in range(slots)]
                    lefts.append([jnp.broadcast_to(x, (8, lanes)) for x in row])
                for jv in range(size // 8):
                    at = slice(jv * 8, (jv + 1) * 8)
                    rights = [kq_ref[g, t, at, :] for t in range(slots)]
                    rights += [uq_ref[g, t, at, :] for t in range(slots)]
                    decayed = d_ref[g, at, :]
                    for i in range(4):
                        acc = st[g][real + i, at, :] * decayed
                        for left, right in zip(lefts[i], rights):
                            acc = acc + left * right
                        new[g, first + i, at, :] = acc
                return 0

            lax.fori_loop(0, per_chunk * step_chunks // 4, update, 0)
        for c in range(step_chunks):
            for g in range(halves):
                block = [new[g, per_chunk * c + e] for e in range(per_chunk)]
                turned = jnp.concatenate(block, axis=0).T
                for h in range(heads):
                    rows[c, pl.ds(g * half * heads + h, half, stride=heads), :] = turned[
                        h * half : (h + 1) * half
                    ]
        for c in range(step_chunks):
            for q in range(requests):
                out_ref[arr_ref[q], :, c * 128 : (c + 1) * 128] = rows[
                    c, q * heads : (q + 1) * heads, :
                ]

    args = (*states, removed, values, keys, units, decay)
    return pl.pallas_call(
        body,
        grid_spec=pltpu.PrefetchScalarGridSpec(
            num_scalar_prefetch=1,
            grid=(steps,),
            in_specs=[pl.BlockSpec(memory_space=pltpu.VMEM) for _ in args],
            out_specs=pl.BlockSpec((requests, heads, 128 * step_chunks), lambda s, a: (0, 0, s)),
            scratch_shapes=[
                vmem((halves, per_chunk * step_chunks, size, lanes), F32),
                vmem((step_chunks, requests * heads, 128), F32),
            ],
        ),
        out_shape=jax.ShapeDtypeStruct((requests, heads, cells), F32),
        compiler_params=pltpu.CompilerParams(vmem_limit_bytes=SCRATCH_LIMIT),
        name="final_states",
    )(arriving, *[pltpu.with_memory_space_constraint(a, pltpu.VMEM) for a in args])


def middle(tok, cols, own, others):
    rows, width = tok.shape

    def body(tok_ref, col, own_ref, *refs):
        out = refs[-1]
        total = dot32(chooser(col, SOURCE, rows, rows), tok_ref[...]) + own_ref[...]
        for o in refs[:-1]:
            total = total + o[...].astype(F32)
        out[...] = total.astype(BF16)

    return run(body, "middle", (), (tok, cols, own, *others), [vmem((rows, width), BF16)])[0]


def channel_mix(place, mids, prevs, cols, norm, mix, key_weight, value_weight):
    parts = len(mids)
    rows, width = mids[0].shape
    total = parts * width
    requests = prevs[0].shape[0]
    slots = rows // requests

    def body(place_ref, *refs):
        mid, prev = refs[:parts], refs[parts : 2 * parts]
        col, nrm, mx, kw, vw = refs[2 * parts : 2 * parts + 5]
        outs, shift = refs[2 * parts + 5 : 3 * parts + 5], refs[3 * parts + 5]
        xs = [m[...].astype(F32) for m in mid]
        mean = sum(jnp.sum(x, axis=1, keepdims=True) for x in xs) / total
        cs = [x - mean for x in xs]
        var = sum(jnp.sum(c * c, axis=1, keepdims=True) for c in cs) / total
        scale = lax.rsqrt(var + 1e-05)
        acc = None
        for k in range(parts):
            at = pl.ds(pl.multiple_of((place_ref[0] ^ k) * width, 128), width)
            now = cs[k] * scale * nrm[2:3, at] + nrm[3:4, at]
            before = jnp.concatenate([prev[k][...].astype(F32), now[: rows - requests]], axis=0)
            term = dot32((now + (before - now) * mx[6:7, at]).astype(BF16), kw[at, :])
            acc = term if k == 0 else acc + term
            if k == 0:
                chosen = jnp.zeros((requests, width), F32)
                number = col[0:requests, COUNT : COUNT + 1]
                for t in range(slots):
                    chosen = jnp.where(
                        number == t + 1, now[t * requests : (t + 1) * requests], chosen
                    )
                unsort = chooser(col, UNSORT, requests, requests)
                shift[...] = dot32(unsort, chosen.astype(BF16)).astype(BF16)
        h = jnp.maximum(acc, 0.0)
        hidden = (h * h).astype(BF16)
        for q in range(parts):
            at = pl.ds(pl.multiple_of((place_ref[0] ^ q) * width, 128), width)
            outs[q][...] = dot32(hidden, vw[:, at]).astype(outs[q].dtype)

    return run(
        body,
        "channel_mix",
        (place,),
        (*mids, *prevs, cols, norm, mix, key_weight, value_weight),
        [vmem((rows, width), F32)]
        + [vmem((rows, width), BF16) for _ in range(parts - 1)]
        + [vmem((requests, width), BF16)],
    )


def finish(mid, own, others, cols):
    rows, width = mid.shape

    def body(mid_ref, own_ref, *refs):
        col, out = refs[-2:]
        total = own_ref[...]
        for o in refs[:-2]:
            total = total + o[...].astype(F32)
        live = col[:, LIVE : LIVE + 1] > 0
        total = jnp.where(live, mid_ref[...].astype(F32) + total, 0.0).astype(BF16)
        out[...] = dot32(chooser(col, BACK, rows, rows), total).astype(BF16)

    return run(body, "finish", (), (mid, own, *others, cols), [vmem((rows, width), BF16)])[0]


def per_device(
    groups,
    parts,
    tokens,
    counts,
    new_owner,
    wkv_state,
    att_shift,
    ffn_shift,
    norm_params,
    mix_coeffs,
    head_params,
    recept_weight,
    key_weight,
    value_weight,
    output_weight,
    decay_down,
    decay_up,
    alpha_down,
    alpha_up,
    gate_down,
    gate_up,
    ffn_key_weight,
    ffn_value_weight,
):
    requests, slots, width = tokens.shape
    heads = wkv_state.shape[1]
    size = width // heads
    rows = requests * slots
    rank = lax.axis_index("req").astype(I32).reshape(1)
    place = lax.axis_index("mdl").astype(I32).reshape(1)
    gather = lambda x: [x] + [xor_permute(x, "mdl", parts, k) for k in range(1, parts)]
    scatter = lambda xs: [xor_permute(xs[k], "mdl", parts, k) for k in range(1, parts)]

    toks = gather(tokens.reshape(rows, width))
    order, arriving, cols, lane_counts, sent = make_plan(
        rank, new_owner, counts, att_shift, ffn_shift, groups, slots
    )
    got = lax.all_to_all(
        sent.reshape(groups, -1, width), "req", split_axis=0, concat_axis=0, tiled=True
    )
    att, ffn = sort_shifts(cols, got.reshape(2 * requests, width))
    atts = gather(att)

    first = toks[1]
    order, first = lax.optimization_barrier((order, first))
    toks = [toks[0], first] + toks[2:]
    packed = pack_states(order, wkv_state, groups)
    payloads = [
        packed[at] if k == 0 else xor_permute(packed[at], "req", groups, k)
        for at, k in enumerate(positions(groups))
    ]
    split = groups // 2
    states = [states_to_lanes(payloads[:split], size), states_to_lanes(payloads[split:], size)]

    normed, low, low_send, new_att = first_norm(
        place,
        toks,
        att,
        cols,
        norm_params,
        mix_coeffs,
        decay_down.T,
        alpha_down.T,
        gate_down,
    )
    low_others = gather(low_send)[1:]
    ffns = gather(ffn)
    recept, key, value = projections(
        place, normed, atts, mix_coeffs, (recept_weight, key_weight, value_weight)
    )
    weights, coefs, vals, keys, units, decay, gate, bonus = head_vectors(
        low,
        low_others,
        recept,
        key,
        value,
        head_params,
        (decay_up, alpha_up, gate_up),
        lane_counts,
        size,
    )
    results = head_outputs(
        place, states, weights, coefs, vals, gate, bonus, head_params, output_weight, parts
    )
    outs, removed = results[:parts], results[parts]
    mid = middle(toks[0], cols, outs[0], scatter(outs))
    new_state = final_states(arriving, states, removed, vals, keys, units, decay, heads)
    results = channel_mix(
        place,
        gather(mid),
        ffns,
        cols,
        norm_params,
        mix_coeffs,
        ffn_key_weight,
        ffn_value_weight,
    )
    outs, new_ffn = results[:parts], results[parts]
    block = finish(mid, outs[0], scatter(outs), cols)
    return (block.reshape(requests, slots, width), new_state, new_att, new_ffn)


def solution(mesh):
    return jax.shard_map(
        functools.partial(per_device, mesh.shape["req"], mesh.shape["mdl"]),
        mesh=mesh,
        in_specs=(
            P("req", None, "mdl"),
            P("req"),
            P(),
            P("req", "mdl", None),
            P("req", "mdl"),
            P("req", "mdl"),
            P(),
            P(),
            P(None, "mdl"),
            P(None, "mdl"),
            P(None, "mdl"),
            P(None, "mdl"),
            P("mdl", None),
            P("mdl", None),
            P(None, "mdl"),
            P("mdl", None),
            P(None, "mdl"),
            P("mdl", None),
            P(None, "mdl"),
            P(None, "mdl"),
            P("mdl", None),
        ),
        out_specs=(P("req", None, "mdl"), P("req", "mdl", None), P("req", "mdl"), P("req", "mdl")),
        check_vma=False,
    )
```

```python
import functools

import jax
import jax.numpy as jnp
from jax import lax
from jax.experimental import pallas as pl
from jax.experimental.pallas import tpu as pltpu
from jax.sharding import PartitionSpec as P

F32 = jnp.float32
BF16 = jnp.bfloat16
I32 = jnp.int32
SCRATCH_LIMIT = 16 * 1024 * 1024


def xor_permute(x, axis, size, k):
    return lax.ppermute(x, axis, [(a, a ^ k) for a in range(size)])


def dot32(a, b):
    return jnp.dot(a, b, preferred_element_type=F32)


def dot32_turned(a, b):
    return lax.dot_general(a, b, (((1,), (1,)), ((), ())), preferred_element_type=F32)


def vmem(shape, dtype):
    return pltpu.VMEM(shape, dtype)


def run(body, name, scalars, args, outs, scratch=(), fetch=(), in_hbm=()):
    far = set(fetch) | set(in_hbm)
    anywhere = pl.BlockSpec(memory_space=pltpu.HBM)
    near = pl.BlockSpec(memory_space=pltpu.VMEM)
    n_scalars, n_args, n_outs = len(scalars), len(args), len(outs)

    def whole(*refs):
        refs = list(refs)
        if not fetch:
            return body(*refs)
        sems = refs.pop()
        first = len(refs) - len(fetch)
        buffers = refs[first:]
        refs = refs[:first]
        copies = []
        for at, (i, buffer) in enumerate(zip(fetch, buffers)):
            copies.append(pltpu.make_async_copy(refs[n_scalars + i], buffer, sems.at[at]))
            refs[n_scalars + i] = buffer
        for c in copies:
            c.start()

        def ready(which=None):
            for c in copies if which is None else [copies[which]]:
                c.wait()

        return body(ready, *refs)

    extra = [pltpu.VMEM(args[i].shape, args[i].dtype) for i in fetch]
    if fetch:
        extra.append(pltpu.SemaphoreType.DMA((len(fetch),)))
    return pl.pallas_call(
        whole,
        grid_spec=pltpu.PrefetchScalarGridSpec(
            num_scalar_prefetch=n_scalars,
            grid=(1,),
            in_specs=[anywhere if i in far else near for i in range(n_args)],
            out_specs=[
                pl.BlockSpec(memory_space=pltpu.SMEM) if o.memory_space == pltpu.SMEM else near
                for o in outs
            ],
            scratch_shapes=list(scratch) + extra,
        ),
        out_shape=[
            jax.ShapeDtypeStruct(o.shape, o.dtype) if o.memory_space == pltpu.SMEM else o
            for o in outs
        ],
        compiler_params=pltpu.CompilerParams(vmem_limit_bytes=SCRATCH_LIMIT),
        name=name,
    )(
        *scalars,
        *[
            pltpu.with_memory_space_constraint(a, pltpu.HBM if i in far else pltpu.VMEM)
            for i, a in enumerate(args)
        ],
    )


def positions(groups):
    return list(range(0, groups, 2)) + list(range(1, groups, 2))


def place_of(k, groups):
    return k // 2 + (k % 2) * (groups // 2)


SOURCE, BACK, LIVE, COUNT, UNSORT, ATT, FFN = range(7)


def plan_and_pack(rank, new_owner, counts, wkv_state, groups, slots):
    requests, heads, cells = wkv_state.shape
    per_pair = requests // groups
    rows = requests * slots

    def body(
        rank_ref, owner_far, cnt_far, wkv, arriving, cols, lanes_ref, *rest
    ):
        packed = rest[:groups]
        owner, cnt, turn, order, inverse, stage, sems, small = rest[groups:]
        me = rank_ref[0]
        get_owner = pltpu.make_async_copy(owner_far, owner, small.at[0])
        get_counts = pltpu.make_async_copy(cnt_far, cnt, small.at[1])
        get_owner.start()
        get_counts.start()
        get_owner.wait()
        get_counts.wait()
        for g in range(groups):
            turn[g] = 0

        def own(i, _):
            spot = place_of((owner[me * requests + i] // requests) ^ me, groups)
            order[spot * per_pair + turn[spot]] = i
            turn[spot] = turn[spot] + 1
            return 0

        lax.fori_loop(0, requests, own, 0, unroll=4)
        copies = []
        for q in range(requests):
            copies.append(pltpu.make_async_copy(wkv.at[order[q]], stage.at[q], sems.at[q]))
            copies[q].start()

        def source(s, _):
            base = place_of(s ^ me, groups) * per_pair

            def one(i, found):
                v = owner[s * requests + i]
                mine = v // requests == me
                spot = v % requests
                arriving[jnp.where(mine, base + found, requests)] = spot
                inverse[jnp.where(mine, spot, requests)] = base + found
                return found + mine.astype(I32)

            lax.fori_loop(0, requests, one, jnp.int32(0), unroll=8)
            return 0

        lax.fori_loop(0, groups, source, 0)

        row = lax.broadcasted_iota(I32, (requests, 128), 0)
        long_row = lax.broadcasted_iota(I32, (rows, 128), 0)
        lane = lax.broadcasted_iota(I32, (requests, 128), 1)
        long_lane = lax.broadcasted_iota(I32, (rows, 128), 1)
        arr = jnp.zeros((requests, 128), I32)
        inv = jnp.zeros((requests, 128), I32)
        num = jnp.zeros((requests, 128), I32)
        back = jnp.zeros((rows, 128), I32)
        lane_row = lax.broadcasted_iota(I32, (8, 128), 1)
        sub_row = lax.broadcasted_iota(I32, (8, 128), 0)
        lane_counts = jnp.zeros((8, 128), I32)
        half = requests // 2
        for q in range(requests):
            at = row == q
            a = arriving[q]
            n = cnt[a]
            arr = jnp.where(at, a, arr)
            num = jnp.where(at, n, num)
            inv = jnp.where(at, inverse[q], inv)
            back = jnp.where(long_row // slots == q, inverse[q], back)
            lane_counts = jnp.where(
                (lane_row % half == q % half) & (sub_row == q // half), n, lane_counts
            )
        lanes_ref[...] = lane_counts
        spot = row // per_pair
        partner = (spot % (groups // 2)) * 2 + spot // (groups // 2)
        got = (me ^ partner) * (2 * per_pair) + row % per_pair
        blocks = []
        for t in range(slots):
            block = jnp.where(lane == SOURCE, arr * slots + t, 0)
            block = jnp.where(lane == LIVE, (num > t).astype(I32), block)
            block = jnp.where(lane == COUNT, num, block)
            block = jnp.where(lane == UNSORT, inv, block)
            block = jnp.where(lane == ATT, got, block)
            block = jnp.where(lane == FFN, got + per_pair, block)
            blocks.append(block)
        table = jnp.concatenate(blocks, axis=0)
        cols[...] = jnp.where(long_lane == BACK, back + (long_row % slots) * requests, table)
        for q in range(requests):
            copies[q].wait()
            packed[q // per_pair][q % per_pair] = stage[q].astype(BF16)

    return run(
        body,
        "plan_and_pack",
        (rank,),
        (new_owner, counts, wkv_state),
        [
            pltpu.SMEM((requests + 1,), I32),
            vmem((rows, 128), I32),
            vmem((8, 128), I32),
        ]
        + [vmem((per_pair, heads, cells), BF16) for _ in range(groups)],
        scratch=[
            pltpu.SMEM(new_owner.shape, I32),
            pltpu.SMEM(counts.shape, I32),
            pltpu.SMEM((groups,), I32),
            pltpu.SMEM((requests,), I32),
            pltpu.SMEM((requests + 1,), I32),
            vmem(wkv_state.shape, F32),
            pltpu.SemaphoreType.DMA((requests,)),
            pltpu.SemaphoreType.DMA((2,)),
        ],
        in_hbm=(0, 1, 2),
    )


def pack_shifts(rank, new_owner, att, ffn, groups, parts):
    requests, width = att.shape
    per_pair = requests // groups

    def body(rank_ref, owner_far, att_far, ffn_far, sent_ref, owner, turn, order, att_ref, ffn_ref, wide, sent_f, sems):
        me = rank_ref[0]
        copies = [
            pltpu.make_async_copy(
                owner_far, owner, sems.at[0]
            ),
            pltpu.make_async_copy(att_far, att_ref, sems.at[1]),
            pltpu.make_async_copy(ffn_far, ffn_ref, sems.at[2]),
        ]
        for c in copies:
            c.start()
        for g in range(groups):
            turn[g] = 0
        copies[0].wait()

        def own(i, _):
            target = owner[me * requests + i] // requests
            order[target * per_pair + turn[target]] = i
            turn[target] = turn[target] + 1
            return 0

        lax.fori_loop(0, requests, own, 0, unroll=4)
        copies[1].wait()
        copies[2].wait()
        wide[0] = att_ref[...].astype(F32)
        wide[1] = ffn_ref[...].astype(F32)
        for d in range(groups):
            for j in range(per_pair):
                at = pl.ds(order[d * per_pair + j], 1)
                to = d * 2 * per_pair + j
                sent_f[to : to + 1, :] = wide[0, at, :]
                sent_f[to + per_pair : to + per_pair + 1, :] = wide[1, at, :]
        for d in range(groups):
            piece = sent_f[d * 2 * per_pair : (d + 1) * 2 * per_pair, :].astype(BF16)
            for m in range(parts):
                sent_ref[d, m] = piece

    return run(
        body,
        "pack_shifts",
        (rank,),
        (new_owner, att, ffn),
        [vmem((groups, parts, 2 * per_pair, width), BF16)],
        scratch=[
            pltpu.SMEM(new_owner.shape, I32),
            pltpu.SMEM((groups,), I32),
            pltpu.SMEM((requests,), I32),
            vmem(att.shape, BF16),
            vmem(ffn.shape, BF16),
            vmem((2, requests, width), F32),
            vmem((2 * requests, width), F32),
            pltpu.SemaphoreType.DMA((3,)),
        ],
        in_hbm=(0, 1, 2),
    )[0]


def chooser(cols, lane, rows, columns):
    return (lax.broadcasted_iota(I32, (rows, columns), 1) == cols[0:rows, lane : lane + 1]).astype(
        BF16
    )


def sort_shifts(cols, got):
    groups, parts, twice, width = got.shape
    requests = groups * twice // 2

    def body(cols_ref, got_ref, att, ffn):
        picks = [chooser(cols_ref, lane, requests, 2 * requests) for lane in (ATT, FFN)]
        for m in range(parts):
            rows = got_ref[:, m].astype(F32).reshape(2 * requests, width).astype(BF16)
            for pick, out in zip(picks, (att, ffn)):
                out[m] = dot32(pick, rows).astype(BF16)

    return run(
        body, "sort_shifts", (), (cols, got), [vmem((parts, requests, width), BF16)] * 2
    )


def states_to_lanes(payloads, size):
    per_pair, heads, cells = payloads[0].shape
    requests = per_pair * len(payloads)
    lanes = heads * requests
    together = 4

    def body(*refs):
        ins, out_ref, rows = refs[: len(payloads)], refs[len(payloads)], refs[len(payloads) + 1]

        def some(step, _):
            for c in range(together):
                at = pl.ds(pl.multiple_of((step * together + c) * 128, 128), 128)
                for k in range(len(payloads)):
                    for j in range(per_pair):
                        first = (k * per_pair + j) * heads
                        rows[c, first : first + heads, :] = ins[k][j, :, at].astype(F32)
            for c in range(together):
                block = jnp.concatenate(
                    [rows[c, pl.ds(h, requests, stride=heads), :] for h in range(heads)], axis=0
                )
                turned = block.T
                chunk = step * together + c
                for e in range(128 // size):
                    out_ref[chunk * (128 // size) + e] = turned[e * size : (e + 1) * size]
            return 0

        lax.fori_loop(0, cells // (128 * together), some, 0)

    return run(
        body,
        "states_to_lanes",
        (),
        payloads,
        [vmem((cells // size, size, lanes), F32)],
        scratch=[vmem((together, requests * heads, 128), F32)],
    )[0]


def first_norm(place, toks, att, cols, norm, mix, down_d, down_a, down_g):
    rows, width = toks[0].shape
    parts = len(toks)
    total = parts * width
    requests = att.shape[1]
    slots = rows // requests
    small = down_d.shape[0]
    rank_g = down_g.shape[1]
    low_width = rank_g + 2 * small

    def body(ready, place_ref, *refs):
        tok = refs[:parts]
        att_ref, col, nrm, mx, dd, da, dg, normed, low, low_send, shift = refs[parts:]
        pick = chooser(col, SOURCE, rows, rows)
        ready()
        xs = [dot32(pick, t[...]) for t in tok]
        mean = sum(jnp.sum(x, axis=1, keepdims=True) for x in xs) / total
        cs = [x - mean for x in xs]
        var = sum(jnp.sum(c * c, axis=1, keepdims=True) for c in cs) / total
        scale = lax.rsqrt(var + 1e-05)
        for k in range(parts):
            at = pl.ds(pl.multiple_of((place_ref[0] ^ k) * width, 128), width)
            normed[k] = cs[k] * scale * nrm[0:1, at] + nrm[1:2, at]
        at = pl.ds(pl.multiple_of(place_ref[0] * width, 128), width)
        now = normed[0]
        before = jnp.concatenate([att_ref[place_ref[0]].astype(F32), now[: rows - requests]], axis=0)
        delta = before - now
        mixed = lambda c: (now + delta * mx[c : c + 1, at]).astype(BF16)
        nothing = jnp.zeros((small, width), BF16)
        low[:, 0:rank_g] = dot32(mixed(5), dg[...])
        low[:, rank_g:low_width] = dot32_turned(
            mixed(1), jnp.concatenate([dd[...], nothing], axis=0)
        ) + dot32_turned(mixed(4), jnp.concatenate([nothing, da[...]], axis=0))
        low_send[...] = low[...].astype(BF16)
        chosen = jnp.zeros((requests, width), F32)
        number = col[0:requests, COUNT : COUNT + 1]
        for t in range(slots):
            chosen = jnp.where(number == t + 1, now[t * requests : (t + 1) * requests], chosen)
        unsort = chooser(col, UNSORT, requests, requests)
        shift[...] = dot32(unsort, chosen.astype(BF16)).astype(BF16)

    return run(
        body,
        "first_norm",
        (place,),
        (*toks, att, cols, norm, mix, down_d, down_a, down_g),
        [
            vmem((parts, rows, width), F32),
            vmem((rows, low_width), F32),
            vmem((rows, low_width), BF16),
            vmem((requests, width), BF16),
        ],
        fetch=(*range(1, parts), *range(parts + 2, parts + 7)),
    )


def projections(place, normed, att, mix, weights):
    parts, rows, width = normed.shape
    requests = att.shape[1]
    out_width = weights[0].shape[1]

    def body(ready, place_ref, n_ref, *refs):
        att_ref, mx, w, outs = refs[0], refs[1], refs[2:5], refs[5:]
        ready(0)
        for which, c in enumerate((0, 2, 3)):
            ready(1 + which)
            for k in range(parts):
                at = pl.ds(pl.multiple_of((place_ref[0] ^ k) * width, 128), width)
                now = n_ref[k]
                before = jnp.concatenate(
                    [att_ref[place_ref[0] ^ k].astype(F32), now[: rows - requests]], axis=0
                )
                mixed = (now + (before - now) * mx[c : c + 1, at]).astype(BF16)
                term = dot32(mixed, w[which][at, :])
                total = term if k == 0 else total + term
            outs[which][...] = total

    return run(
        body,
        "projections",
        (place,),
        (normed, att, mix, *weights),
        [vmem((rows, out_width), F32) for _ in weights],
        fetch=(2, 3, 4, 5),
    )


def swap_groups(arrays, group):
    arrays = list(arrays)
    lanes = arrays[0].shape[1]
    where = lax.broadcasted_iota(I32, arrays[0].shape, 1) // group
    bit = 1
    while bit < len(arrays):
        low = (where // bit) % 2 == 0
        out = list(arrays)
        for a in range(len(arrays)):
            if a & bit == 0:
                first, second = arrays[a], arrays[a | bit]
                out[a] = jnp.where(low, first, pltpu.roll(second, bit * group, 1))
                out[a | bit] = jnp.where(low, pltpu.roll(first, lanes - bit * group, 1), second)
        arrays = out
        bit *= 2
    return arrays


def fold_eight(items, flags):
    shift = 1
    for flag in flags:
        items = [
            jnp.where(flag, a, b) + pltpu.roll(jnp.where(flag, b, a), shift, 0)
            for a, b in zip(items[0::2], items[1::2])
        ]
        shift *= 2
    return items[0]


def head_vectors(low_own, low_others, recept, key, value, head_params, ups, lane_counts, size):
    rows, width = recept.shape
    lanes = 128
    heads = width // size
    group = lanes // heads
    slots = 4
    halves = rows // slots // group
    n_groups = width // 128
    small = ups[0].shape[0]
    rank_g = ups[2].shape[0]
    n_others = len(low_others)
    pairs = [(t, b) for t in range(slots) for b in range(t + 1)]

    def body(ready, low, *refs):
        others = refs[:n_others]
        (r_ref, k_ref, v_ref, hp, du, au, gu, cnt) = refs[n_others : n_others + 8]
        (w_out, c_out, v_out, kq_out, uq_out, d_out, g_out, b_out, vec) = refs[n_others + 8 :]
        total = low[...]
        for o in others:
            total = total + o[...].astype(F32)
        glow = jax.nn.sigmoid(total[:, 0:rank_g]).astype(BF16)
        pair = total[:, rank_g : rank_g + 2 * small]
        nothing = jnp.zeros((small, width), BF16)
        ready()
        decay_in = dot32(
            jnp.tanh(pair).astype(BF16), jnp.concatenate([du[...], nothing], axis=0)
        )
        context_in = dot32(pair.astype(BF16), jnp.concatenate([nothing, au[...]], axis=0))
        decay = jnp.exp(-0.606531 * jax.nn.sigmoid(hp[0:1] + decay_in))
        context = jax.nn.sigmoid(hp[1:2] + context_in)
        g_out[...] = dot32(glow, gu[...])
        r = r_ref[...]
        k = k_ref[...]
        v = v_ref[...]
        scaled = k * hp[2:3]
        kmod = k * (1.0 + (context - 1.0) * hp[3:4])
        rk = r * kmod * hp[4:5]
        lane_r = lax.broadcasted_iota(I32, (128, 128), 0)
        lane_c = lax.broadcasted_iota(I32, (128, 128), 1)
        ones = ((lane_r // size) == (lane_c // size)).astype(BF16)
        for g in range(n_groups):
            at = slice(g * 128, (g + 1) * 128)
            high = rk[:, at].astype(BF16)
            rest = (rk[:, at] - high.astype(F32)).astype(BF16)
            b_out[:, at] = (dot32(high, ones) + dot32(rest, ones)) * v[:, at]

        for index, array in enumerate((r, kmod, scaled, decay, context, v)):
            pieces = []
            for g in range(n_groups):
                turned = array[:, g * 128 : (g + 1) * 128].T
                pieces += [turned[e * size : (e + 1) * size] for e in range(128 // size)]
            for at, piece in enumerate(swap_groups(pieces, group)):
                vec[index, at % halves, at // halves] = piece

        ksum = lambda x, y: jnp.sum(x * y, axis=0, keepdims=True)
        for g in range(halves):
            valid = [cnt[g : g + 1, :] > t for t in range(slots)]
            for t in range(slots):
                s = vec[2, g, t]
                unit = s * lax.rsqrt(jnp.sum(s * s, axis=0, keepdims=True) + 1e-06)
                vec[2, g, t] = unit
                vec[4, g, t] = unit * vec[4, g, t]

            def back_through(x, top, base):
                for b in range(top, -1, -1):
                    at = base + pairs.index((top + 1, b))
                    c_out[g, at : at + 1, :] = jnp.where(valid[b], ksum(vec[1, g, b], x), 0.0)
                    moved = vec[3, g, b] * x - vec[2, g, b] * ksum(vec[4, g, b], x)
                    x = jnp.where(valid[b], moved, x)
                return x

            for t in range(slots):
                w_out[g, t] = back_through(vec[2, g, t], t - 1, 0)
                x = vec[0, g, t]
                at = len(pairs) + pairs.index((t, t))
                c_out[g, at : at + 1, :] = ksum(vec[1, g, t], x)
                x = vec[3, g, t] * x - vec[2, g, t] * ksum(vec[4, g, t], x)
                w_out[g, slots + t] = back_through(x, t - 1, len(pairs))
            run_decay = jnp.ones((size, lanes), F32)
            for t in range(slots - 1, -1, -1):
                kq_out[g, t] = jnp.where(valid[t], vec[1, g, t] * run_decay, 0.0)
                uq_out[g, t] = jnp.where(valid[t], -(vec[4, g, t] * run_decay), 0.0)
                run_decay = jnp.where(valid[t], run_decay * vec[3, g, t], run_decay)
                v_out[g, t] = vec[5, g, t]
            d_out[g] = run_decay

    return run(
        body,
        "head_vectors",
        (),
        (low_own, *low_others, recept, key, value, head_params, *ups, lane_counts),
        [
            vmem((halves, 2 * slots, size, lanes), F32),
            vmem((halves, 2 * len(pairs), lanes), F32),
            vmem((halves, slots, size, lanes), F32),
            vmem((halves, slots, size, lanes), F32),
            vmem((halves, slots, size, lanes), F32),
            vmem((halves, size, lanes), F32),
            vmem((rows, width), F32),
            vmem((rows, width), F32),
        ],
        scratch=[vmem((6, halves, slots, size, lanes), F32)],
        fetch=tuple(range(n_others + 4, n_others + 8)),
    )


def head_outputs(place, states, weights, coefs, values, gate, bonus, head_params, out_weight, parts):
    rows, width = gate.shape
    halves = len(states)
    size, lanes = states[0].shape[1:]
    slots = values.shape[1]
    group = rows // slots // halves
    n_groups = width // 128
    pairs = [(t, b) for t in range(slots) for b in range(t + 1)]
    quad = 4

    def body(ready, place_ref, *refs):
        st = refs[:halves]
        w_ref, c_ref, v_ref, gate_ref, bonus_ref, hp, wo = refs[halves : halves + 7]
        outs = refs[halves + 7 : halves + 7 + parts]
        p_out, prod, done = refs[halves + 7 + parts :]
        sub = lax.broadcasted_iota(I32, (8, lanes), 0)
        folds = [(sub // s) % 2 == 0 for s in (1, 2, 4)]
        for g in range(halves):
            for part in range(2 * slots // quad):

                def products(block, _):
                    ws = [w_ref[g, part * quad + w] for w in range(quad)]
                    sums = [[] for _ in range(quad)]
                    for i in range(8):
                        s = st[g][block * 8 + i]
                        for w in range(quad):
                            term = s * ws[w]
                            acc = term[0:8]
                            for jv in range(1, size // 8):
                                acc = acc + term[jv * 8 : (jv + 1) * 8]
                            sums[w].append(acc)
                    at = pl.ds(pl.multiple_of(block * 8, 8), 8)
                    for w in range(quad):
                        prod[g, part * quad + w, at, :] = fold_eight(sums[w], folds)
                    return 0

                lax.fori_loop(0, size // 8, products, 0)

        by_group = [None] * (halves * slots)
        for g in range(halves):
            for t in range(slots):
                removed = prod[g, t]
                y = prod[g, slots + t]
                for b in range(t + 1):
                    at = pairs.index((t, b))
                    if b < t:
                        removed = removed + c_ref[g, at : at + 1, :] * v_ref[g, b]
                    at += len(pairs)
                    y = y + c_ref[g, at : at + 1, :] * v_ref[g, b]
                p_out[g, t] = removed
                center = y - jnp.mean(y, axis=0, keepdims=True)
                spread = jnp.mean(center * center, axis=0, keepdims=True)
                by_group[t * halves + g] = center * lax.rsqrt(spread + 0.00064)
        backs = swap_groups(by_group, group)
        ready()
        each = 128 // size
        for g in range(n_groups):
            at = slice(g * 128, (g + 1) * 128)
            turned = jnp.concatenate(backs[each * g : each * (g + 1)], axis=0).T
            full = (turned * hp[5:6, at] + hp[6:7, at] + bonus_ref[:, at]) * gate_ref[:, at]
            done[:, at] = full.astype(BF16)
        for q in range(parts):
            at = pl.ds(pl.multiple_of((place_ref[0] ^ q) * width, 128), width)
            outs[q][...] = dot32(done[...], wo[:, at]).astype(outs[q].dtype)

    return run(
        body,
        "head_outputs",
        (place,),
        (*states, weights, coefs, values, gate, bonus, head_params, out_weight),
        [vmem((rows, width), F32)]
        + [vmem((rows, width), BF16) for _ in range(parts - 1)]
        + [vmem(values.shape, F32)],
        scratch=[vmem(weights.shape, F32), vmem((rows, width), BF16)],
        fetch=(halves + 5, halves + 6),
    )


def final_states(arriving, states, removed, values, keys, units, decay, heads):
    halves = len(states)
    size, _, lanes = states[0].shape
    slots = removed.shape[1]
    half = lanes // heads
    requests = half * halves
    step_chunks = 4
    per_chunk = 128 // size
    steps = size // (per_chunk * step_chunks)
    cells = size * size

    def body(arr_ref, *refs):
        st = refs[:halves]
        p_ref, v_ref, kq_ref, uq_ref, d_ref, out_ref, new, rows = refs[halves:]
        step = pl.program_id(0)
        for g in range(halves):

            def update(block, _):
                first = block * 4
                real = step * (per_chunk * step_chunks) + first
                lefts = []
                for i in range(4):
                    row = [v_ref[g, t, pl.ds(real + i, 1), :] for t in range(slots)]
                    row += [p_ref[g, t, pl.ds(real + i, 1), :] for t in range(slots)]
                    lefts.append([jnp.broadcast_to(x, (8, lanes)) for x in row])
                for jv in range(size // 8):
                    at = slice(jv * 8, (jv + 1) * 8)
                    rights = [kq_ref[g, t, at, :] for t in range(slots)]
                    rights += [uq_ref[g, t, at, :] for t in range(slots)]
                    decayed = d_ref[g, at, :]
                    for i in range(4):
                        acc = st[g][real + i, at, :] * decayed
                        for left, right in zip(lefts[i], rights):
                            acc = acc + left * right
                        new[g, first + i, at, :] = acc
                return 0

            lax.fori_loop(0, per_chunk * step_chunks // 4, update, 0)
        for c in range(step_chunks):
            for g in range(halves):
                block = [new[g, per_chunk * c + e] for e in range(per_chunk)]
                turned = jnp.concatenate(block, axis=0).T
                for h in range(heads):
                    rows[c, pl.ds(g * half * heads + h, half, stride=heads), :] = turned[
                        h * half : (h + 1) * half
                    ]
        for c in range(step_chunks):
            for q in range(requests):
                out_ref[arr_ref[q], :, c * 128 : (c + 1) * 128] = rows[
                    c, q * heads : (q + 1) * heads, :
                ]

    args = (*states, removed, values, keys, units, decay)
    return pl.pallas_call(
        body,
        grid_spec=pltpu.PrefetchScalarGridSpec(
            num_scalar_prefetch=1,
            grid=(steps,),
            in_specs=[pl.BlockSpec(memory_space=pltpu.VMEM) for _ in args],
            out_specs=pl.BlockSpec((requests, heads, 128 * step_chunks), lambda s, a: (0, 0, s)),
            scratch_shapes=[
                vmem((halves, per_chunk * step_chunks, size, lanes), F32),
                vmem((step_chunks, requests * heads, 128), F32),
            ],
        ),
        out_shape=jax.ShapeDtypeStruct((requests, heads, cells), F32),
        compiler_params=pltpu.CompilerParams(vmem_limit_bytes=SCRATCH_LIMIT),
        name="final_states",
    )(arriving, *[pltpu.with_memory_space_constraint(a, pltpu.VMEM) for a in args])


def middle(tok, cols, own, others):
    rows, width = tok.shape

    def body(tok_ref, col, own_ref, *refs):
        out = refs[-1]
        total = dot32(chooser(col, SOURCE, rows, rows), tok_ref[...]) + own_ref[...]
        for o in refs[:-1]:
            total = total + o[...].astype(F32)
        out[...] = total.astype(BF16)

    return run(body, "middle", (), (tok, cols, own, *others), [vmem((rows, width), BF16)])[0]


def channel_mix(place, mids, prev, cols, norm, mix, key_weight, value_weight):
    parts = len(mids)
    rows, width = mids[0].shape
    total = parts * width
    requests = prev.shape[1]
    slots = rows // requests

    def body(ready, place_ref, *refs):
        mid = refs[:parts]
        prev_ref, col, nrm, mx, kw, vw = refs[parts : parts + 6]
        outs, shift = refs[parts + 6 : 2 * parts + 6], refs[2 * parts + 6]
        xs = [m[...].astype(F32) for m in mid]
        mean = sum(jnp.sum(x, axis=1, keepdims=True) for x in xs) / total
        cs = [x - mean for x in xs]
        var = sum(jnp.sum(c * c, axis=1, keepdims=True) for c in cs) / total
        scale = lax.rsqrt(var + 1e-05)
        ready()
        acc = None
        for k in range(parts):
            at = pl.ds(pl.multiple_of((place_ref[0] ^ k) * width, 128), width)
            now = cs[k] * scale * nrm[2:3, at] + nrm[3:4, at]
            before = jnp.concatenate([prev_ref[place_ref[0] ^ k].astype(F32), now[: rows - requests]], axis=0)
            term = dot32((now + (before - now) * mx[6:7, at]).astype(BF16), kw[at, :])
            acc = term if k == 0 else acc + term
            if k == 0:
                chosen = jnp.zeros((requests, width), F32)
                number = col[0:requests, COUNT : COUNT + 1]
                for t in range(slots):
                    chosen = jnp.where(
                        number == t + 1, now[t * requests : (t + 1) * requests], chosen
                    )
                unsort = chooser(col, UNSORT, requests, requests)
                shift[...] = dot32(unsort, chosen.astype(BF16)).astype(BF16)
        h = jnp.maximum(acc, 0.0)
        hidden = (h * h).astype(BF16)
        for q in range(parts):
            at = pl.ds(pl.multiple_of((place_ref[0] ^ q) * width, 128), width)
            outs[q][...] = dot32(hidden, vw[:, at]).astype(outs[q].dtype)

    return run(
        body,
        "channel_mix",
        (place,),
        (*mids, prev, cols, norm, mix, key_weight, value_weight),
        [vmem((rows, width), F32)]
        + [vmem((rows, width), BF16) for _ in range(parts - 1)]
        + [vmem((requests, width), BF16)],
        fetch=(parts + 2, parts + 3),
    )


def finish(mid, own, others, cols):
    rows, width = mid.shape

    def body(mid_ref, own_ref, *refs):
        col, out = refs[-2:]
        total = own_ref[...]
        for o in refs[:-2]:
            total = total + o[...].astype(F32)
        live = col[:, LIVE : LIVE + 1] > 0
        total = jnp.where(live, mid_ref[...].astype(F32) + total, 0.0).astype(BF16)
        out[...] = dot32(chooser(col, BACK, rows, rows), total).astype(BF16)

    return run(body, "finish", (), (mid, own, *others, cols), [vmem((rows, width), BF16)])[0]


def per_device(
    groups,
    parts,
    tokens,
    counts,
    new_owner,
    wkv_state,
    att_shift,
    ffn_shift,
    norm_params,
    mix_coeffs,
    head_params,
    recept_weight,
    key_weight,
    value_weight,
    output_weight,
    decay_down,
    decay_up,
    alpha_down,
    alpha_up,
    gate_down,
    gate_up,
    ffn_key_weight,
    ffn_value_weight,
):
    requests, slots, width = tokens.shape
    heads = wkv_state.shape[1]
    size = width // heads
    rows = requests * slots
    rank = lax.axis_index("req").astype(I32).reshape(1)
    place = lax.axis_index("mdl").astype(I32).reshape(1)
    gather = lambda x: [x] + [xor_permute(x, "mdl", parts, k) for k in range(1, parts)]
    scatter = lambda xs: [xor_permute(xs[k], "mdl", parts, k) for k in range(1, parts)]

    toks = gather(tokens.reshape(rows, width))
    sent = pack_shifts(rank, new_owner, att_shift, ffn_shift, groups, parts)
    later, *toks = lax.optimization_barrier((rank, *toks))
    arriving, cols, lane_counts, *packed = plan_and_pack(
        later, new_owner, counts, wkv_state, groups, slots
    )
    payloads = [
        packed[at] if k == 0 else xor_permute(packed[at], "req", groups, k)
        for at, k in enumerate(positions(groups))
    ]
    split = groups // 2
    states = [states_to_lanes(payloads[:split], size), states_to_lanes(payloads[split:], size)]
    got = lax.all_to_all(
        sent.reshape(groups * parts, -1, width),
        ("req", "mdl"),
        split_axis=0,
        concat_axis=0,
        tiled=True,
    )
    att, ffn = sort_shifts(cols, got.reshape(groups, parts, -1, width))

    normed, low, low_send, new_att = first_norm(
        place,
        toks,
        att,
        cols,
        norm_params,
        mix_coeffs,
        decay_down.T,
        alpha_down.T,
        gate_down,
    )
    low_others = gather(low_send)[1:]
    recept, key, value = projections(
        place, normed, att, mix_coeffs, (recept_weight, key_weight, value_weight)
    )
    weights, coefs, vals, keys, units, decay, gate, bonus = head_vectors(
        low,
        low_others,
        recept,
        key,
        value,
        head_params,
        (decay_up, alpha_up, gate_up),
        lane_counts,
        size,
    )
    results = head_outputs(
        place, states, weights, coefs, vals, gate, bonus, head_params, output_weight, parts
    )
    outs, removed = results[:parts], results[parts]
    mid = middle(toks[0], cols, outs[0], scatter(outs))
    new_state = final_states(arriving, states, removed, vals, keys, units, decay, heads)
    results = channel_mix(
        place,
        gather(mid),
        ffn,
        cols,
        norm_params,
        mix_coeffs,
        ffn_key_weight,
        ffn_value_weight,
    )
    outs, new_ffn = results[:parts], results[parts]
    block = finish(mid, outs[0], scatter(outs), cols)
    return (block.reshape(requests, slots, width), new_state, new_att, new_ffn)


def solution(mesh):
    return jax.shard_map(
        functools.partial(per_device, mesh.shape["req"], mesh.shape["mdl"]),
        mesh=mesh,
        in_specs=(
            P("req", None, "mdl"),
            P("req"),
            P(),
            P("req", "mdl", None),
            P("req", "mdl"),
            P("req", "mdl"),
            P(),
            P(),
            P(None, "mdl"),
            P(None, "mdl"),
            P(None, "mdl"),
            P(None, "mdl"),
            P("mdl", None),
            P("mdl", None),
            P(None, "mdl"),
            P("mdl", None),
            P(None, "mdl"),
            P("mdl", None),
            P(None, "mdl"),
            P(None, "mdl"),
            P("mdl", None),
        ),
        out_specs=(P("req", None, "mdl"), P("req", "mdl", None), P("req", "mdl"), P("req", "mdl")),
        check_vma=False,
    )
```

```python
import functools

import jax
import jax.numpy as jnp
from jax import lax
from jax.experimental import pallas as pl
from jax.experimental.pallas import tpu as pltpu
from jax.sharding import PartitionSpec as P

F32 = jnp.float32
BF16 = jnp.bfloat16
I32 = jnp.int32
SCRATCH_LIMIT = 16 * 1024 * 1024


def xor_permute(x, axis, size, k):
    return lax.ppermute(x, axis, [(a, a ^ k) for a in range(size)])


def dot32(a, b):
    return jnp.dot(a, b, preferred_element_type=F32)


def dot32_turned(a, b):
    return lax.dot_general(a, b, (((1,), (1,)), ((), ())), preferred_element_type=F32)


def vmem(shape, dtype):
    return pltpu.VMEM(shape, dtype)


def run(body, name, scalars, args, outs, scratch=(), fetch=(), in_hbm=(), bring=()):
    n_own, n_made = len(args), len(outs)
    args = (*args, *bring)
    outs = [*outs, *[vmem(b.shape, b.dtype) for b in bring]]
    far = set(fetch) | set(in_hbm) | set(range(n_own, len(args)))
    anywhere = pl.BlockSpec(memory_space=pltpu.HBM)
    near = pl.BlockSpec(memory_space=pltpu.VMEM)
    n_scalars, n_args, n_outs = len(scalars), len(args), len(outs)

    def whole(*refs):
        if not bring:
            return inner(*refs)
        refs = list(refs)
        sems = refs.pop()
        first = n_scalars + n_own
        sources = refs[first : first + len(bring)]
        del refs[first : first + len(bring)]
        first += n_made
        targets = refs[first : first + len(bring)]
        del refs[first : first + len(bring)]
        copies = [
            pltpu.make_async_copy(a, b, sems.at[i])
            for i, (a, b) in enumerate(zip(sources, targets))
        ]
        for c in copies:
            c.start()
        inner(*refs)
        for c in copies:
            c.wait()

    def inner(*refs):
        refs = list(refs)
        if not fetch:
            return body(*refs)
        sems = refs.pop()
        first = len(refs) - len(fetch)
        buffers = refs[first:]
        refs = refs[:first]
        copies = []
        for at, (i, buffer) in enumerate(zip(fetch, buffers)):
            copies.append(pltpu.make_async_copy(refs[n_scalars + i], buffer, sems.at[at]))
            refs[n_scalars + i] = buffer
        for c in copies:
            c.start()

        def ready(which=None):
            for c in copies if which is None else [copies[which]]:
                c.wait()

        return body(ready, *refs)

    extra = [pltpu.VMEM(args[i].shape, args[i].dtype) for i in fetch]
    if fetch:
        extra.append(pltpu.SemaphoreType.DMA((len(fetch),)))
    if bring:
        extra.append(pltpu.SemaphoreType.DMA((len(bring),)))
    return pl.pallas_call(
        whole,
        grid_spec=pltpu.PrefetchScalarGridSpec(
            num_scalar_prefetch=n_scalars,
            grid=(1,),
            in_specs=[anywhere if i in far else near for i in range(n_args)],
            out_specs=[
                pl.BlockSpec(memory_space=pltpu.SMEM) if o.memory_space == pltpu.SMEM else near
                for o in outs
            ],
            scratch_shapes=list(scratch) + extra,
        ),
        out_shape=[
            jax.ShapeDtypeStruct(o.shape, o.dtype) if o.memory_space == pltpu.SMEM else o
            for o in outs
        ],
        compiler_params=pltpu.CompilerParams(vmem_limit_bytes=SCRATCH_LIMIT),
        name=name,
    )(
        *scalars,
        *[
            pltpu.with_memory_space_constraint(a, pltpu.HBM if i in far else pltpu.VMEM)
            for i, a in enumerate(args)
        ],
    )


def positions(groups):
    return list(range(0, groups, 2)) + list(range(1, groups, 2))


def place_of(k, groups):
    return k // 2 + (k % 2) * (groups // 2)


SOURCE, BACK, LIVE, COUNT, UNSORT, ATT, FFN = range(7)


def make_plan(rank, new_owner, counts, att, ffn, groups, parts, slots):
    requests, width = att.shape
    per_pair = requests // groups
    rows = requests * slots

    def body(
        rank_ref, owner_far, cnt_far, att_far, ffn_far,
        order, arriving, cols, lanes_ref, sent_ref,
        owner, cnt, turn, inverse, att_ref, ffn_ref, wide, sent_f, sems,
    ):
        me = rank_ref[0]
        copies = [
            pltpu.make_async_copy(owner_far, owner, sems.at[0]),
            pltpu.make_async_copy(cnt_far, cnt, sems.at[1]),
            pltpu.make_async_copy(att_far, att_ref, sems.at[2]),
            pltpu.make_async_copy(ffn_far, ffn_ref, sems.at[3]),
        ]
        for c in copies:
            c.start()
        for g in range(groups):
            turn[g] = 0
        copies[0].wait()

        def own(i, _):
            spot = place_of((owner[me * requests + i] // requests) ^ me, groups)
            order[spot * per_pair + turn[spot]] = i
            turn[spot] = turn[spot] + 1
            return 0

        lax.fori_loop(0, requests, own, 0, unroll=4)
        for c in copies[1:]:
            c.wait()
        wide[0] = att_ref[...].astype(F32)
        wide[1] = ffn_ref[...].astype(F32)
        for d in range(groups):
            base = place_of(me ^ d, groups) * per_pair
            for j in range(per_pair):
                at = pl.ds(order[base + j], 1)
                to = d * 2 * per_pair + j
                sent_f[to : to + 1, :] = wide[0, at, :]
                sent_f[to + per_pair : to + per_pair + 1, :] = wide[1, at, :]
        for d in range(groups):
            piece = sent_f[d * 2 * per_pair : (d + 1) * 2 * per_pair, :].astype(BF16)
            for m in range(parts):
                sent_ref[d, m] = piece

        def source(s, _):
            base = place_of(s ^ me, groups) * per_pair

            def one(i, found):
                v = owner[s * requests + i]
                mine = v // requests == me
                spot = v % requests
                arriving[jnp.where(mine, base + found, requests)] = spot
                inverse[jnp.where(mine, spot, requests)] = base + found
                return found + mine.astype(I32)

            lax.fori_loop(0, requests, one, jnp.int32(0), unroll=8)
            return 0

        lax.fori_loop(0, groups, source, 0)
        row = lax.broadcasted_iota(I32, (requests, 128), 0)
        long_row = lax.broadcasted_iota(I32, (rows, 128), 0)
        lane = lax.broadcasted_iota(I32, (requests, 128), 1)
        long_lane = lax.broadcasted_iota(I32, (rows, 128), 1)
        arr = jnp.zeros((requests, 128), I32)
        inv = jnp.zeros((requests, 128), I32)
        num = jnp.zeros((requests, 128), I32)
        back = jnp.zeros((rows, 128), I32)
        lane_row = lax.broadcasted_iota(I32, (8, 128), 1)
        sub_row = lax.broadcasted_iota(I32, (8, 128), 0)
        lane_counts = jnp.zeros((8, 128), I32)
        half = requests // 2
        for q in range(requests):
            at = row == q
            a = arriving[q]
            n = cnt[a]
            arr = jnp.where(at, a, arr)
            num = jnp.where(at, n, num)
            inv = jnp.where(at, inverse[q], inv)
            back = jnp.where(long_row // slots == q, inverse[q], back)
            lane_counts = jnp.where(
                (lane_row % half == q % half) & (sub_row == q // half), n, lane_counts
            )
        lanes_ref[...] = lane_counts
        spot = row // per_pair
        partner = (spot % (groups // 2)) * 2 + spot // (groups // 2)
        got = (me ^ partner) * (2 * per_pair) + row % per_pair
        blocks = []
        for t in range(slots):
            block = jnp.where(lane == SOURCE, arr * slots + t, 0)
            block = jnp.where(lane == LIVE, (num > t).astype(I32), block)
            block = jnp.where(lane == COUNT, num, block)
            block = jnp.where(lane == UNSORT, inv, block)
            block = jnp.where(lane == ATT, got, block)
            block = jnp.where(lane == FFN, got + per_pair, block)
            blocks.append(block)
        table = jnp.concatenate(blocks, axis=0)
        cols[...] = jnp.where(long_lane == BACK, back + (long_row % slots) * requests, table)

    return run(
        body,
        "make_plan",
        (rank,),
        (new_owner, counts, att, ffn),
        [
            pltpu.SMEM((requests,), I32),
            pltpu.SMEM((requests + 1,), I32),
            vmem((rows, 128), I32),
            vmem((8, 128), I32),
            vmem((groups, parts, 2 * per_pair, width), BF16),
        ],
        scratch=[
            pltpu.SMEM(new_owner.shape, I32),
            pltpu.SMEM(counts.shape, I32),
            pltpu.SMEM((groups,), I32),
            pltpu.SMEM((requests + 1,), I32),
            vmem(att.shape, BF16),
            vmem(ffn.shape, BF16),
            vmem((2, requests, width), F32),
            vmem((2 * requests, width), F32),
            pltpu.SemaphoreType.DMA((4,)),
        ],
        in_hbm=(0, 1, 2, 3),
    )


def pack_states(order, wkv_state, groups):
    requests, heads, cells = wkv_state.shape
    per_pair = requests // groups

    def body(order_ref, wkv, *rest):
        packed = rest[:groups]
        stage, sems = rest[groups:]
        copies = []
        for q in range(requests):
            copies.append(pltpu.make_async_copy(wkv.at[order_ref[q]], stage.at[q], sems.at[q]))
            copies[q].start()
        for q in range(requests):
            copies[q].wait()
            packed[q // per_pair][q % per_pair] = stage[q].astype(BF16)

    return run(
        body,
        "pack_states",
        (order,),
        (wkv_state,),
        [vmem((per_pair, heads, cells), BF16) for _ in range(groups)],
        scratch=[vmem(wkv_state.shape, F32), pltpu.SemaphoreType.DMA((requests,))],
        in_hbm=(0,),
    )


def chooser(cols, lane, rows, columns):
    return (lax.broadcasted_iota(I32, (rows, columns), 1) == cols[0:rows, lane : lane + 1]).astype(
        BF16
    )


def sort_shifts(cols, got):
    groups, parts, twice, width = got.shape
    requests = groups * twice // 2

    def body(ready, cols_ref, got_ref, att, ffn):
        ready()
        picks = [chooser(cols_ref, lane, requests, 2 * requests) for lane in (ATT, FFN)]
        for m in range(parts):
            rows = got_ref[:, m].astype(F32).reshape(2 * requests, width).astype(BF16)
            for pick, out in zip(picks, (att, ffn)):
                out[m] = dot32(pick, rows).astype(BF16)

    return run(
        body,
        "sort_shifts",
        (),
        (cols, got),
        [vmem((parts, requests, width), BF16)] * 2,
        fetch=(0, 1),
    )


def states_to_lanes(payloads, size, bring):
    per_pair, heads, cells = payloads[0].shape
    requests = per_pair * len(payloads)
    lanes = heads * requests
    together = 4

    def body(*refs):
        ins, out_ref, rows = refs[: len(payloads)], refs[len(payloads)], refs[len(payloads) + 1]

        def some(step, _):
            for c in range(together):
                at = pl.ds(pl.multiple_of((step * together + c) * 128, 128), 128)
                for k in range(len(payloads)):
                    for j in range(per_pair):
                        first = (k * per_pair + j) * heads
                        rows[c, first : first + heads, :] = ins[k][j, :, at].astype(F32)
            for c in range(together):
                block = jnp.concatenate(
                    [rows[c, pl.ds(h, requests, stride=heads), :] for h in range(heads)], axis=0
                )
                turned = block.T
                chunk = step * together + c
                for e in range(128 // size):
                    out_ref[chunk * (128 // size) + e] = turned[e * size : (e + 1) * size]
            return 0

        lax.fori_loop(0, cells // (128 * together), some, 0)

    return run(
        body,
        "states_to_lanes",
        (),
        payloads,
        [vmem((cells // size, size, lanes), F32)],
        scratch=[vmem((together, requests * heads, 128), F32)],
        bring=bring,
    )


def first_norm(place, toks, att, cols, norm, mix, down_d, down_a, down_g):
    rows, width = toks[0].shape
    parts = len(toks)
    total = parts * width
    requests = att.shape[1]
    slots = rows // requests
    small = down_d.shape[0]
    rank_g = down_g.shape[1]
    low_width = rank_g + 2 * small

    def body(ready, place_ref, *refs):
        tok = refs[:parts]
        att_ref, col, nrm, mx, dd, da, dg, normed, low, low_send, shift = refs[parts:]
        ready()
        pick = chooser(col, SOURCE, rows, rows)
        xs = [dot32(pick, t[...]) for t in tok]
        mean = sum(jnp.sum(x, axis=1, keepdims=True) for x in xs) / total
        cs = [x - mean for x in xs]
        var = sum(jnp.sum(c * c, axis=1, keepdims=True) for c in cs) / total
        scale = lax.rsqrt(var + 1e-05)
        for k in range(parts):
            at = pl.ds(pl.multiple_of((place_ref[0] ^ k) * width, 128), width)
            normed[k] = cs[k] * scale * nrm[0:1, at] + nrm[1:2, at]
        at = pl.ds(pl.multiple_of(place_ref[0] * width, 128), width)
        now = normed[0]
        before = jnp.concatenate([att_ref[place_ref[0]].astype(F32), now[: rows - requests]], axis=0)
        delta = before - now
        mixed = lambda c: (now + delta * mx[c : c + 1, at]).astype(BF16)
        nothing = jnp.zeros((small, width), BF16)
        low[:, 0:rank_g] = dot32(mixed(5), dg[...])
        low[:, rank_g:low_width] = dot32_turned(
            mixed(1), jnp.concatenate([dd[...], nothing], axis=0)
        ) + dot32_turned(mixed(4), jnp.concatenate([nothing, da[...]], axis=0))
        low_send[...] = low[...].astype(BF16)
        chosen = jnp.zeros((requests, width), F32)
        number = col[0:requests, COUNT : COUNT + 1]
        for t in range(slots):
            chosen = jnp.where(number == t + 1, now[t * requests : (t + 1) * requests], chosen)
        unsort = chooser(col, UNSORT, requests, requests)
        shift[...] = dot32(unsort, chosen.astype(BF16)).astype(BF16)

    return run(
        body,
        "first_norm",
        (place,),
        (*toks, att, cols, norm, mix, down_d, down_a, down_g),
        [
            vmem((parts, rows, width), F32),
            vmem((rows, low_width), F32),
            vmem((rows, low_width), BF16),
            vmem((requests, width), BF16),
        ],
        fetch=(*range(1, parts), *range(parts + 1, parts + 7)),
    )


def projections(place, normed, att, mix, weights):
    parts, rows, width = normed.shape
    requests = att.shape[1]
    out_width = weights[0].shape[1]

    def body(place_ref, n_ref, *refs):
        att_ref, mx, w, outs = refs[0], refs[1], refs[2:5], refs[5:]
        for which, c in enumerate((0, 2, 3)):
            for k in range(parts):
                at = pl.ds(pl.multiple_of((place_ref[0] ^ k) * width, 128), width)
                now = n_ref[k]
                before = jnp.concatenate(
                    [att_ref[place_ref[0] ^ k].astype(F32), now[: rows - requests]], axis=0
                )
                mixed = (now + (before - now) * mx[c : c + 1, at]).astype(BF16)
                term = dot32(mixed, w[which][at, :])
                total = term if k == 0 else total + term
            outs[which][...] = total

    return run(
        body,
        "projections",
        (place,),
        (normed, att, mix, *weights),
        [vmem((rows, out_width), F32) for _ in weights],
    )


def swap_groups(arrays, group):
    arrays = list(arrays)
    lanes = arrays[0].shape[1]
    where = lax.broadcasted_iota(I32, arrays[0].shape, 1) // group
    bit = 1
    while bit < len(arrays):
        low = (where // bit) % 2 == 0
        out = list(arrays)
        for a in range(len(arrays)):
            if a & bit == 0:
                first, second = arrays[a], arrays[a | bit]
                out[a] = jnp.where(low, first, pltpu.roll(second, bit * group, 1))
                out[a | bit] = jnp.where(low, pltpu.roll(first, lanes - bit * group, 1), second)
        arrays = out
        bit *= 2
    return arrays


def fold_eight(items, flags):
    shift = 1
    for flag in flags:
        items = [
            jnp.where(flag, a, b) + pltpu.roll(jnp.where(flag, b, a), shift, 0)
            for a, b in zip(items[0::2], items[1::2])
        ]
        shift *= 2
    return items[0]


def head_vectors(low_own, low_others, recept, key, value, head_params, ups, lane_counts, size):
    rows, width = recept.shape
    lanes = 128
    heads = width // size
    group = lanes // heads
    slots = 4
    halves = rows // slots // group
    n_groups = width // 128
    small = ups[0].shape[0]
    rank_g = ups[2].shape[0]
    n_others = len(low_others)
    pairs = [(t, b) for t in range(slots) for b in range(t + 1)]

    def body(low, *refs):
        others = refs[:n_others]
        (r_ref, k_ref, v_ref, hp, du, au, gu, cnt) = refs[n_others : n_others + 8]
        (w_out, c_out, v_out, kq_out, uq_out, d_out, g_out, b_out, vec) = refs[n_others + 8 :]
        total = low[...]
        for o in others:
            total = total + o[...].astype(F32)
        glow = jax.nn.sigmoid(total[:, 0:rank_g]).astype(BF16)
        pair = total[:, rank_g : rank_g + 2 * small]
        nothing = jnp.zeros((small, width), BF16)
        decay_in = dot32(
            jnp.tanh(pair).astype(BF16), jnp.concatenate([du[...], nothing], axis=0)
        )
        context_in = dot32(pair.astype(BF16), jnp.concatenate([nothing, au[...]], axis=0))
        decay = jnp.exp(-0.606531 * jax.nn.sigmoid(hp[0:1] + decay_in))
        context = jax.nn.sigmoid(hp[1:2] + context_in)
        g_out[...] = dot32(glow, gu[...])
        r = r_ref[...]
        k = k_ref[...]
        v = v_ref[...]
        scaled = k * hp[2:3]
        kmod = k * (1.0 + (context - 1.0) * hp[3:4])
        rk = r * kmod * hp[4:5]
        lane_r = lax.broadcasted_iota(I32, (128, 128), 0)
        lane_c = lax.broadcasted_iota(I32, (128, 128), 1)
        ones = ((lane_r // size) == (lane_c // size)).astype(BF16)
        for g in range(n_groups):
            at = slice(g * 128, (g + 1) * 128)
            high = rk[:, at].astype(BF16)
            rest = (rk[:, at] - high.astype(F32)).astype(BF16)
            b_out[:, at] = (dot32(high, ones) + dot32(rest, ones)) * v[:, at]

        for index, array in enumerate((r, kmod, scaled, decay, context, v)):
            pieces = []
            for g in range(n_groups):
                turned = array[:, g * 128 : (g + 1) * 128].T
                pieces += [turned[e * size : (e + 1) * size] for e in range(128 // size)]
            for at, piece in enumerate(swap_groups(pieces, group)):
                vec[index, at % halves, at // halves] = piece

        ksum = lambda x, y: jnp.sum(x * y, axis=0, keepdims=True)
        for g in range(halves):
            valid = [cnt[g : g + 1, :] > t for t in range(slots)]
            for t in range(slots):
                s = vec[2, g, t]
                unit = s * lax.rsqrt(jnp.sum(s * s, axis=0, keepdims=True) + 1e-06)
                vec[2, g, t] = unit
                vec[4, g, t] = unit * vec[4, g, t]

            def back_through(x, top, base):
                for b in range(top, -1, -1):
                    at = base + pairs.index((top + 1, b))
                    c_out[g, at : at + 1, :] = jnp.where(valid[b], ksum(vec[1, g, b], x), 0.0)
                    moved = vec[3, g, b] * x - vec[2, g, b] * ksum(vec[4, g, b], x)
                    x = jnp.where(valid[b], moved, x)
                return x

            for t in range(slots):
                w_out[g, t] = back_through(vec[2, g, t], t - 1, 0)
                x = vec[0, g, t]
                at = len(pairs) + pairs.index((t, t))
                c_out[g, at : at + 1, :] = ksum(vec[1, g, t], x)
                x = vec[3, g, t] * x - vec[2, g, t] * ksum(vec[4, g, t], x)
                w_out[g, slots + t] = back_through(x, t - 1, len(pairs))
            run_decay = jnp.ones((size, lanes), F32)
            for t in range(slots - 1, -1, -1):
                kq_out[g, t] = jnp.where(valid[t], vec[1, g, t] * run_decay, 0.0)
                uq_out[g, t] = jnp.where(valid[t], -(vec[4, g, t] * run_decay), 0.0)
                run_decay = jnp.where(valid[t], run_decay * vec[3, g, t], run_decay)
                v_out[g, t] = vec[5, g, t]
            d_out[g] = run_decay

    return run(
        body,
        "head_vectors",
        (),
        (low_own, *low_others, recept, key, value, head_params, *ups, lane_counts),
        [
            vmem((halves, 2 * slots, size, lanes), F32),
            vmem((halves, 2 * len(pairs), lanes), F32),
            vmem((halves, slots, size, lanes), F32),
            vmem((halves, slots, size, lanes), F32),
            vmem((halves, slots, size, lanes), F32),
            vmem((halves, size, lanes), F32),
            vmem((rows, width), F32),
            vmem((rows, width), F32),
        ],
        scratch=[vmem((6, halves, slots, size, lanes), F32)],
    )


def head_outputs(place, states, weights, coefs, values, gate, bonus, head_params, out_weight, parts):
    rows, width = gate.shape
    halves = len(states)
    size, lanes = states[0].shape[1:]
    slots = values.shape[1]
    group = rows // slots // halves
    n_groups = width // 128
    pairs = [(t, b) for t in range(slots) for b in range(t + 1)]
    quad = 4

    def body(place_ref, *refs):
        st = refs[:halves]
        w_ref, c_ref, v_ref, gate_ref, bonus_ref, hp, wo = refs[halves : halves + 7]
        outs = refs[halves + 7 : halves + 7 + parts]
        p_out, prod, done = refs[halves + 7 + parts :]
        sub = lax.broadcasted_iota(I32, (8, lanes), 0)
        folds = [(sub // s) % 2 == 0 for s in (1, 2, 4)]
        for g in range(halves):
            for part in range(2 * slots // quad):

                def products(block, _):
                    ws = [w_ref[g, part * quad + w] for w in range(quad)]
                    sums = [[] for _ in range(quad)]
                    for i in range(8):
                        s = st[g][block * 8 + i]
                        for w in range(quad):
                            term = s * ws[w]
                            acc = term[0:8]
                            for jv in range(1, size // 8):
                                acc = acc + term[jv * 8 : (jv + 1) * 8]
                            sums[w].append(acc)
                    at = pl.ds(pl.multiple_of(block * 8, 8), 8)
                    for w in range(quad):
                        prod[g, part * quad + w, at, :] = fold_eight(sums[w], folds)
                    return 0

                lax.fori_loop(0, size // 8, products, 0)

        by_group = [None] * (halves * slots)
        for g in range(halves):
            for t in range(slots):
                removed = prod[g, t]
                y = prod[g, slots + t]
                for b in range(t + 1):
                    at = pairs.index((t, b))
                    if b < t:
                        removed = removed + c_ref[g, at : at + 1, :] * v_ref[g, b]
                    at += len(pairs)
                    y = y + c_ref[g, at : at + 1, :] * v_ref[g, b]
                p_out[g, t] = removed
                center = y - jnp.mean(y, axis=0, keepdims=True)
                spread = jnp.mean(center * center, axis=0, keepdims=True)
                by_group[t * halves + g] = center * lax.rsqrt(spread + 0.00064)
        backs = swap_groups(by_group, group)
        each = 128 // size
        for g in range(n_groups):
            at = slice(g * 128, (g + 1) * 128)
            turned = jnp.concatenate(backs[each * g : each * (g + 1)], axis=0).T
            full = (turned * hp[5:6, at] + hp[6:7, at] + bonus_ref[:, at]) * gate_ref[:, at]
            done[:, at] = full.astype(BF16)
        for q in range(parts):
            at = pl.ds(pl.multiple_of((place_ref[0] ^ q) * width, 128), width)
            outs[q][...] = dot32(done[...], wo[:, at]).astype(outs[q].dtype)

    return run(
        body,
        "head_outputs",
        (place,),
        (*states, weights, coefs, values, gate, bonus, head_params, out_weight),
        [vmem((rows, width), F32)]
        + [vmem((rows, width), BF16) for _ in range(parts - 1)]
        + [vmem(values.shape, F32)],
        scratch=[vmem(weights.shape, F32), vmem((rows, width), BF16)],
    )


def final_states(arriving, states, removed, values, keys, units, decay, heads):
    halves = len(states)
    size, _, lanes = states[0].shape
    slots = removed.shape[1]
    half = lanes // heads
    requests = half * halves
    step_chunks = 4
    per_chunk = 128 // size
    steps = size // (per_chunk * step_chunks)
    cells = size * size

    def body(arr_ref, *refs):
        st = refs[:halves]
        p_ref, v_ref, kq_ref, uq_ref, d_ref, out_ref, new, rows = refs[halves:]
        step = pl.program_id(0)
        for g in range(halves):

            def update(block, _):
                first = block * 4
                real = step * (per_chunk * step_chunks) + first
                lefts = []
                for i in range(4):
                    row = [v_ref[g, t, pl.ds(real + i, 1), :] for t in range(slots)]
                    row += [p_ref[g, t, pl.ds(real + i, 1), :] for t in range(slots)]
                    lefts.append([jnp.broadcast_to(x, (8, lanes)) for x in row])
                for jv in range(size // 8):
                    at = slice(jv * 8, (jv + 1) * 8)
                    rights = [kq_ref[g, t, at, :] for t in range(slots)]
                    rights += [uq_ref[g, t, at, :] for t in range(slots)]
                    decayed = d_ref[g, at, :]
                    for i in range(4):
                        acc = st[g][real + i, at, :] * decayed
                        for left, right in zip(lefts[i], rights):
                            acc = acc + left * right
                        new[g, first + i, at, :] = acc
                return 0

            lax.fori_loop(0, per_chunk * step_chunks // 4, update, 0)
        for c in range(step_chunks):
            for g in range(halves):
                block = [new[g, per_chunk * c + e] for e in range(per_chunk)]
                turned = jnp.concatenate(block, axis=0).T
                for h in range(heads):
                    rows[c, pl.ds(g * half * heads + h, half, stride=heads), :] = turned[
                        h * half : (h + 1) * half
                    ]
        for c in range(step_chunks):
            for q in range(requests):
                out_ref[arr_ref[q], :, c * 128 : (c + 1) * 128] = rows[
                    c, q * heads : (q + 1) * heads, :
                ]

    args = (*states, removed, values, keys, units, decay)
    return pl.pallas_call(
        body,
        grid_spec=pltpu.PrefetchScalarGridSpec(
            num_scalar_prefetch=1,
            grid=(steps,),
            in_specs=[pl.BlockSpec(memory_space=pltpu.VMEM) for _ in args],
            out_specs=pl.BlockSpec((requests, heads, 128 * step_chunks), lambda s, a: (0, 0, s)),
            scratch_shapes=[
                vmem((halves, per_chunk * step_chunks, size, lanes), F32),
                vmem((step_chunks, requests * heads, 128), F32),
            ],
        ),
        out_shape=jax.ShapeDtypeStruct((requests, heads, cells), F32),
        compiler_params=pltpu.CompilerParams(vmem_limit_bytes=SCRATCH_LIMIT),
        name="final_states",
    )(arriving, *[pltpu.with_memory_space_constraint(a, pltpu.VMEM) for a in args])


def middle(tok, cols, own, others):
    rows, width = tok.shape

    def body(tok_ref, col, own_ref, *refs):
        out = refs[-1]
        total = dot32(chooser(col, SOURCE, rows, rows), tok_ref[...]) + own_ref[...]
        for o in refs[:-1]:
            total = total + o[...].astype(F32)
        out[...] = total.astype(BF16)

    return run(body, "middle", (), (tok, cols, own, *others), [vmem((rows, width), BF16)])[0]


def channel_mix(place, mids, prev, cols, norm, mix, key_weight, value_weight):
    parts = len(mids)
    rows, width = mids[0].shape
    total = parts * width
    requests = prev.shape[1]
    slots = rows // requests

    def body(ready, place_ref, *refs):
        mid = refs[:parts]
        prev_ref, col, nrm, mx, kw, vw = refs[parts : parts + 6]
        outs, shift = refs[parts + 6 : 2 * parts + 6], refs[2 * parts + 6]
        xs = [m[...].astype(F32) for m in mid]
        mean = sum(jnp.sum(x, axis=1, keepdims=True) for x in xs) / total
        cs = [x - mean for x in xs]
        var = sum(jnp.sum(c * c, axis=1, keepdims=True) for c in cs) / total
        scale = lax.rsqrt(var + 1e-05)
        ready()
        acc = None
        for k in range(parts):
            at = pl.ds(pl.multiple_of((place_ref[0] ^ k) * width, 128), width)
            now = cs[k] * scale * nrm[2:3, at] + nrm[3:4, at]
            before = jnp.concatenate([prev_ref[place_ref[0] ^ k].astype(F32), now[: rows - requests]], axis=0)
            term = dot32((now + (before - now) * mx[6:7, at]).astype(BF16), kw[at, :])
            acc = term if k == 0 else acc + term
            if k == 0:
                chosen = jnp.zeros((requests, width), F32)
                number = col[0:requests, COUNT : COUNT + 1]
                for t in range(slots):
                    chosen = jnp.where(
                        number == t + 1, now[t * requests : (t + 1) * requests], chosen
                    )
                unsort = chooser(col, UNSORT, requests, requests)
                shift[...] = dot32(unsort, chosen.astype(BF16)).astype(BF16)
        h = jnp.maximum(acc, 0.0)
        hidden = (h * h).astype(BF16)
        for q in range(parts):
            at = pl.ds(pl.multiple_of((place_ref[0] ^ q) * width, 128), width)
            outs[q][...] = dot32(hidden, vw[:, at]).astype(outs[q].dtype)

    return run(
        body,
        "channel_mix",
        (place,),
        (*mids, prev, cols, norm, mix, key_weight, value_weight),
        [vmem((rows, width), F32)]
        + [vmem((rows, width), BF16) for _ in range(parts - 1)]
        + [vmem((requests, width), BF16)],
        fetch=(parts + 2, parts + 3),
    )


def finish(mid, own, others, cols):
    rows, width = mid.shape

    def body(mid_ref, own_ref, *refs):
        col, out = refs[-2:]
        total = own_ref[...]
        for o in refs[:-2]:
            total = total + o[...].astype(F32)
        live = col[:, LIVE : LIVE + 1] > 0
        total = jnp.where(live, mid_ref[...].astype(F32) + total, 0.0).astype(BF16)
        out[...] = dot32(chooser(col, BACK, rows, rows), total).astype(BF16)

    return run(body, "finish", (), (mid, own, *others, cols), [vmem((rows, width), BF16)])[0]


def per_device(
    groups,
    parts,
    tokens,
    counts,
    new_owner,
    wkv_state,
    att_shift,
    ffn_shift,
    norm_params,
    mix_coeffs,
    head_params,
    recept_weight,
    key_weight,
    value_weight,
    output_weight,
    decay_down,
    decay_up,
    alpha_down,
    alpha_up,
    gate_down,
    gate_up,
    ffn_key_weight,
    ffn_value_weight,
):
    requests, slots, width = tokens.shape
    heads = wkv_state.shape[1]
    size = width // heads
    rows = requests * slots
    rank = lax.axis_index("req").astype(I32).reshape(1)
    place = lax.axis_index("mdl").astype(I32).reshape(1)
    gather = lambda x: [x] + [xor_permute(x, "mdl", parts, k) for k in range(1, parts)]
    scatter = lambda xs: [xor_permute(xs[k], "mdl", parts, k) for k in range(1, parts)]

    toks = gather(tokens.reshape(rows, width))
    order, arriving, cols, lane_counts, sent = make_plan(
        rank, new_owner, counts, att_shift, ffn_shift, groups, parts, slots
    )
    order, toks[1], toks[2] = lax.optimization_barrier((order, toks[1], toks[2]))
    packed = pack_states(order, wkv_state, groups)
    got = lax.all_to_all(
        sent.reshape(groups * parts, -1, width),
        ("req", "mdl"),
        split_axis=0,
        concat_axis=0,
        tiled=True,
    )
    att, ffn = sort_shifts(cols, got.reshape(groups, parts, -1, width))

    normed, low, low_send, new_att = first_norm(
        place,
        toks,
        att,
        cols,
        norm_params,
        mix_coeffs,
        decay_down.T,
        alpha_down.T,
        gate_down,
    )
    partners = positions(groups)
    issue = [1] + [k for k in partners if k > 1]
    moved = {k: xor_permute(packed[partners.index(k)], "req", groups, k) for k in issue}
    moved[0] = packed[0]
    payloads = [moved[k] for k in partners]
    split = groups // 2
    first_half, recept_near, key_near, mix_near = states_to_lanes(
        payloads[:split], size, (recept_weight, key_weight, mix_coeffs)
    )
    second_half, value_near, out_near, head_near, *ups = states_to_lanes(
        payloads[split:],
        size,
        (value_weight, output_weight, head_params, decay_up, alpha_up, gate_up),
    )
    states = [first_half, second_half]
    low_others = gather(low_send)[1:]
    recept, key, value = projections(
        place, normed, att, mix_near, (recept_near, key_near, value_near)
    )
    weights, coefs, vals, keys, units, decay, gate, bonus = head_vectors(
        low,
        low_others,
        recept,
        key,
        value,
        head_near,
        ups,
        lane_counts,
        size,
    )
    results = head_outputs(
        place, states, weights, coefs, vals, gate, bonus, head_near, out_near, parts
    )
    outs, removed = results[:parts], results[parts]
    mid = middle(toks[0], cols, outs[0], scatter(outs))
    new_state = final_states(arriving, states, removed, vals, keys, units, decay, heads)
    results = channel_mix(
        place,
        gather(mid),
        ffn,
        cols,
        norm_params,
        mix_coeffs,
        ffn_key_weight,
        ffn_value_weight,
    )
    outs, new_ffn = results[:parts], results[parts]
    block = finish(mid, outs[0], scatter(outs), cols)
    return (block.reshape(requests, slots, width), new_state, new_att, new_ffn)


def solution(mesh):
    return jax.shard_map(
        functools.partial(per_device, mesh.shape["req"], mesh.shape["mdl"]),
        mesh=mesh,
        in_specs=(
            P("req", None, "mdl"),
            P("req"),
            P(),
            P("req", "mdl", None),
            P("req", "mdl"),
            P("req", "mdl"),
            P(),
            P(),
            P(None, "mdl"),
            P(None, "mdl"),
            P(None, "mdl"),
            P(None, "mdl"),
            P("mdl", None),
            P("mdl", None),
            P(None, "mdl"),
            P("mdl", None),
            P(None, "mdl"),
            P("mdl", None),
            P(None, "mdl"),
            P(None, "mdl"),
            P("mdl", None),
        ),
        out_specs=(P("req", None, "mdl"), P("req", "mdl", None), P("req", "mdl"), P("req", "mdl")),
        check_vma=False,
    )
```

```python
import functools

import jax
import jax.numpy as jnp
from jax import lax
from jax.experimental import pallas as pl
from jax.experimental.pallas import tpu as pltpu
from jax.sharding import PartitionSpec as P

F32 = jnp.float32
BF16 = jnp.bfloat16
I32 = jnp.int32
SCRATCH_LIMIT = 16 * 1024 * 1024


def xor_permute(x, axis, size, k):
    return lax.ppermute(x, axis, [(a, a ^ k) for a in range(size)])


def dot32(a, b):
    return jnp.dot(a, b, preferred_element_type=F32)


def dot32_turned(a, b):
    return lax.dot_general(a, b, (((1,), (1,)), ((), ())), preferred_element_type=F32)


def vmem(shape, dtype):
    return pltpu.VMEM(shape, dtype)


def run(body, name, scalars, args, outs, scratch=(), fetch=(), in_hbm=(), bring=()):
    n_own, n_made = len(args), len(outs)
    args = (*args, *bring)
    outs = [*outs, *[vmem(b.shape, b.dtype) for b in bring]]
    far = set(fetch) | set(in_hbm) | set(range(n_own, len(args)))
    anywhere = pl.BlockSpec(memory_space=pltpu.HBM)
    near = pl.BlockSpec(memory_space=pltpu.VMEM)
    n_scalars, n_args, n_outs = len(scalars), len(args), len(outs)

    def whole(*refs):
        if not bring:
            return inner(*refs)
        refs = list(refs)
        sems = refs.pop()
        first = n_scalars + n_own
        sources = refs[first : first + len(bring)]
        del refs[first : first + len(bring)]
        first += n_made
        targets = refs[first : first + len(bring)]
        del refs[first : first + len(bring)]
        copies = [
            pltpu.make_async_copy(a, b, sems.at[i])
            for i, (a, b) in enumerate(zip(sources, targets))
        ]
        for c in copies:
            c.start()
        inner(*refs)
        for c in copies:
            c.wait()

    def inner(*refs):
        refs = list(refs)
        if not fetch:
            return body(*refs)
        sems = refs.pop()
        first = len(refs) - len(fetch)
        buffers = refs[first:]
        refs = refs[:first]
        copies = []
        for at, (i, buffer) in enumerate(zip(fetch, buffers)):
            copies.append(pltpu.make_async_copy(refs[n_scalars + i], buffer, sems.at[at]))
            refs[n_scalars + i] = buffer
        for c in copies:
            c.start()

        def ready(which=None):
            for c in copies if which is None else [copies[which]]:
                c.wait()

        return body(ready, *refs)

    extra = [pltpu.VMEM(args[i].shape, args[i].dtype) for i in fetch]
    if fetch:
        extra.append(pltpu.SemaphoreType.DMA((len(fetch),)))
    if bring:
        extra.append(pltpu.SemaphoreType.DMA((len(bring),)))
    return pl.pallas_call(
        whole,
        grid_spec=pltpu.PrefetchScalarGridSpec(
            num_scalar_prefetch=n_scalars,
            grid=(1,),
            in_specs=[anywhere if i in far else near for i in range(n_args)],
            out_specs=[
                pl.BlockSpec(memory_space=pltpu.SMEM) if o.memory_space == pltpu.SMEM else near
                for o in outs
            ],
            scratch_shapes=list(scratch) + extra,
        ),
        out_shape=[
            jax.ShapeDtypeStruct(o.shape, o.dtype) if o.memory_space == pltpu.SMEM else o
            for o in outs
        ],
        compiler_params=pltpu.CompilerParams(vmem_limit_bytes=SCRATCH_LIMIT),
        name=name,
    )(
        *scalars,
        *[
            pltpu.with_memory_space_constraint(a, pltpu.HBM if i in far else pltpu.VMEM)
            for i, a in enumerate(args)
        ],
    )


def positions(groups):
    return list(range(0, groups, 2)) + list(range(1, groups, 2))


def place_of(k, groups):
    return k // 2 + (k % 2) * (groups // 2)


SOURCE, BACK, LIVE, COUNT, UNSORT, ATT, FFN = range(7)


def make_plan(rank, new_owner, counts, att, ffn, groups, parts, slots):
    requests, width = att.shape
    per_pair = requests // groups
    rows = requests * slots

    def body(
        rank_ref, owner_far, cnt_far, att_far, ffn_far,
        order, arriving, cols, lanes_ref, sent_ref,
        owner, cnt, turn, inverse, att_ref, ffn_ref, wide, sent_f, sems,
    ):
        me = rank_ref[0]
        copies = [
            pltpu.make_async_copy(owner_far, owner, sems.at[0]),
            pltpu.make_async_copy(cnt_far, cnt, sems.at[1]),
            pltpu.make_async_copy(att_far, att_ref, sems.at[2]),
            pltpu.make_async_copy(ffn_far, ffn_ref, sems.at[3]),
        ]
        for c in copies:
            c.start()
        for g in range(groups):
            turn[g] = 0
        copies[0].wait()

        def own(i, _):
            spot = place_of((owner[me * requests + i] // requests) ^ me, groups)
            order[spot * per_pair + turn[spot]] = i
            turn[spot] = turn[spot] + 1
            return 0

        lax.fori_loop(0, requests, own, 0, unroll=4)
        for c in copies[1:]:
            c.wait()
        wide[0] = att_ref[...].astype(F32)
        wide[1] = ffn_ref[...].astype(F32)
        for d in range(groups):
            base = place_of(me ^ d, groups) * per_pair
            for j in range(per_pair):
                at = pl.ds(order[base + j], 1)
                to = d * 2 * per_pair + j
                sent_f[to : to + 1, :] = wide[0, at, :]
                sent_f[to + per_pair : to + per_pair + 1, :] = wide[1, at, :]
        for d in range(groups):
            piece = sent_f[d * 2 * per_pair : (d + 1) * 2 * per_pair, :].astype(BF16)
            for m in range(parts):
                sent_ref[d, m] = piece

        def source(s, _):
            base = place_of(s ^ me, groups) * per_pair

            def one(i, found):
                v = owner[s * requests + i]
                mine = v // requests == me
                spot = v % requests
                arriving[jnp.where(mine, base + found, requests)] = spot
                inverse[jnp.where(mine, spot, requests)] = base + found
                return found + mine.astype(I32)

            lax.fori_loop(0, requests, one, jnp.int32(0), unroll=8)
            return 0

        lax.fori_loop(0, groups, source, 0)
        row = lax.broadcasted_iota(I32, (requests, 128), 0)
        long_row = lax.broadcasted_iota(I32, (rows, 128), 0)
        lane = lax.broadcasted_iota(I32, (requests, 128), 1)
        long_lane = lax.broadcasted_iota(I32, (rows, 128), 1)
        arr = jnp.zeros((requests, 128), I32)
        inv = jnp.zeros((requests, 128), I32)
        num = jnp.zeros((requests, 128), I32)
        back = jnp.zeros((rows, 128), I32)
        lane_row = lax.broadcasted_iota(I32, (8, 128), 1)
        sub_row = lax.broadcasted_iota(I32, (8, 128), 0)
        lane_counts = jnp.zeros((8, 128), I32)
        half = requests // 2
        for q in range(requests):
            at = row == q
            a = arriving[q]
            n = cnt[a]
            arr = jnp.where(at, a, arr)
            num = jnp.where(at, n, num)
            inv = jnp.where(at, inverse[q], inv)
            back = jnp.where(long_row // slots == q, inverse[q], back)
            lane_counts = jnp.where(
                (lane_row % half == q % half) & (sub_row == q // half), n, lane_counts
            )
        lanes_ref[...] = lane_counts
        spot = row // per_pair
        partner = (spot % (groups // 2)) * 2 + spot // (groups // 2)
        got = (me ^ partner) * (2 * per_pair) + row % per_pair
        blocks = []
        for t in range(slots):
            block = jnp.where(lane == SOURCE, arr * slots + t, 0)
            block = jnp.where(lane == LIVE, (num > t).astype(I32), block)
            block = jnp.where(lane == COUNT, num, block)
            block = jnp.where(lane == UNSORT, inv, block)
            block = jnp.where(lane == ATT, got, block)
            block = jnp.where(lane == FFN, got + per_pair, block)
            blocks.append(block)
        table = jnp.concatenate(blocks, axis=0)
        cols[...] = jnp.where(long_lane == BACK, back + (long_row % slots) * requests, table)

    return run(
        body,
        "make_plan",
        (rank,),
        (new_owner, counts, att, ffn),
        [
            pltpu.SMEM((requests,), I32),
            pltpu.SMEM((requests + 1,), I32),
            vmem((rows, 128), I32),
            vmem((8, 128), I32),
            vmem((groups, parts, 2 * per_pair, width), BF16),
        ],
        scratch=[
            pltpu.SMEM(new_owner.shape, I32),
            pltpu.SMEM(counts.shape, I32),
            pltpu.SMEM((groups,), I32),
            pltpu.SMEM((requests + 1,), I32),
            vmem(att.shape, BF16),
            vmem(ffn.shape, BF16),
            vmem((2, requests, width), F32),
            vmem((2 * requests, width), F32),
            pltpu.SemaphoreType.DMA((4,)),
        ],
        in_hbm=(0, 1, 2, 3),
    )


def pack_states(order, wkv_state, groups):
    requests, heads, cells = wkv_state.shape
    per_pair = requests // groups

    def body(order_ref, wkv, *rest):
        packed = rest[:groups]
        stage, sems = rest[groups:]
        copies = []
        for q in range(requests):
            copies.append(pltpu.make_async_copy(wkv.at[order_ref[q]], stage.at[q], sems.at[q]))
            copies[q].start()
        for q in range(requests):
            copies[q].wait()
            packed[q // per_pair][q % per_pair] = stage[q].astype(BF16)

    return run(
        body,
        "pack_states",
        (order,),
        (wkv_state,),
        [vmem((per_pair, heads, cells), BF16) for _ in range(groups)],
        scratch=[vmem(wkv_state.shape, F32), pltpu.SemaphoreType.DMA((requests,))],
        in_hbm=(0,),
    )


def chooser(cols, lane, rows, columns):
    return (lax.broadcasted_iota(I32, (rows, columns), 1) == cols[0:rows, lane : lane + 1]).astype(
        BF16
    )


def sort_shifts(cols, got):
    groups, parts, twice, width = got.shape
    requests = groups * twice // 2

    def body(ready, cols_ref, got_ref, att, ffn):
        ready()
        picks = [chooser(cols_ref, lane, requests, 2 * requests) for lane in (ATT, FFN)]
        for m in range(parts):
            rows = got_ref[:, m].astype(F32).reshape(2 * requests, width).astype(BF16)
            for pick, out in zip(picks, (att, ffn)):
                out[m] = dot32(pick, rows).astype(BF16)

    return run(
        body,
        "sort_shifts",
        (),
        (cols, got),
        [vmem((parts, requests, width), BF16)] * 2,
        fetch=(0, 1),
    )


def states_to_lanes(payloads, size, bring):
    per_pair, heads, cells = payloads[0].shape
    requests = per_pair * len(payloads)
    lanes = heads * requests
    together = 4

    def body(*refs):
        ins, out_ref, rows = refs[: len(payloads)], refs[len(payloads)], refs[len(payloads) + 1]

        def some(step, _):
            for c in range(together):
                at = pl.ds(pl.multiple_of((step * together + c) * 128, 128), 128)
                for k in range(len(payloads)):
                    for j in range(per_pair):
                        first = (k * per_pair + j) * heads
                        rows[c, first : first + heads, :] = ins[k][j, :, at].astype(F32)
            for c in range(together):
                block = jnp.concatenate(
                    [rows[c, pl.ds(h, requests, stride=heads), :] for h in range(heads)], axis=0
                )
                turned = block.T
                chunk = step * together + c
                for e in range(128 // size):
                    out_ref[chunk * (128 // size) + e] = turned[e * size : (e + 1) * size]
            return 0

        lax.fori_loop(0, cells // (128 * together), some, 0)

    return run(
        body,
        "states_to_lanes",
        (),
        payloads,
        [vmem((cells // size, size, lanes), F32)],
        scratch=[vmem((together, requests * heads, 128), F32)],
        bring=bring,
    )


def first_norm(place, toks, att, cols, norm, mix, down_d, down_a, down_g):
    rows, width = toks[0].shape
    parts = len(toks)
    total = parts * width
    requests = att.shape[1]
    slots = rows // requests
    small = down_d.shape[0]
    rank_g = down_g.shape[1]
    low_width = rank_g + 2 * small

    def body(ready, place_ref, *refs):
        tok = refs[:parts]
        att_ref, col, nrm, mx, dd, da, dg, normed, low, low_send, shift = refs[parts:]
        ready()
        pick = chooser(col, SOURCE, rows, rows)
        xs = [dot32(pick, t[...]) for t in tok]
        mean = sum(jnp.sum(x, axis=1, keepdims=True) for x in xs) / total
        cs = [x - mean for x in xs]
        var = sum(jnp.sum(c * c, axis=1, keepdims=True) for c in cs) / total
        scale = lax.rsqrt(var + 1e-05)
        for k in range(parts):
            at = pl.ds(pl.multiple_of((place_ref[0] ^ k) * width, 128), width)
            normed[k] = cs[k] * scale * nrm[0:1, at] + nrm[1:2, at]
        at = pl.ds(pl.multiple_of(place_ref[0] * width, 128), width)
        now = normed[0]
        before = jnp.concatenate([att_ref[place_ref[0]].astype(F32), now[: rows - requests]], axis=0)
        delta = before - now
        mixed = lambda c: (now + delta * mx[c : c + 1, at]).astype(BF16)
        nothing = jnp.zeros((small, width), BF16)
        low[:, 0:rank_g] = dot32(mixed(5), dg[...])
        low[:, rank_g:low_width] = dot32_turned(
            mixed(1), jnp.concatenate([dd[...], nothing], axis=0)
        ) + dot32_turned(mixed(4), jnp.concatenate([nothing, da[...]], axis=0))
        low_send[...] = low[...].astype(BF16)
        chosen = jnp.zeros((requests, width), F32)
        number = col[0:requests, COUNT : COUNT + 1]
        for t in range(slots):
            chosen = jnp.where(number == t + 1, now[t * requests : (t + 1) * requests], chosen)
        unsort = chooser(col, UNSORT, requests, requests)
        shift[...] = dot32(unsort, chosen.astype(BF16)).astype(BF16)

    return run(
        body,
        "first_norm",
        (place,),
        (*toks, att, cols, norm, mix, down_d, down_a, down_g),
        [
            vmem((parts, rows, width), F32),
            vmem((rows, low_width), F32),
            vmem((rows, low_width), BF16),
            vmem((requests, width), BF16),
        ],
        fetch=(*range(1, parts), *range(parts + 1, parts + 7)),
    )


def projections(place, normed, att, mix, weights):
    parts, rows, width = normed.shape
    requests = att.shape[1]
    out_width = weights[0].shape[1]

    def body(place_ref, n_ref, *refs):
        att_ref, mx, w, outs = refs[0], refs[1], refs[2:5], refs[5:]
        for which, c in enumerate((0, 2, 3)):
            for k in range(parts):
                at = pl.ds(pl.multiple_of((place_ref[0] ^ k) * width, 128), width)
                now = n_ref[k]
                before = jnp.concatenate(
                    [att_ref[place_ref[0] ^ k].astype(F32), now[: rows - requests]], axis=0
                )
                mixed = (now + (before - now) * mx[c : c + 1, at]).astype(BF16)
                term = dot32(mixed, w[which][at, :])
                total = term if k == 0 else total + term
            outs[which][...] = total

    return run(
        body,
        "projections",
        (place,),
        (normed, att, mix, *weights),
        [vmem((rows, out_width), F32) for _ in weights],
    )


def swap_groups(arrays, group):
    arrays = list(arrays)
    lanes = arrays[0].shape[1]
    where = lax.broadcasted_iota(I32, arrays[0].shape, 1) // group
    bit = 1
    while bit < len(arrays):
        low = (where // bit) % 2 == 0
        out = list(arrays)
        for a in range(len(arrays)):
            if a & bit == 0:
                first, second = arrays[a], arrays[a | bit]
                out[a] = jnp.where(low, first, pltpu.roll(second, bit * group, 1))
                out[a | bit] = jnp.where(low, pltpu.roll(first, lanes - bit * group, 1), second)
        arrays = out
        bit *= 2
    return arrays


def fold_eight(items, flags):
    shift = 1
    for flag in flags:
        items = [
            jnp.where(flag, a, b) + pltpu.roll(jnp.where(flag, b, a), shift, 0)
            for a, b in zip(items[0::2], items[1::2])
        ]
        shift *= 2
    return items[0]


def head_vectors(low_own, low_others, recept, key, value, head_params, ups, lane_counts, size):
    rows, width = recept.shape
    lanes = 128
    heads = width // size
    group = lanes // heads
    slots = 4
    halves = rows // slots // group
    n_groups = width // 128
    small = ups[0].shape[0]
    rank_g = ups[2].shape[0]
    n_others = len(low_others)
    pairs = [(t, b) for t in range(slots) for b in range(t + 1)]

    def body(low, *refs):
        others = refs[:n_others]
        (r_ref, k_ref, v_ref, hp, du, au, gu, cnt) = refs[n_others : n_others + 8]
        (w_out, c_out, v_out, kq_out, uq_out, d_out, g_out, b_out, vec) = refs[n_others + 8 :]
        total = low[...]
        for o in others:
            total = total + o[...].astype(F32)
        glow = jax.nn.sigmoid(total[:, 0:rank_g]).astype(BF16)
        pair = total[:, rank_g : rank_g + 2 * small]
        nothing = jnp.zeros((small, width), BF16)
        decay_in = dot32(
            jnp.tanh(pair).astype(BF16), jnp.concatenate([du[...], nothing], axis=0)
        )
        context_in = dot32(pair.astype(BF16), jnp.concatenate([nothing, au[...]], axis=0))
        decay = jnp.exp(-0.606531 * jax.nn.sigmoid(hp[0:1] + decay_in))
        context = jax.nn.sigmoid(hp[1:2] + context_in)
        g_out[...] = dot32(glow, gu[...])
        r = r_ref[...]
        k = k_ref[...]
        v = v_ref[...]
        scaled = k * hp[2:3]
        kmod = k * (1.0 + (context - 1.0) * hp[3:4])
        rk = r * kmod * hp[4:5]
        lane_r = lax.broadcasted_iota(I32, (128, 128), 0)
        lane_c = lax.broadcasted_iota(I32, (128, 128), 1)
        ones = ((lane_r // size) == (lane_c // size)).astype(BF16)
        for g in range(n_groups):
            at = slice(g * 128, (g + 1) * 128)
            high = rk[:, at].astype(BF16)
            rest = (rk[:, at] - high.astype(F32)).astype(BF16)
            b_out[:, at] = (dot32(high, ones) + dot32(rest, ones)) * v[:, at]

        for index, array in enumerate((r, kmod, scaled, decay, context, v)):
            pieces = []
            for g in range(n_groups):
                turned = array[:, g * 128 : (g + 1) * 128].T
                pieces += [turned[e * size : (e + 1) * size] for e in range(128 // size)]
            for at, piece in enumerate(swap_groups(pieces, group)):
                vec[index, at % halves, at // halves] = piece

        ksum = lambda x, y: jnp.sum(x * y, axis=0, keepdims=True)
        for g in range(halves):
            valid = [cnt[g : g + 1, :] > t for t in range(slots)]
            for t in range(slots):
                s = vec[2, g, t]
                unit = s * lax.rsqrt(jnp.sum(s * s, axis=0, keepdims=True) + 1e-06)
                vec[2, g, t] = unit
                vec[4, g, t] = unit * vec[4, g, t]

            def back_through(x, top, base):
                for b in range(top, -1, -1):
                    at = base + pairs.index((top + 1, b))
                    c_out[g, at : at + 1, :] = jnp.where(valid[b], ksum(vec[1, g, b], x), 0.0)
                    moved = vec[3, g, b] * x - vec[2, g, b] * ksum(vec[4, g, b], x)
                    x = jnp.where(valid[b], moved, x)
                return x

            for t in range(slots):
                w_out[g, t] = back_through(vec[2, g, t], t - 1, 0)
                x = vec[0, g, t]
                at = len(pairs) + pairs.index((t, t))
                c_out[g, at : at + 1, :] = ksum(vec[1, g, t], x)
                x = vec[3, g, t] * x - vec[2, g, t] * ksum(vec[4, g, t], x)
                w_out[g, slots + t] = back_through(x, t - 1, len(pairs))
            run_decay = jnp.ones((size, lanes), F32)
            for t in range(slots - 1, -1, -1):
                kq_out[g, t] = jnp.where(valid[t], vec[1, g, t] * run_decay, 0.0)
                uq_out[g, t] = jnp.where(valid[t], -(vec[4, g, t] * run_decay), 0.0)
                run_decay = jnp.where(valid[t], run_decay * vec[3, g, t], run_decay)
                v_out[g, t] = vec[5, g, t]
            d_out[g] = run_decay

    return run(
        body,
        "head_vectors",
        (),
        (low_own, *low_others, recept, key, value, head_params, *ups, lane_counts),
        [
            vmem((halves, 2 * slots, size, lanes), F32),
            vmem((halves, 2 * len(pairs), lanes), F32),
            vmem((halves, slots, size, lanes), F32),
            vmem((halves, slots, size, lanes), F32),
            vmem((halves, slots, size, lanes), F32),
            vmem((halves, size, lanes), F32),
            vmem((rows, width), F32),
            vmem((rows, width), F32),
        ],
        scratch=[vmem((6, halves, slots, size, lanes), F32)],
    )


def head_outputs(place, states, weights, coefs, values, gate, bonus, head_params, out_weight, parts):
    rows, width = gate.shape
    halves = len(states)
    size, lanes = states[0].shape[1:]
    slots = values.shape[1]
    group = rows // slots // halves
    n_groups = width // 128
    pairs = [(t, b) for t in range(slots) for b in range(t + 1)]
    quad = 4

    def body(place_ref, *refs):
        st = refs[:halves]
        w_ref, c_ref, v_ref, gate_ref, bonus_ref, hp, wo = refs[halves : halves + 7]
        outs = refs[halves + 7 : halves + 7 + parts]
        p_out, prod, done = refs[halves + 7 + parts :]
        sub = lax.broadcasted_iota(I32, (8, lanes), 0)
        folds = [(sub // s) % 2 == 0 for s in (1, 2, 4)]
        for g in range(halves):
            for part in range(2 * slots // quad):

                def products(block, _):
                    ws = [w_ref[g, part * quad + w] for w in range(quad)]
                    sums = [[] for _ in range(quad)]
                    for i in range(8):
                        s = st[g][block * 8 + i]
                        for w in range(quad):
                            term = s * ws[w]
                            acc = term[0:8]
                            for jv in range(1, size // 8):
                                acc = acc + term[jv * 8 : (jv + 1) * 8]
                            sums[w].append(acc)
                    at = pl.ds(pl.multiple_of(block * 8, 8), 8)
                    for w in range(quad):
                        prod[g, part * quad + w, at, :] = fold_eight(sums[w], folds)
                    return 0

                lax.fori_loop(0, size // 8, products, 0)

        by_group = [None] * (halves * slots)
        for g in range(halves):
            for t in range(slots):
                removed = prod[g, t]
                y = prod[g, slots + t]
                for b in range(t + 1):
                    at = pairs.index((t, b))
                    if b < t:
                        removed = removed + c_ref[g, at : at + 1, :] * v_ref[g, b]
                    at += len(pairs)
                    y = y + c_ref[g, at : at + 1, :] * v_ref[g, b]
                p_out[g, t] = removed
                center = y - jnp.mean(y, axis=0, keepdims=True)
                spread = jnp.mean(center * center, axis=0, keepdims=True)
                by_group[t * halves + g] = center * lax.rsqrt(spread + 0.00064)
        backs = swap_groups(by_group, group)
        each = 128 // size
        for g in range(n_groups):
            at = slice(g * 128, (g + 1) * 128)
            turned = jnp.concatenate(backs[each * g : each * (g + 1)], axis=0).T
            full = (turned * hp[5:6, at] + hp[6:7, at] + bonus_ref[:, at]) * gate_ref[:, at]
            done[:, at] = full.astype(BF16)
        for q in range(parts):
            at = pl.ds(pl.multiple_of((place_ref[0] ^ q) * width, 128), width)
            outs[q][...] = dot32(done[...], wo[:, at]).astype(outs[q].dtype)

    return run(
        body,
        "head_outputs",
        (place,),
        (*states, weights, coefs, values, gate, bonus, head_params, out_weight),
        [vmem((rows, width), F32)]
        + [vmem((rows, width), BF16) for _ in range(parts - 1)]
        + [vmem(values.shape, F32)],
        scratch=[vmem(weights.shape, F32), vmem((rows, width), BF16)],
    )


def final_states(arriving, states, removed, values, keys, units, decay, heads):
    halves = len(states)
    size, _, lanes = states[0].shape
    slots = removed.shape[1]
    half = lanes // heads
    requests = half * halves
    step_chunks = 4
    per_chunk = 128 // size
    steps = size // (per_chunk * step_chunks)
    cells = size * size

    def body(arr_ref, *refs):
        st = refs[:halves]
        p_ref, v_ref, kq_ref, uq_ref, d_ref, out_ref, new, rows = refs[halves:]
        step = pl.program_id(0)
        for g in range(halves):

            def update(block, _):
                first = block * 4
                real = step * (per_chunk * step_chunks) + first
                lefts = []
                for i in range(4):
                    row = [v_ref[g, t, pl.ds(real + i, 1), :] for t in range(slots)]
                    row += [p_ref[g, t, pl.ds(real + i, 1), :] for t in range(slots)]
                    lefts.append([jnp.broadcast_to(x, (8, lanes)) for x in row])
                for jv in range(size // 8):
                    at = slice(jv * 8, (jv + 1) * 8)
                    rights = [kq_ref[g, t, at, :] for t in range(slots)]
                    rights += [uq_ref[g, t, at, :] for t in range(slots)]
                    decayed = d_ref[g, at, :]
                    for i in range(4):
                        acc = st[g][real + i, at, :] * decayed
                        for left, right in zip(lefts[i], rights):
                            acc = acc + left * right
                        new[g, first + i, at, :] = acc
                return 0

            lax.fori_loop(0, per_chunk * step_chunks // 4, update, 0)
        for c in range(step_chunks):
            for g in range(halves):
                block = [new[g, per_chunk * c + e] for e in range(per_chunk)]
                turned = jnp.concatenate(block, axis=0).T
                for h in range(heads):
                    rows[c, pl.ds(g * half * heads + h, half, stride=heads), :] = turned[
                        h * half : (h + 1) * half
                    ]
        for c in range(step_chunks):
            for q in range(requests):
                out_ref[arr_ref[q], :, c * 128 : (c + 1) * 128] = rows[
                    c, q * heads : (q + 1) * heads, :
                ]

    args = (*states, removed, values, keys, units, decay)
    return pl.pallas_call(
        body,
        grid_spec=pltpu.PrefetchScalarGridSpec(
            num_scalar_prefetch=1,
            grid=(steps,),
            in_specs=[pl.BlockSpec(memory_space=pltpu.VMEM) for _ in args],
            out_specs=pl.BlockSpec((requests, heads, 128 * step_chunks), lambda s, a: (0, 0, s)),
            scratch_shapes=[
                vmem((halves, per_chunk * step_chunks, size, lanes), F32),
                vmem((step_chunks, requests * heads, 128), F32),
            ],
        ),
        out_shape=jax.ShapeDtypeStruct((requests, heads, cells), F32),
        compiler_params=pltpu.CompilerParams(vmem_limit_bytes=SCRATCH_LIMIT),
        name="final_states",
    )(arriving, *[pltpu.with_memory_space_constraint(a, pltpu.VMEM) for a in args])


def middle(tok, cols, own, others):
    rows, width = tok.shape

    def body(tok_ref, col, own_ref, *refs):
        out = refs[-1]
        total = dot32(chooser(col, SOURCE, rows, rows), tok_ref[...]) + own_ref[...]
        for o in refs[:-1]:
            total = total + o[...].astype(F32)
        out[...] = total.astype(BF16)

    return run(body, "middle", (), (tok, cols, own, *others), [vmem((rows, width), BF16)])[0]


def channel_mix(place, mids, prev, cols, norm, mix, key_weight, value_weight):
    parts = len(mids)
    rows, width = mids[0].shape
    total = parts * width
    requests = prev.shape[1]
    slots = rows // requests

    def body(ready, place_ref, *refs):
        mid = refs[:parts]
        prev_ref, col, nrm, mx, kw, vw = refs[parts : parts + 6]
        outs, shift = refs[parts + 6 : 2 * parts + 6], refs[2 * parts + 6]
        xs = [m[...].astype(F32) for m in mid]
        mean = sum(jnp.sum(x, axis=1, keepdims=True) for x in xs) / total
        cs = [x - mean for x in xs]
        var = sum(jnp.sum(c * c, axis=1, keepdims=True) for c in cs) / total
        scale = lax.rsqrt(var + 1e-05)
        ready()
        acc = None
        for k in range(parts):
            at = pl.ds(pl.multiple_of((place_ref[0] ^ k) * width, 128), width)
            now = cs[k] * scale * nrm[2:3, at] + nrm[3:4, at]
            before = jnp.concatenate([prev_ref[place_ref[0] ^ k].astype(F32), now[: rows - requests]], axis=0)
            term = dot32((now + (before - now) * mx[6:7, at]).astype(BF16), kw[at, :])
            acc = term if k == 0 else acc + term
            if k == 0:
                chosen = jnp.zeros((requests, width), F32)
                number = col[0:requests, COUNT : COUNT + 1]
                for t in range(slots):
                    chosen = jnp.where(
                        number == t + 1, now[t * requests : (t + 1) * requests], chosen
                    )
                unsort = chooser(col, UNSORT, requests, requests)
                shift[...] = dot32(unsort, chosen.astype(BF16)).astype(BF16)
        h = jnp.maximum(acc, 0.0)
        hidden = (h * h).astype(BF16)
        for q in range(parts):
            at = pl.ds(pl.multiple_of((place_ref[0] ^ q) * width, 128), width)
            outs[q][...] = dot32(hidden, vw[:, at]).astype(outs[q].dtype)

    return run(
        body,
        "channel_mix",
        (place,),
        (*mids, prev, cols, norm, mix, key_weight, value_weight),
        [vmem((rows, width), F32)]
        + [vmem((rows, width), BF16) for _ in range(parts - 1)]
        + [vmem((requests, width), BF16)],
        fetch=(parts + 2, parts + 3),
    )


def finish(mid, own, others, cols):
    rows, width = mid.shape

    def body(mid_ref, own_ref, *refs):
        col, out = refs[-2:]
        total = own_ref[...]
        for o in refs[:-2]:
            total = total + o[...].astype(F32)
        live = col[:, LIVE : LIVE + 1] > 0
        total = jnp.where(live, mid_ref[...].astype(F32) + total, 0.0).astype(BF16)
        out[...] = dot32(chooser(col, BACK, rows, rows), total).astype(BF16)

    return run(body, "finish", (), (mid, own, *others, cols), [vmem((rows, width), BF16)])[0]


def per_device(
    groups,
    parts,
    tokens,
    counts,
    new_owner,
    wkv_state,
    att_shift,
    ffn_shift,
    norm_params,
    mix_coeffs,
    head_params,
    recept_weight,
    key_weight,
    value_weight,
    output_weight,
    decay_down,
    decay_up,
    alpha_down,
    alpha_up,
    gate_down,
    gate_up,
    ffn_key_weight,
    ffn_value_weight,
):
    requests, slots, width = tokens.shape
    heads = wkv_state.shape[1]
    size = width // heads
    rows = requests * slots
    rank = lax.axis_index("req").astype(I32).reshape(1)
    place = lax.axis_index("mdl").astype(I32).reshape(1)
    gather = lambda x: [x] + [xor_permute(x, "mdl", parts, k) for k in range(1, parts)]
    scatter = lambda xs: [xor_permute(xs[k], "mdl", parts, k) for k in range(1, parts)]

    toks = gather(tokens.reshape(rows, width))
    order, arriving, cols, lane_counts, sent = make_plan(
        rank, new_owner, counts, att_shift, ffn_shift, groups, parts, slots
    )
    order, toks[2], toks[3] = lax.optimization_barrier((order, toks[2], toks[3]))
    packed = pack_states(order, wkv_state, groups)
    got = lax.all_to_all(
        sent.reshape(groups * parts, -1, width),
        ("req", "mdl"),
        split_axis=0,
        concat_axis=0,
        tiled=True,
    )
    att, ffn = sort_shifts(cols, got.reshape(groups, parts, -1, width))

    normed, low, low_send, new_att = first_norm(
        place,
        toks,
        att,
        cols,
        norm_params,
        mix_coeffs,
        decay_down.T,
        alpha_down.T,
        gate_down,
    )
    partners = positions(groups)
    issue = [1] + [k for k in partners if k > 1]
    moved = {k: xor_permute(packed[partners.index(k)], "req", groups, k) for k in issue}
    moved[0] = packed[0]
    payloads = [moved[k] for k in partners]
    split = groups // 2
    first_half, recept_near, key_near, mix_near = states_to_lanes(
        payloads[:split], size, (recept_weight, key_weight, mix_coeffs)
    )
    second_half, value_near, out_near, head_near, *ups = states_to_lanes(
        payloads[split:],
        size,
        (value_weight, output_weight, head_params, decay_up, alpha_up, gate_up),
    )
    states = [first_half, second_half]
    low_others = gather(low_send)[1:]
    recept, key, value = projections(
        place, normed, att, mix_near, (recept_near, key_near, value_near)
    )
    weights, coefs, vals, keys, units, decay, gate, bonus = head_vectors(
        low,
        low_others,
        recept,
        key,
        value,
        head_near,
        ups,
        lane_counts,
        size,
    )
    results = head_outputs(
        place, states, weights, coefs, vals, gate, bonus, head_near, out_near, parts
    )
    outs, removed = results[:parts], results[parts]
    mid = middle(toks[0], cols, outs[0], scatter(outs))
    new_state = final_states(arriving, states, removed, vals, keys, units, decay, heads)
    results = channel_mix(
        place,
        gather(mid),
        ffn,
        cols,
        norm_params,
        mix_coeffs,
        ffn_key_weight,
        ffn_value_weight,
    )
    outs, new_ffn = results[:parts], results[parts]
    block = finish(mid, outs[0], scatter(outs), cols)
    return (block.reshape(requests, slots, width), new_state, new_att, new_ffn)


def solution(mesh):
    return jax.shard_map(
        functools.partial(per_device, mesh.shape["req"], mesh.shape["mdl"]),
        mesh=mesh,
        in_specs=(
            P("req", None, "mdl"),
            P("req"),
            P(),
            P("req", "mdl", None),
            P("req", "mdl"),
            P("req", "mdl"),
            P(),
            P(),
            P(None, "mdl"),
            P(None, "mdl"),
            P(None, "mdl"),
            P(None, "mdl"),
            P("mdl", None),
            P("mdl", None),
            P(None, "mdl"),
            P("mdl", None),
            P(None, "mdl"),
            P("mdl", None),
            P(None, "mdl"),
            P(None, "mdl"),
            P("mdl", None),
        ),
        out_specs=(P("req", None, "mdl"), P("req", "mdl", None), P("req", "mdl"), P("req", "mdl")),
        check_vma=False,
    )
```

```python
import functools

import jax
import jax.numpy as jnp
from jax import lax
from jax.experimental import pallas as pl
from jax.experimental.pallas import tpu as pltpu
from jax.sharding import PartitionSpec as P

F32 = jnp.float32
BF16 = jnp.bfloat16
I32 = jnp.int32
SCRATCH_LIMIT = 16 * 1024 * 1024


def xor_permute(x, axis, size, k):
    return lax.ppermute(x, axis, [(a, a ^ k) for a in range(size)])


def dot32(a, b):
    return jnp.dot(a, b, preferred_element_type=F32)


def dot32_turned(a, b):
    return lax.dot_general(a, b, (((1,), (1,)), ((), ())), preferred_element_type=F32)


def full_spec(shape):
    return pl.BlockSpec(shape, lambda *_: (0,) * len(shape))


def vmem(shape, dtype):
    return pltpu.VMEM(shape, dtype)


def run(body, name, scalars, args, outs, scratch=(), fetch=(), in_hbm=(), bring=()):
    n_own, n_made = len(args), len(outs)
    args = (*args, *bring)
    outs = [*outs, *[vmem(b.shape, b.dtype) for b in bring]]
    far = set(fetch) | set(in_hbm) | set(range(n_own, len(args)))
    anywhere = pl.BlockSpec(memory_space=pltpu.HBM)
    near = pl.BlockSpec(memory_space=pltpu.VMEM)
    n_scalars, n_args, n_outs = len(scalars), len(args), len(outs)

    def whole(*refs):
        if not bring:
            return inner(*refs)
        refs = list(refs)
        sems = refs.pop()
        first = n_scalars + n_own
        sources = refs[first : first + len(bring)]
        del refs[first : first + len(bring)]
        first += n_made
        targets = refs[first : first + len(bring)]
        del refs[first : first + len(bring)]
        copies = [
            pltpu.make_async_copy(a, b, sems.at[i])
            for i, (a, b) in enumerate(zip(sources, targets))
        ]
        for c in copies:
            c.start()
        inner(*refs)
        for c in copies:
            c.wait()

    def inner(*refs):
        refs = list(refs)
        if not fetch:
            return body(*refs)
        sems = refs.pop()
        first = len(refs) - len(fetch)
        buffers = refs[first:]
        refs = refs[:first]
        copies = []
        for at, (i, buffer) in enumerate(zip(fetch, buffers)):
            copies.append(pltpu.make_async_copy(refs[n_scalars + i], buffer, sems.at[at]))
            refs[n_scalars + i] = buffer
        for c in copies:
            c.start()

        def ready(which=None):
            for c in copies if which is None else [copies[which]]:
                c.wait()

        return body(ready, *refs)

    extra = [pltpu.VMEM(args[i].shape, args[i].dtype) for i in fetch]
    if fetch:
        extra.append(pltpu.SemaphoreType.DMA((len(fetch),)))
    if bring:
        extra.append(pltpu.SemaphoreType.DMA((len(bring),)))
    return pl.pallas_call(
        whole,
        grid_spec=pltpu.PrefetchScalarGridSpec(
            num_scalar_prefetch=n_scalars,
            grid=(1,),
            in_specs=[anywhere if i in far else near for i in range(n_args)],
            out_specs=[
                full_spec(o.shape)
                if isinstance(o, jax.ShapeDtypeStruct)
                else pl.BlockSpec(memory_space=pltpu.SMEM)
                if o.memory_space == pltpu.SMEM
                else near
                for o in outs
            ],
            scratch_shapes=list(scratch) + extra,
        ),
        out_shape=[
            o
            if isinstance(o, jax.ShapeDtypeStruct) or o.memory_space != pltpu.SMEM
            else jax.ShapeDtypeStruct(o.shape, o.dtype)
            for o in outs
        ],
        compiler_params=pltpu.CompilerParams(vmem_limit_bytes=SCRATCH_LIMIT),
        name=name,
    )(
        *scalars,
        *[
            pltpu.with_memory_space_constraint(a, pltpu.HBM if i in far else pltpu.VMEM)
            for i, a in enumerate(args)
        ],
    )


def positions(groups):
    return list(range(0, groups, 2)) + list(range(1, groups, 2))


def place_of(k, groups):
    return k // 2 + (k % 2) * (groups // 2)


SOURCE, BACK, LIVE, COUNT, UNSORT, ATT, FFN = range(7)


def make_plan(rank, new_owner, counts, att, ffn, groups, parts, slots):
    requests, width = att.shape
    per_pair = requests // groups
    rows = requests * slots

    def body(
        rank_ref, owner_far, cnt_far, att_far, ffn_far,
        order, arriving, cols, lanes_ref, sent_ref,
        owner, cnt, turn, inverse, att_ref, ffn_ref, wide, sent_f, sems,
    ):
        me = rank_ref[0]
        copies = [
            pltpu.make_async_copy(owner_far, owner, sems.at[0]),
            pltpu.make_async_copy(cnt_far, cnt, sems.at[1]),
            pltpu.make_async_copy(att_far, att_ref, sems.at[2]),
            pltpu.make_async_copy(ffn_far, ffn_ref, sems.at[3]),
        ]
        for c in copies:
            c.start()
        for g in range(groups):
            turn[g] = 0
        copies[0].wait()

        def own(i, _):
            spot = place_of((owner[me * requests + i] // requests) ^ me, groups)
            order[spot * per_pair + turn[spot]] = i
            turn[spot] = turn[spot] + 1
            return 0

        lax.fori_loop(0, requests, own, 0, unroll=4)
        for c in copies[1:]:
            c.wait()
        wide[0] = att_ref[...].astype(F32)
        wide[1] = ffn_ref[...].astype(F32)
        for d in range(groups):
            base = place_of(me ^ d, groups) * per_pair
            for j in range(per_pair):
                at = pl.ds(order[base + j], 1)
                to = d * 2 * per_pair + j
                sent_f[to : to + 1, :] = wide[0, at, :]
                sent_f[to + per_pair : to + per_pair + 1, :] = wide[1, at, :]
        for d in range(groups):
            piece = sent_f[d * 2 * per_pair : (d + 1) * 2 * per_pair, :].astype(BF16)
            for m in range(parts):
                sent_ref[d, m] = piece

        def source(s, _):
            base = place_of(s ^ me, groups) * per_pair

            def one(i, found):
                v = owner[s * requests + i]
                mine = v // requests == me
                spot = v % requests
                arriving[jnp.where(mine, base + found, requests)] = spot
                inverse[jnp.where(mine, spot, requests)] = base + found
                return found + mine.astype(I32)

            lax.fori_loop(0, requests, one, jnp.int32(0), unroll=8)
            return 0

        lax.fori_loop(0, groups, source, 0)
        row = lax.broadcasted_iota(I32, (requests, 128), 0)
        long_row = lax.broadcasted_iota(I32, (rows, 128), 0)
        lane = lax.broadcasted_iota(I32, (requests, 128), 1)
        long_lane = lax.broadcasted_iota(I32, (rows, 128), 1)
        arr = jnp.zeros((requests, 128), I32)
        inv = jnp.zeros((requests, 128), I32)
        num = jnp.zeros((requests, 128), I32)
        back = jnp.zeros((rows, 128), I32)
        lane_row = lax.broadcasted_iota(I32, (8, 128), 1)
        sub_row = lax.broadcasted_iota(I32, (8, 128), 0)
        lane_counts = jnp.zeros((8, 128), I32)
        half = requests // 2
        for q in range(requests):
            at = row == q
            a = arriving[q]
            n = cnt[a]
            arr = jnp.where(at, a, arr)
            num = jnp.where(at, n, num)
            inv = jnp.where(at, inverse[q], inv)
            back = jnp.where(long_row // slots == q, inverse[q], back)
            lane_counts = jnp.where(
                (lane_row % half == q % half) & (sub_row == q // half), n, lane_counts
            )
        lanes_ref[...] = lane_counts
        spot = row // per_pair
        partner = (spot % (groups // 2)) * 2 + spot // (groups // 2)
        got = (me ^ partner) * (2 * per_pair) + row % per_pair
        blocks = []
        for t in range(slots):
            block = jnp.where(lane == SOURCE, arr * slots + t, 0)
            block = jnp.where(lane == LIVE, (num > t).astype(I32), block)
            block = jnp.where(lane == COUNT, num, block)
            block = jnp.where(lane == UNSORT, inv, block)
            block = jnp.where(lane == ATT, got, block)
            block = jnp.where(lane == FFN, got + per_pair, block)
            blocks.append(block)
        table = jnp.concatenate(blocks, axis=0)
        cols[...] = jnp.where(long_lane == BACK, back + (long_row % slots) * requests, table)

    return run(
        body,
        "make_plan",
        (rank,),
        (new_owner, counts, att, ffn),
        [
            pltpu.SMEM((requests,), I32),
            pltpu.SMEM((requests + 1,), I32),
            vmem((rows, 128), I32),
            vmem((8, 128), I32),
            vmem((groups, parts, 2 * per_pair, width), BF16),
        ],
        scratch=[
            pltpu.SMEM(new_owner.shape, I32),
            pltpu.SMEM(counts.shape, I32),
            pltpu.SMEM((groups,), I32),
            pltpu.SMEM((requests + 1,), I32),
            vmem(att.shape, BF16),
            vmem(ffn.shape, BF16),
            vmem((2, requests, width), F32),
            vmem((2 * requests, width), F32),
            pltpu.SemaphoreType.DMA((4,)),
        ],
        in_hbm=(0, 1, 2, 3),
    )


def pack_states(order, wkv_state, groups):
    requests, heads, cells = wkv_state.shape
    per_pair = requests // groups

    def body(order_ref, wkv, *rest):
        packed = rest[:groups]
        stage, sems = rest[groups:]
        copies = []
        for q in range(requests):
            copies.append(pltpu.make_async_copy(wkv.at[order_ref[q]], stage.at[q], sems.at[q]))
            copies[q].start()
        for q in range(requests):
            copies[q].wait()
            packed[q // per_pair][q % per_pair] = stage[q].astype(BF16)

    return run(
        body,
        "pack_states",
        (order,),
        (wkv_state,),
        [vmem((per_pair, heads, cells), BF16) for _ in range(groups)],
        scratch=[vmem(wkv_state.shape, F32), pltpu.SemaphoreType.DMA((requests,))],
        in_hbm=(0,),
    )


def chooser(cols, lane, rows, columns):
    return (lax.broadcasted_iota(I32, (rows, columns), 1) == cols[0:rows, lane : lane + 1]).astype(
        BF16
    )


def sort_shifts(cols, got):
    groups, parts, twice, width = got.shape
    requests = groups * twice // 2

    def body(ready, cols_ref, got_ref, att, ffn):
        ready()
        picks = [chooser(cols_ref, lane, requests, 2 * requests) for lane in (ATT, FFN)]
        for m in range(parts):
            rows = got_ref[:, m].astype(F32).reshape(2 * requests, width).astype(BF16)
            for pick, out in zip(picks, (att, ffn)):
                out[m] = dot32(pick, rows).astype(BF16)

    return run(
        body,
        "sort_shifts",
        (),
        (cols, got),
        [vmem((parts, requests, width), BF16)] * 2,
        fetch=(0, 1),
    )


def states_to_lanes(payloads, size, bring):
    per_pair, heads, cells = payloads[0].shape
    requests = per_pair * len(payloads)
    lanes = heads * requests
    together = 4

    def body(*refs):
        ins, out_ref, rows = refs[: len(payloads)], refs[len(payloads)], refs[len(payloads) + 1]

        def some(step, _):
            for c in range(together):
                at = pl.ds(pl.multiple_of((step * together + c) * 128, 128), 128)
                for k in range(len(payloads)):
                    for j in range(per_pair):
                        first = (k * per_pair + j) * heads
                        rows[c, first : first + heads, :] = ins[k][j, :, at].astype(F32)
            for c in range(together):
                block = jnp.concatenate(
                    [rows[c, pl.ds(h, requests, stride=heads), :] for h in range(heads)], axis=0
                )
                turned = block.T
                chunk = step * together + c
                for e in range(128 // size):
                    out_ref[chunk * (128 // size) + e] = turned[e * size : (e + 1) * size]
            return 0

        lax.fori_loop(0, cells // (128 * together), some, 0)

    return run(
        body,
        "states_to_lanes",
        (),
        payloads,
        [vmem((cells // size, size, lanes), F32)],
        scratch=[vmem((together, requests * heads, 128), F32)],
        bring=bring,
    )


def first_norm(place, toks, att, cols, norm, mix, down_d, down_a, down_g):
    rows, width = toks[0].shape
    parts = len(toks)
    total = parts * width
    requests = att.shape[1]
    slots = rows // requests
    small = down_d.shape[0]
    rank_g = down_g.shape[1]
    low_width = rank_g + 2 * small

    def body(ready, place_ref, *refs):
        tok = refs[:parts]
        att_ref, col, nrm, mx, dd, da, dg, normed, low, low_send, shift = refs[parts:]
        ready()
        pick = chooser(col, SOURCE, rows, rows)
        xs = [dot32(pick, t[...]) for t in tok]
        mean = sum(jnp.sum(x, axis=1, keepdims=True) for x in xs) / total
        cs = [x - mean for x in xs]
        var = sum(jnp.sum(c * c, axis=1, keepdims=True) for c in cs) / total
        scale = lax.rsqrt(var + 1e-05)
        for k in range(parts):
            at = pl.ds(pl.multiple_of((place_ref[0] ^ k) * width, 128), width)
            normed[k] = cs[k] * scale * nrm[0:1, at] + nrm[1:2, at]
        at = pl.ds(pl.multiple_of(place_ref[0] * width, 128), width)
        now = normed[0]
        before = jnp.concatenate([att_ref[place_ref[0]].astype(F32), now[: rows - requests]], axis=0)
        delta = before - now
        mixed = lambda c: (now + delta * mx[c : c + 1, at]).astype(BF16)
        nothing = jnp.zeros((small, width), BF16)
        low[:, 0:rank_g] = dot32(mixed(5), dg[...])
        low[:, rank_g:low_width] = dot32_turned(
            mixed(1), jnp.concatenate([dd[...], nothing], axis=0)
        ) + dot32_turned(mixed(4), jnp.concatenate([nothing, da[...]], axis=0))
        low_send[...] = low[...].astype(BF16)
        chosen = jnp.zeros((requests, width), F32)
        number = col[0:requests, COUNT : COUNT + 1]
        for t in range(slots):
            chosen = jnp.where(number == t + 1, now[t * requests : (t + 1) * requests], chosen)
        unsort = chooser(col, UNSORT, requests, requests)
        shift[...] = dot32(unsort, chosen.astype(BF16)).astype(BF16)

    return run(
        body,
        "first_norm",
        (place,),
        (*toks, att, cols, norm, mix, down_d, down_a, down_g),
        [
            vmem((parts, rows, width), F32),
            vmem((rows, low_width), F32),
            vmem((rows, low_width), BF16),
            vmem((requests, width), BF16),
        ],
        fetch=(*range(1, parts), *range(parts + 1, parts + 7)),
    )


def projections(place, normed, att, mix, weights):
    parts, rows, width = normed.shape
    requests = att.shape[1]
    out_width = weights[0].shape[1]

    def body(place_ref, n_ref, *refs):
        att_ref, mx, w, outs = refs[0], refs[1], refs[2:5], refs[5:]
        for which, c in enumerate((0, 2, 3)):
            for k in range(parts):
                at = pl.ds(pl.multiple_of((place_ref[0] ^ k) * width, 128), width)
                now = n_ref[k]
                before = jnp.concatenate(
                    [att_ref[place_ref[0] ^ k].astype(F32), now[: rows - requests]], axis=0
                )
                mixed = (now + (before - now) * mx[c : c + 1, at]).astype(BF16)
                term = dot32(mixed, w[which][at, :])
                total = term if k == 0 else total + term
            outs[which][...] = total

    return run(
        body,
        "projections",
        (place,),
        (normed, att, mix, *weights),
        [vmem((rows, out_width), F32) for _ in weights],
    )


def swap_groups(arrays, group):
    arrays = list(arrays)
    lanes = arrays[0].shape[1]
    where = lax.broadcasted_iota(I32, arrays[0].shape, 1) // group
    bit = 1
    while bit < len(arrays):
        low = (where // bit) % 2 == 0
        out = list(arrays)
        for a in range(len(arrays)):
            if a & bit == 0:
                first, second = arrays[a], arrays[a | bit]
                out[a] = jnp.where(low, first, pltpu.roll(second, bit * group, 1))
                out[a | bit] = jnp.where(low, pltpu.roll(first, lanes - bit * group, 1), second)
        arrays = out
        bit *= 2
    return arrays


def fold_eight(items, flags):
    shift = 1
    for flag in flags:
        items = [
            jnp.where(flag, a, b) + pltpu.roll(jnp.where(flag, b, a), shift, 0)
            for a, b in zip(items[0::2], items[1::2])
        ]
        shift *= 2
    return items[0]


def head_vectors(low_own, low_others, recept, key, value, head_params, ups, lane_counts, size):
    rows, width = recept.shape
    lanes = 128
    heads = width // size
    group = lanes // heads
    slots = 4
    halves = rows // slots // group
    n_groups = width // 128
    small = ups[0].shape[0]
    rank_g = ups[2].shape[0]
    n_others = len(low_others)
    pairs = [(t, b) for t in range(slots) for b in range(t + 1)]

    def body(low, *refs):
        others = refs[:n_others]
        (r_ref, k_ref, v_ref, hp, du, au, gu, cnt) = refs[n_others : n_others + 8]
        (w_out, c_out, v_out, kq_out, uq_out, d_out, g_out, b_out, vec) = refs[n_others + 8 :]
        total = low[...]
        for o in others:
            total = total + o[...].astype(F32)
        glow = jax.nn.sigmoid(total[:, 0:rank_g]).astype(BF16)
        pair = total[:, rank_g : rank_g + 2 * small]
        nothing = jnp.zeros((small, width), BF16)
        decay_in = dot32(
            jnp.tanh(pair).astype(BF16), jnp.concatenate([du[...], nothing], axis=0)
        )
        context_in = dot32(pair.astype(BF16), jnp.concatenate([nothing, au[...]], axis=0))
        decay = jnp.exp(-0.606531 * jax.nn.sigmoid(hp[0:1] + decay_in))
        context = jax.nn.sigmoid(hp[1:2] + context_in)
        g_out[...] = dot32(glow, gu[...])
        r = r_ref[...]
        k = k_ref[...]
        v = v_ref[...]
        scaled = k * hp[2:3]
        kmod = k * (1.0 + (context - 1.0) * hp[3:4])
        rk = r * kmod * hp[4:5]
        lane_r = lax.broadcasted_iota(I32, (128, 128), 0)
        lane_c = lax.broadcasted_iota(I32, (128, 128), 1)
        ones = ((lane_r // size) == (lane_c // size)).astype(BF16)
        for g in range(n_groups):
            at = slice(g * 128, (g + 1) * 128)
            high = rk[:, at].astype(BF16)
            rest = (rk[:, at] - high.astype(F32)).astype(BF16)
            b_out[:, at] = (dot32(high, ones) + dot32(rest, ones)) * v[:, at]

        for index, array in enumerate((r, kmod, scaled, decay, context, v)):
            pieces = []
            for g in range(n_groups):
                turned = array[:, g * 128 : (g + 1) * 128].T
                pieces += [turned[e * size : (e + 1) * size] for e in range(128 // size)]
            for at, piece in enumerate(swap_groups(pieces, group)):
                vec[index, at % halves, at // halves] = piece

        ksum = lambda x, y: jnp.sum(x * y, axis=0, keepdims=True)
        for g in range(halves):
            valid = [cnt[g : g + 1, :] > t for t in range(slots)]
            for t in range(slots):
                s = vec[2, g, t]
                unit = s * lax.rsqrt(jnp.sum(s * s, axis=0, keepdims=True) + 1e-06)
                vec[2, g, t] = unit
                vec[4, g, t] = unit * vec[4, g, t]

            def back_through(x, top, base):
                for b in range(top, -1, -1):
                    at = base + pairs.index((top + 1, b))
                    c_out[g, at : at + 1, :] = jnp.where(valid[b], ksum(vec[1, g, b], x), 0.0)
                    moved = vec[3, g, b] * x - vec[2, g, b] * ksum(vec[4, g, b], x)
                    x = jnp.where(valid[b], moved, x)
                return x

            for t in range(slots):
                w_out[g, t] = back_through(vec[2, g, t], t - 1, 0)
                x = vec[0, g, t]
                at = len(pairs) + pairs.index((t, t))
                c_out[g, at : at + 1, :] = ksum(vec[1, g, t], x)
                x = vec[3, g, t] * x - vec[2, g, t] * ksum(vec[4, g, t], x)
                w_out[g, slots + t] = back_through(x, t - 1, len(pairs))
            run_decay = jnp.ones((size, lanes), F32)
            for t in range(slots - 1, -1, -1):
                kq_out[g, t] = jnp.where(valid[t], vec[1, g, t] * run_decay, 0.0)
                uq_out[g, t] = jnp.where(valid[t], -(vec[4, g, t] * run_decay), 0.0)
                run_decay = jnp.where(valid[t], run_decay * vec[3, g, t], run_decay)
                v_out[g, t] = vec[5, g, t]
            d_out[g] = run_decay

    return run(
        body,
        "head_vectors",
        (),
        (low_own, *low_others, recept, key, value, head_params, *ups, lane_counts),
        [
            vmem((halves, 2 * slots, size, lanes), F32),
            vmem((halves, 2 * len(pairs), lanes), F32),
            vmem((halves, slots, size, lanes), F32),
            vmem((halves, slots, size, lanes), F32),
            vmem((halves, slots, size, lanes), F32),
            vmem((halves, size, lanes), F32),
            vmem((rows, width), F32),
            vmem((rows, width), F32),
        ],
        scratch=[vmem((6, halves, slots, size, lanes), F32)],
    )


def head_outputs(place, states, weights, coefs, values, gate, bonus, head_params, out_weight, parts):
    rows, width = gate.shape
    halves = len(states)
    size, lanes = states[0].shape[1:]
    slots = values.shape[1]
    group = rows // slots // halves
    n_groups = width // 128
    pairs = [(t, b) for t in range(slots) for b in range(t + 1)]
    quad = 4

    def body(place_ref, *refs):
        st = refs[:halves]
        w_ref, c_ref, v_ref, gate_ref, bonus_ref, hp, wo = refs[halves : halves + 7]
        outs = refs[halves + 7 : halves + 7 + parts]
        p_out, prod, done = refs[halves + 7 + parts :]
        sub = lax.broadcasted_iota(I32, (8, lanes), 0)
        folds = [(sub // s) % 2 == 0 for s in (1, 2, 4)]
        for g in range(halves):
            for part in range(2 * slots // quad):

                def products(block, _):
                    ws = [w_ref[g, part * quad + w] for w in range(quad)]
                    sums = [[] for _ in range(quad)]
                    for i in range(8):
                        s = st[g][block * 8 + i]
                        for w in range(quad):
                            term = s * ws[w]
                            acc = term[0:8]
                            for jv in range(1, size // 8):
                                acc = acc + term[jv * 8 : (jv + 1) * 8]
                            sums[w].append(acc)
                    at = pl.ds(pl.multiple_of(block * 8, 8), 8)
                    for w in range(quad):
                        prod[g, part * quad + w, at, :] = fold_eight(sums[w], folds)
                    return 0

                lax.fori_loop(0, size // 8, products, 0)

        by_group = [None] * (halves * slots)
        for g in range(halves):
            for t in range(slots):
                removed = prod[g, t]
                y = prod[g, slots + t]
                for b in range(t + 1):
                    at = pairs.index((t, b))
                    if b < t:
                        removed = removed + c_ref[g, at : at + 1, :] * v_ref[g, b]
                    at += len(pairs)
                    y = y + c_ref[g, at : at + 1, :] * v_ref[g, b]
                p_out[g, t] = removed
                center = y - jnp.mean(y, axis=0, keepdims=True)
                spread = jnp.mean(center * center, axis=0, keepdims=True)
                by_group[t * halves + g] = center * lax.rsqrt(spread + 0.00064)
        backs = swap_groups(by_group, group)
        each = 128 // size
        for g in range(n_groups):
            at = slice(g * 128, (g + 1) * 128)
            turned = jnp.concatenate(backs[each * g : each * (g + 1)], axis=0).T
            full = (turned * hp[5:6, at] + hp[6:7, at] + bonus_ref[:, at]) * gate_ref[:, at]
            done[:, at] = full.astype(BF16)
        for q in range(parts):
            at = pl.ds(pl.multiple_of((place_ref[0] ^ q) * width, 128), width)
            outs[q][...] = dot32(done[...], wo[:, at]).astype(outs[q].dtype)

    return run(
        body,
        "head_outputs",
        (place,),
        (*states, weights, coefs, values, gate, bonus, head_params, out_weight),
        [vmem((rows, width), F32)]
        + [vmem((rows, width), BF16) for _ in range(parts - 1)]
        + [vmem(values.shape, F32)],
        scratch=[vmem(weights.shape, F32), vmem((rows, width), BF16)],
    )


def final_states(arriving, states, removed, values, keys, units, decay, heads):
    halves = len(states)
    size, _, lanes = states[0].shape
    slots = removed.shape[1]
    half = lanes // heads
    requests = half * halves
    step_chunks = 4
    per_chunk = 128 // size
    steps = size // (per_chunk * step_chunks)
    cells = size * size

    def body(arr_ref, *refs):
        st = refs[:halves]
        p_ref, v_ref, kq_ref, uq_ref, d_ref, out_ref, new, rows = refs[halves:]
        step = pl.program_id(0)
        for g in range(halves):

            def update(block, _):
                first = block * 4
                real = step * (per_chunk * step_chunks) + first
                lefts = []
                for i in range(4):
                    row = [v_ref[g, t, pl.ds(real + i, 1), :] for t in range(slots)]
                    row += [p_ref[g, t, pl.ds(real + i, 1), :] for t in range(slots)]
                    lefts.append([jnp.broadcast_to(x, (8, lanes)) for x in row])
                for jv in range(size // 8):
                    at = slice(jv * 8, (jv + 1) * 8)
                    rights = [kq_ref[g, t, at, :] for t in range(slots)]
                    rights += [uq_ref[g, t, at, :] for t in range(slots)]
                    decayed = d_ref[g, at, :]
                    for i in range(4):
                        acc = st[g][real + i, at, :] * decayed
                        for left, right in zip(lefts[i], rights):
                            acc = acc + left * right
                        new[g, first + i, at, :] = acc
                return 0

            lax.fori_loop(0, per_chunk * step_chunks // 4, update, 0)
        for c in range(step_chunks):
            for g in range(halves):
                block = [new[g, per_chunk * c + e] for e in range(per_chunk)]
                turned = jnp.concatenate(block, axis=0).T
                for h in range(heads):
                    rows[c, pl.ds(g * half * heads + h, half, stride=heads), :] = turned[
                        h * half : (h + 1) * half
                    ]
        for c in range(step_chunks):
            for q in range(requests):
                out_ref[arr_ref[q], :, c * 128 : (c + 1) * 128] = rows[
                    c, q * heads : (q + 1) * heads, :
                ]

    args = (*states, removed, values, keys, units, decay)
    return pl.pallas_call(
        body,
        grid_spec=pltpu.PrefetchScalarGridSpec(
            num_scalar_prefetch=1,
            grid=(steps,),
            in_specs=[pl.BlockSpec(memory_space=pltpu.VMEM) for _ in args],
            out_specs=pl.BlockSpec((requests, heads, 128 * step_chunks), lambda s, a: (0, 0, s)),
            scratch_shapes=[
                vmem((halves, per_chunk * step_chunks, size, lanes), F32),
                vmem((step_chunks, requests * heads, 128), F32),
            ],
        ),
        out_shape=jax.ShapeDtypeStruct((requests, heads, cells), F32),
        compiler_params=pltpu.CompilerParams(vmem_limit_bytes=SCRATCH_LIMIT),
        name="final_states",
    )(arriving, *[pltpu.with_memory_space_constraint(a, pltpu.VMEM) for a in args])


def middle(tok, cols, own, others):
    rows, width = tok.shape

    def body(tok_ref, col, own_ref, *refs):
        out = refs[-1]
        total = dot32(chooser(col, SOURCE, rows, rows), tok_ref[...]) + own_ref[...]
        for o in refs[:-1]:
            total = total + o[...].astype(F32)
        out[...] = total.astype(BF16)

    return run(body, "middle", (), (tok, cols, own, *others), [vmem((rows, width), BF16)])[0]


def channel_mix(place, mids, prev, cols, norm, mix, key_weight, value_weight):
    parts = len(mids)
    rows, width = mids[0].shape
    total = parts * width
    requests = prev.shape[1]
    slots = rows // requests

    def body(ready, place_ref, *refs):
        mid = refs[:parts]
        prev_ref, col, nrm, mx, kw, vw = refs[parts : parts + 6]
        outs, shift = refs[parts + 6 : 2 * parts + 6], refs[2 * parts + 6]
        xs = [m[...].astype(F32) for m in mid]
        mean = sum(jnp.sum(x, axis=1, keepdims=True) for x in xs) / total
        cs = [x - mean for x in xs]
        var = sum(jnp.sum(c * c, axis=1, keepdims=True) for c in cs) / total
        scale = lax.rsqrt(var + 1e-05)
        ready()
        acc = None
        for k in range(parts):
            at = pl.ds(pl.multiple_of((place_ref[0] ^ k) * width, 128), width)
            now = cs[k] * scale * nrm[2:3, at] + nrm[3:4, at]
            before = jnp.concatenate([prev_ref[place_ref[0] ^ k].astype(F32), now[: rows - requests]], axis=0)
            term = dot32((now + (before - now) * mx[6:7, at]).astype(BF16), kw[at, :])
            acc = term if k == 0 else acc + term
            if k == 0:
                chosen = jnp.zeros((requests, width), F32)
                number = col[0:requests, COUNT : COUNT + 1]
                for t in range(slots):
                    chosen = jnp.where(
                        number == t + 1, now[t * requests : (t + 1) * requests], chosen
                    )
                unsort = chooser(col, UNSORT, requests, requests)
                shift[...] = dot32(unsort, chosen.astype(BF16)).astype(BF16)
        h = jnp.maximum(acc, 0.0)
        hidden = (h * h).astype(BF16)
        for q in range(parts):
            at = pl.ds(pl.multiple_of((place_ref[0] ^ q) * width, 128), width)
            outs[q][...] = dot32(hidden, vw[:, at]).astype(outs[q].dtype)

    return run(
        body,
        "channel_mix",
        (place,),
        (*mids, prev, cols, norm, mix, key_weight, value_weight),
        [vmem((rows, width), F32)]
        + [vmem((rows, width), BF16) for _ in range(parts - 1)]
        + [vmem((requests, width), BF16)],
        fetch=(parts + 2, parts + 3),
    )


def finish(mid, own, others, cols, slots):
    rows, width = mid.shape

    def body(mid_ref, own_ref, *refs):
        col, out = refs[-2:]
        total = own_ref[...]
        for o in refs[:-2]:
            total = total + o[...].astype(F32)
        live = col[:, LIVE : LIVE + 1] > 0
        total = jnp.where(live, mid_ref[...].astype(F32) + total, 0.0).astype(BF16)
        done = dot32(chooser(col, BACK, rows, rows), total)
        out[...] = done.reshape(rows // slots, slots, width).astype(BF16)

    whole = jax.ShapeDtypeStruct((rows // slots, slots, width), BF16)
    return run(body, "finish", (), (mid, own, *others, cols), [whole])[0]


def per_device(
    groups,
    parts,
    tokens,
    counts,
    new_owner,
    wkv_state,
    att_shift,
    ffn_shift,
    norm_params,
    mix_coeffs,
    head_params,
    recept_weight,
    key_weight,
    value_weight,
    output_weight,
    decay_down,
    decay_up,
    alpha_down,
    alpha_up,
    gate_down,
    gate_up,
    ffn_key_weight,
    ffn_value_weight,
):
    requests, slots, width = tokens.shape
    heads = wkv_state.shape[1]
    size = width // heads
    rows = requests * slots
    rank = lax.axis_index("req").astype(I32).reshape(1)
    place = lax.axis_index("mdl").astype(I32).reshape(1)
    gather = lambda x: [x] + [xor_permute(x, "mdl", parts, k) for k in range(1, parts)]
    scatter = lambda xs: [xor_permute(xs[k], "mdl", parts, k) for k in range(1, parts)]

    toks = gather(tokens.reshape(rows, width))
    order, arriving, cols, lane_counts, sent = make_plan(
        rank, new_owner, counts, att_shift, ffn_shift, groups, parts, slots
    )
    order, toks[2], toks[3] = lax.optimization_barrier((order, toks[2], toks[3]))
    packed = pack_states(order, wkv_state, groups)
    got = lax.all_to_all(
        sent.reshape(groups * parts, -1, width),
        ("req", "mdl"),
        split_axis=0,
        concat_axis=0,
        tiled=True,
    )
    att, ffn = sort_shifts(cols, got.reshape(groups, parts, -1, width))

    normed, low, low_send, new_att = first_norm(
        place,
        toks,
        att,
        cols,
        norm_params,
        mix_coeffs,
        decay_down.T,
        alpha_down.T,
        gate_down,
    )
    partners = positions(groups)
    issue = [1] + [k for k in partners if k > 1]
    moved = {k: xor_permute(packed[partners.index(k)], "req", groups, k) for k in issue}
    moved[0] = packed[0]
    payloads = [moved[k] for k in partners]
    split = groups // 2
    first_half, recept_near, key_near, mix_near = states_to_lanes(
        payloads[:split], size, (recept_weight, key_weight, mix_coeffs)
    )
    second_half, value_near, out_near, head_near, *ups = states_to_lanes(
        payloads[split:],
        size,
        (value_weight, output_weight, head_params, decay_up, alpha_up, gate_up),
    )
    states = [first_half, second_half]
    low_others = gather(low_send)[1:]
    recept, key, value = projections(
        place, normed, att, mix_near, (recept_near, key_near, value_near)
    )
    weights, coefs, vals, keys, units, decay, gate, bonus = head_vectors(
        low,
        low_others,
        recept,
        key,
        value,
        head_near,
        ups,
        lane_counts,
        size,
    )
    results = head_outputs(
        place, states, weights, coefs, vals, gate, bonus, head_near, out_near, parts
    )
    outs, removed = results[:parts], results[parts]
    mid = middle(toks[0], cols, outs[0], scatter(outs))
    new_state = final_states(arriving, states, removed, vals, keys, units, decay, heads)
    results = channel_mix(
        place,
        gather(mid),
        ffn,
        cols,
        norm_params,
        mix_coeffs,
        ffn_key_weight,
        ffn_value_weight,
    )
    outs, new_ffn = results[:parts], results[parts]
    block = finish(mid, outs[0], scatter(outs), cols, slots)
    return (block, new_state, new_att, new_ffn)


def solution(mesh):
    return jax.shard_map(
        functools.partial(per_device, mesh.shape["req"], mesh.shape["mdl"]),
        mesh=mesh,
        in_specs=(
            P("req", None, "mdl"),
            P("req"),
            P(),
            P("req", "mdl", None),
            P("req", "mdl"),
            P("req", "mdl"),
            P(),
            P(),
            P(None, "mdl"),
            P(None, "mdl"),
            P(None, "mdl"),
            P(None, "mdl"),
            P("mdl", None),
            P("mdl", None),
            P(None, "mdl"),
            P("mdl", None),
            P(None, "mdl"),
            P("mdl", None),
            P(None, "mdl"),
            P(None, "mdl"),
            P("mdl", None),
        ),
        out_specs=(P("req", None, "mdl"), P("req", "mdl", None), P("req", "mdl"), P("req", "mdl")),
        check_vma=False,
    )
```
